32 devices in a mesh: chain: 4 (over x, core), rows: 8 (over z, y).
Axes of the slice: x: 2, y: 2, z: 4, core: 2. Of those that a mesh axis runs over, the one named last changes fastest.
Arguments:
- right_side: bfloat16 [8, 64, 128, 256], P('chain', 'rows'), may hold values from -3 to 3
- lower_blocks: bfloat16 [8, 64, 6, 128, 128], P('chain', 'rows'), may hold values from -0.5 to 0.5
- block_scale: float32 [8, 64, 6], P('chain', 'rows'), may hold values from 0.1 to 0.6
- diag_inverse: bfloat16 [8, 64, 128, 128], P('chain', 'rows'), may hold values from -0.11 to 1.11
- depend_rows: int32 [8, 64, 6], P('chain', 'rows'), may hold values from 0 to 63, as said below
Outputs:
- solution: bfloat16 [8, 64, 128, 256], P('chain', 'rows')
The draws below stay inside these ranges and needn't reach their ends.
Inputs may be any that keep to these rules, and one draw needn't show every extreme that they name: depend_rows[l, q, k] names a block row of level l - 1 (unused at level 0) from q - 2 to q + 2.
All inputs are finite; a program needn't handle non-finite values.
Results may differ from the reference program's by a relative error of at most 0.03.
Values may be sent and summed in bfloat16 or wider, within the bound.
No kernel may reach another device: no remote copies, remote signals or barrier semaphores. Data moves between devices by JAX's collectives and lax.ppermute only.
A program may use at most 64 MiB of HBM per device.

```python
import math
import jax
import jax.numpy as jnp
from jax import lax

BLOCK = 128
CASES = 256
LOWER = 6
REACH = 2
LEVELS = 8
LEVEL_ROWS = 64


def draw_diag_inverse(key, part):
    array_shape = (LEVELS, LEVEL_ROWS, BLOCK, BLOCK)
    jitter = jnp.clip(jax.random.normal(key, array_shape, jnp.float32), -4.0, 4.0) * (0.3 / math.sqrt(BLOCK))
    jitter = jnp.clip(jitter, -0.1, 0.1)
    return (jitter + jnp.eye(BLOCK, dtype=jnp.float32)).astype(jnp.bfloat16)


def draw_depend_rows(key, part):
    places = jnp.arange(LEVEL_ROWS, dtype=jnp.int32)
    lowest = jnp.maximum(places - REACH, 0)
    highest = jnp.minimum(places + REACH + 1, LEVEL_ROWS)
    array_shape = (LEVELS, LEVEL_ROWS, LOWER)
    return jax.random.randint(key, array_shape, lowest[None, :, None], highest[None, :, None], jnp.int32)


def levels(own_key, extent, split, smallest, top_value):
    factor_of, own = 1.0, jax.random.fold_in(own_key, 6)
    for axis_at, shards_of in split:
        heights = jnp.exp(jax.random.uniform(jax.random.fold_in(own, axis_at), (shards_of,), jnp.float32, smallest / len(split), top_value / len(split)))
        factor_of = factor_of * jnp.repeat(heights, extent[axis_at] // shards_of).reshape([-1 if axis == axis_at else 1 for axis in range(len(extent))])
    return factor_of


def gaussian(rng, dims, spread, bound, pieces=(), held_as=jnp.bfloat16):
    result = jax.random.normal(rng, dims, jnp.float32) * spread
    if len(pieces) > 0:
        result = levels(rng, dims, pieces, -0.22, 0.18) * result
    return jnp.clip(result, min=-bound, max=bound).astype(held_as)


def setup_inputs(seed: int = 0) -> dict:
    seeds = jax.random.split(jax.random.key(seed), 6)
    return {
        "right_side": gaussian(seeds[0], (LEVELS, LEVEL_ROWS, BLOCK, CASES), 0.5, 3.0, ((0, 4), (1, 8))),
        "lower_blocks": gaussian(seeds[1], (LEVELS, LEVEL_ROWS, LOWER, BLOCK, BLOCK), BLOCK ** -0.5, 0.5, ((0, 4), (1, 8))),
        "block_scale": jnp.clip(jnp.exp(math.log(0.6) - 1.7917595 * jax.random.uniform(seeds[2], (LEVELS, LEVEL_ROWS, LOWER), jnp.float32) ** levels(seeds[2], (LEVELS, LEVEL_ROWS, LOWER), ((0, 4), (1, 8)), -0.2, 0.2)), 0.1, 0.6),
        "diag_inverse": draw_diag_inverse(jax.random.fold_in(seeds[5], 71), 0),
        "depend_rows": draw_depend_rows(jax.random.fold_in(seeds[5], 71), 0),
    }


def one_level(previous, inputs):
    right_side, blocks, scales, inverse, depend = inputs
    picked_rows = previous[depend]
    scaled = (scales[:, :, None, None] * picked_rows.astype(jnp.float32)).astype(jnp.bfloat16)
    scaled = lax.optimization_barrier(scaled)
    totals = jnp.einsum("qkab,qkbn->qan", blocks.astype(jnp.float32), scaled.astype(jnp.float32))
    remainder = (right_side.astype(jnp.float32) - totals).astype(jnp.bfloat16)
    remainder = lax.optimization_barrier(remainder)
    solved = jnp.einsum("qab,qbn->qan", inverse.astype(jnp.float32), remainder.astype(jnp.float32)).astype(jnp.bfloat16)
    return solved, solved


def reference(right_side, lower_blocks, block_scale, diag_inverse, depend_rows):
    initial = jnp.zeros(right_side.shape[1:], jnp.bfloat16)
    _, solution = lax.scan(one_level, initial, (right_side, lower_blocks, block_scale, diag_inverse, depend_rows))
    return solution
```

```python
import functools

import jax
import jax.numpy as jnp
from jax import lax
from jax.experimental import pallas as pl
from jax.experimental.pallas import tpu as pltpu
from jax.sharding import PartitionSpec as P

REACH = 2
SPAN = 2 * REACH + 1
AXES = ("chain", "rows")
VMEM = pl.BlockSpec(memory_space=pltpu.VMEM)
SMEM = pl.BlockSpec(memory_space=pltpu.SMEM)
ANY = pl.BlockSpec(memory_space=pl.ANY)


def even_mate(row, rows):
    return row ^ 1


def odd_mate(row, rows):
    mate = row + 1 if row % 2 else row - 1
    return mate if 0 <= mate < rows else row


def same_row(row, rows):
    return row


def swap_groups(chain, taken=()):
    return {g: g ^ 1 for g in range(chain) if g not in taken}


def hop_pairs(group, mate, chain, rows):
    if group % 2 == 0:
        moves = swap_groups(chain)
    else:
        moves = swap_groups(chain, range(group - 1, group + 3))
        moves.update({group: group + 1, group - 1: group, group + 1: group + 2, group + 2: group - 1})
    return [
        (source * rows + r, target * rows + (mate(r, rows) if source == group else r))
        for source, target in moves.items()
        for r in range(rows)
    ]


def first_pairs(mate, chain, rows):
    pairs = []
    for r in range(rows):
        target = mate(r, rows)
        if target == r:
            moves = swap_groups(chain)
        else:
            pairs.append((r, target))
            moves = swap_groups(chain, range(4))
            moves.update({1: 2, 2: 3, 3: 1})
        pairs += [(a * rows + r, b * rows + r) for a, b in moves.items()]
    return pairs


def inner_pairs(mate, chain, rows):
    return [
        (g * rows + r, g * rows + mate(r, rows))
        for g in range(1, chain)
        for r in range(rows)
        if mate(r, rows) != r
    ]


def dot(a, b):
    return jnp.dot(a, b, preferred_element_type=jnp.float32)


def by_parity(odd, low_value, high_value, even_ref, odd_ref):
    @pl.when(odd == 0)
    def _():
        even_ref[...] = high_value()
        odd_ref[...] = low_value()

    @pl.when(odd == 1)
    def _():
        even_ref[...] = low_value()
        odd_ref[...] = high_value()


def first_kernel(meta, inverse, right, solved, even_out, odd_out):
    count = right.shape[1]
    for q in range(count):
        solved[q] = dot(inverse[0, q], right[0, q]).astype(solved.dtype)
    by_parity(
        meta[1],
        lambda: solved[:REACH],
        lambda: solved[count - REACH :],
        even_out,
        odd_out,
    )


def prepare_kernel(meta, depend, scale, lower, inverse, right, first, wide_a, wide_b, base_b, even_out, odd_out, acc, row_form):
    step = pl.program_id(0)
    last = pl.num_programs(0) - 1
    block = lower.shape[-1]
    width = SPAN * block
    for level, wide in ((0, wide_a), (1, wide_b)):
        wide[...] = jnp.zeros_like(wide)
        for half in range(2):
            q = 2 * step + half
            acc[...] = jnp.zeros_like(acc)
            for k in range(lower.shape[2]):
                product = dot(inverse[level, half], lower[level, half, k])
                acc[depend[level, q, k]] += scale[level, q, k] * product
            for d in range(SPAN):
                column = (d + half) * block
                value = (-acc[d]).astype(wide.dtype)
                wide[0, half * block : (half + 1) * block, column : column + block] = value
                if level == 0:
                    row_form[half, :, d * block : (d + 1) * block] = value
    for half in range(2):
        base_b[half] = dot(inverse[1, half], right[0, half])

    def emit(ref):
        ref[:, :, :width] = row_form[...]
        ref[:, :, width:] = first[...]

    odd = meta[1]
    at_low, at_high = step == 0, step == last

    @pl.when((at_low & (odd == 1)) | (at_high & (odd == 0)))
    def _():
        emit(even_out)

    @pl.when((at_low & (odd == 0)) | (at_high & (odd == 1)))
    def _():
        emit(odd_out)


def order_kernel(meta, even_in, odd_in, edges):
    odd = meta[1]
    edges[1 - odd] = even_in[...]
    edges[odd] = odd_in[...]


def flat(ref, start, count):
    block = ref[start : start + count]
    return block.reshape(count * block.shape[1], block.shape[2])


def second_level(wide_b, base_b, level_a, solved):
    for p in range(wide_b.shape[0]):
        rows = dot(wide_b[p], flat(level_a, 2 * p, SPAN + 1)) + flat(base_b, 2 * p, 2)
        solved[2 * p : 2 * p + 2] = rows.astype(solved.dtype).reshape(2, *solved.shape[1:])


def finish(odd, level_a, solved, out, sends, sem_a, sem_b, copy_a):
    count = solved.shape[0]
    copy_b = pltpu.make_async_copy(solved, out.at[1], sem_b)
    copy_b.start()
    if sends:
        by_parity(
            odd,
            lambda: solved[: 2 * REACH],
            lambda: solved[count - 2 * REACH :],
            *sends,
        )
    copy_a.wait()
    copy_b.wait()


def first_step(group, meta, first, even_in, odd_in, wide_b, base_b, out, solved, *rest):
    *sends, level_a, sem_a, sem_b = rest

    @pl.when(meta[0] == group)
    def _():
        odd = meta[1]
        count = first.shape[0]
        low, high = 0, count + REACH
        level_a[REACH : REACH + count] = first[...]
        level_a[pl.ds(jnp.where(odd == 1, low, high), REACH)] = even_in[...]
        level_a[pl.ds(jnp.where(odd == 1, high, low), REACH)] = odd_in[...]
        copy_a = pltpu.make_async_copy(level_a.at[pl.ds(REACH, count)], out.at[0], sem_a)
        copy_a.start()
        second_level(wide_b, base_b, level_a, solved)
        finish(odd, level_a, solved, out, sends, sem_a, sem_b, copy_a)


def later_step(group, meta, centre, even_in, odd_in, edges, first, wide_a, wide_b, base_b, out_in, out, solved, *rest):
    *sends, window, level_a, sem_a, sem_b = rest

    @pl.when(meta[0] == group)
    def _():
        odd = meta[1]
        count, block = first.shape[0], first.shape[1]
        width = SPAN * block
        halo = 2 * REACH
        low, high = 0, count + halo
        window[halo : halo + count] = centre[...]
        window[pl.ds(jnp.where(odd == 1, low, high), halo)] = even_in[...]
        window[pl.ds(jnp.where(odd == 1, high, low), halo)] = odd_in[...]
        for p in range(wide_a.shape[0]):
            rows = dot(wide_a[p], flat(window, REACH + 2 * p, SPAN + 1)) + flat(first, 2 * p, 2).astype(jnp.float32)
            level_a[REACH + 2 * p : REACH + 2 * p + 2] = rows.astype(level_a.dtype).reshape(2, *level_a.shape[1:])
        copy_a = pltpu.make_async_copy(level_a.at[pl.ds(REACH, count)], out.at[0], sem_a)
        copy_a.start()
        for side in range(2):
            for i in range(REACH):
                at = side * (count + REACH) + i
                row = dot(edges[side, i, :, :width], flat(window, at, SPAN)) + edges[side, i, :, width:].astype(jnp.float32)
                level_a[at] = row.astype(level_a.dtype)
        second_level(wide_b, base_b, level_a, solved)
        finish(odd, level_a, solved, out, sends, sem_a, sem_b, copy_a)


def shaped(shape, dtype=jnp.bfloat16):
    return jax.ShapeDtypeStruct(shape, dtype)


def params(**more):
    return pltpu.CompilerParams(vmem_limit_bytes=32 * 1024 * 1024, **more)


def per_device(chain, rows, right_side, lower_blocks, block_scale, diag_inverse, depend_rows):
    _, count, block, cases = right_side.shape
    terms = lower_blocks.shape[2]
    width = SPAN * block
    row = lax.axis_index("rows")
    meta = jnp.stack([lax.axis_index("chain"), row % 2]).astype(jnp.int32)
    offset = depend_rows - (row * count + jnp.arange(count, dtype=jnp.int32))[None, :, None] + REACH
    offset = jnp.clip(offset, 0, SPAN - 1)

    first, even_edge, odd_edge = pl.pallas_call(
        first_kernel,
        grid=(1,),
        in_specs=[
            SMEM,
            pl.BlockSpec((1, count, block, block), lambda i: (0, 0, 0, 0)),
            pl.BlockSpec((1, count, block, cases), lambda i: (0, 0, 0, 0)),
        ],
        out_specs=[
            pl.BlockSpec((count, block, cases), lambda i: (0, 0, 0)),
            pl.BlockSpec((REACH, block, cases), lambda i: (0, 0, 0)),
            pl.BlockSpec((REACH, block, cases), lambda i: (0, 0, 0)),
        ],
        out_shape=[shaped((count, block, cases)), shaped((REACH, block, cases)), shaped((REACH, block, cases))],
        compiler_params=params(),
        name="first_level",
    )(meta, diag_inverse, right_side)
    even_x = lax.ppermute(even_edge, AXES, first_pairs(even_mate, chain, rows))
    odd_x = lax.ppermute(odd_edge, AXES, first_pairs(odd_mate, chain, rows))

    pairs = count // 2
    wide_a, wide_b, base_b, even_w, odd_w = pl.pallas_call(
        prepare_kernel,
        grid=(pairs,),
        in_specs=[
            SMEM,
            SMEM,
            SMEM,
            pl.BlockSpec((2, 2, terms, block, block), lambda i: (0, i, 0, 0, 0)),
            pl.BlockSpec((2, 2, block, block), lambda i: (0, i, 0, 0)),
            pl.BlockSpec((1, 2, block, cases), lambda i: (1, i, 0, 0)),
            pl.BlockSpec((2, block, cases), lambda i: (i, 0, 0)),
        ],
        out_specs=[
            pl.BlockSpec((1, 2 * block, width + block), lambda i: (i, 0, 0)),
            pl.BlockSpec((1, 2 * block, width + block), lambda i: (i, 0, 0)),
            pl.BlockSpec((2, block, cases), lambda i: (i, 0, 0)),
            pl.BlockSpec((REACH, block, width + cases), lambda i: (0, 0, 0)),
            pl.BlockSpec((REACH, block, width + cases), lambda i: (0, 0, 0)),
        ],
        out_shape=[
            shaped((pairs, 2 * block, width + block)),
            shaped((pairs, 2 * block, width + block)),
            shaped((count, block, cases), jnp.float32),
            shaped((REACH, block, width + cases)),
            shaped((REACH, block, width + cases)),
        ],
        scratch_shapes=[
            pltpu.VMEM((SPAN, block, block), jnp.float32),
            pltpu.VMEM((2, block, width), jnp.bfloat16),
        ],
        compiler_params=params(),
        name="prepare",
    )(meta, offset, block_scale, lower_blocks, diag_inverse, right_side, first)
    even_w = lax.ppermute(even_w, AXES, inner_pairs(even_mate, chain, rows))
    odd_w = lax.ppermute(odd_w, AXES, inner_pairs(odd_mate, chain, rows))

    halo = 2 * REACH
    sem = [pltpu.SemaphoreType.DMA, pltpu.SemaphoreType.DMA]
    level_a = pltpu.VMEM((count + 2 * REACH, block, cases), jnp.bfloat16)
    solved_shape = shaped((count, block, cases))
    send_shape = [shaped((halo, block, cases))] * 2

    out, *sent = pl.pallas_call(
        functools.partial(first_step, 0),
        in_specs=[SMEM] + [VMEM] * 5,
        out_specs=[ANY] + [VMEM] * 3,
        out_shape=[shaped(right_side.shape), solved_shape, *send_shape],
        scratch_shapes=[level_a, *sem],
        compiler_params=params(),
        name="step_0",
    )(meta, first, even_x, odd_x, wide_b, base_b)

    edges = pl.pallas_call(
        order_kernel,
        in_specs=[SMEM, VMEM, VMEM],
        out_specs=VMEM,
        out_shape=shaped((2, *even_w.shape)),
        compiler_params=params(),
        name="order",
    )(meta, even_w, odd_w)

    for group in range(1, chain):
        mates = (same_row, even_mate, odd_mate)
        received = [
            lax.ppermute(value, AXES, hop_pairs(group - 1, mate, chain, rows))
            for value, mate in zip(sent, mates)
        ]
        final = group == chain - 1
        outs = [solved_shape] + ([] if final else send_shape)
        out, *sent = pl.pallas_call(
            functools.partial(later_step, group),
            in_specs=[SMEM] + [VMEM] * 8 + [ANY],
            out_specs=[ANY] + [VMEM] * len(outs),
            out_shape=[shaped(right_side.shape), *outs],
            scratch_shapes=[
                pltpu.VMEM((count + 2 * halo, block, cases), jnp.bfloat16),
                level_a,
                *sem,
            ],
            input_output_aliases={9: 0},
            compiler_params=params(),
            name=f"step_{group}",
        )(meta, *received, edges, first, wide_a, wide_b, base_b, out)
    return out


def solution(mesh):
    placed = (
        P("chain", "rows", None, None),
        P("chain", "rows", None, None, None),
        P("chain", "rows", None),
        P("chain", "rows", None, None),
        P("chain", "rows", None),
    )
    return jax.shard_map(
        functools.partial(per_device, mesh.shape["chain"], mesh.shape["rows"]),
        mesh=mesh,
        in_specs=placed,
        out_specs=P("chain", "rows", None, None),
        check_vma=False,
    )
```

```python
import functools

import jax
import jax.numpy as jnp
from jax import lax
from jax.experimental import pallas as pl
from jax.experimental.pallas import tpu as pltpu
from jax.sharding import PartitionSpec as P

REACH = 2
SPAN = 2 * REACH + 1
CHUNKS = 2
EDGE = SPAN + CHUNKS
AXES = ("chain", "rows")
VMEM = pl.BlockSpec(memory_space=pltpu.VMEM)
SMEM = pl.BlockSpec(memory_space=pltpu.SMEM)
ANY = pl.BlockSpec(memory_space=pl.ANY)
HBM = pl.BlockSpec(memory_space=pltpu.HBM)


def even_mate(row, rows):
    return row ^ 1


def odd_mate(row, rows):
    mate = row + 1 if row % 2 else row - 1
    return mate if 0 <= mate < rows else row


def same_row(row, rows):
    return row


def swap_groups(chain, taken=()):
    return {g: g ^ 1 for g in range(chain) if g not in taken}


def hop_pairs(group, mate, chain, rows, within):
    if group % 2 == 0:
        moves = swap_groups(chain)
    else:
        moves = swap_groups(chain, range(group - 1, group + 3))
        moves.update({group: group + 1, group - 1: group, group + 1: group + 2, group + 2: group - 1})
    stay = ()
    if within and group < 2:
        stay = range(2, chain) if group == 0 else range(3, chain)
        moves = {0: 1, 1: 0} if group == 0 else {0: 1, 1: 2, 2: 0}
    pairs = []
    for r in range(rows):
        target = mate(r, rows)
        own = dict(moves)
        if stay and target == r:
            own = {0: 1, 1: 0, **swap_groups(chain, (0, 1))} if group == 0 else {0: 1, 1: 2, 2: 3, 3: 0, **swap_groups(chain, range(4))}
        else:
            own.update({g: g for g in stay})
        pairs += [
            (source * rows + r, dest * rows + (target if source == group or source in stay and target != r else r))
            for source, dest in own.items()
        ]
    return pairs


def first_pairs(mate, chain, rows):
    pairs = []
    for r in range(rows):
        target = mate(r, rows)
        if target == r:
            moves = swap_groups(chain)
        else:
            pairs.append((r, target))
            moves = swap_groups(chain, range(4))
            moves.update({1: 2, 2: 3, 3: 1})
        pairs += [(a * rows + r, b * rows + r) for a, b in moves.items()]
    return pairs


def inner_pairs(mate, chain, rows):
    pairs = []
    for r in range(rows):
        target = mate(r, rows)
        if target == r:
            moves = swap_groups(chain)
        else:
            pairs += [(g * rows + r, g * rows + target) for g in (1, 2)]
            moves = swap_groups(chain, range(4))
            moves.update({0: 3, 3: 0})
        pairs += [(a * rows + r, b * rows + r) for a, b in moves.items()]
    return pairs


def dot(a, b):
    return jnp.dot(a, b, preferred_element_type=jnp.float32)


def by_parity(odd, low_value, high_value, even_ref, odd_ref):
    @pl.when(odd == 0)
    def _():
        even_ref[...] = high_value()
        odd_ref[...] = low_value()

    @pl.when(odd == 1)
    def _():
        even_ref[...] = low_value()
        odd_ref[...] = high_value()


def first_kernel(meta, inverse_hbm, right_hbm, solved, *rest):
    *sends, inverse, right, sems = rest
    count = inverse.shape[0]
    parts = 2
    size = count // parts
    loads = []
    for part in range(parts):
        rows = pl.ds(part * size, size)
        loads.append(
            (
                pltpu.make_async_copy(inverse_hbm.at[0, rows], inverse.at[rows], sems.at[0, part]),
                pltpu.make_async_copy(right_hbm.at[0, rows], right.at[rows], sems.at[1, part]),
            )
        )
    for pair in loads:
        for load in pair:
            load.start()
    for part in range(parts):
        for load in loads[part]:
            load.wait()
        for q in range(part * size, (part + 1) * size):
            solved[q] = dot(inverse[q], right[q]).astype(solved.dtype)
    by_parity(meta[1], lambda: solved[:REACH], lambda: solved[count - REACH :], *sends)


def premultiply(depend, scale, lower, inverse, wide, acc, level, q, half, keep=None):
    block = lower.shape[-1]
    terms = lower.shape[2]
    acc[...] = jnp.zeros_like(acc)
    beside = jnp.concatenate([lower[0, half, k] for k in range(terms)], axis=1)
    products = dot(inverse[0, half], beside)
    for k in range(terms):
        acc[depend[level, q, k]] += scale[level, q, k] * products[:, k * block : (k + 1) * block]
    at = slice(half * block, (half + 1) * block)
    for d in range(SPAN):
        value = (-acc[d]).astype(wide.dtype)
        wide[0, at, (d + half) * block : (d + half + 1) * block] = value
        if keep is not None:
            keep[half, d] = value
    other = 0 if half else SPAN
    wide[0, at, other * block : (other + 1) * block] = jnp.zeros((block, block), wide.dtype)


def prepare_a_kernel(meta, depend, scale, lower, inverse, first, wide, even_out, odd_out, acc, keep):
    step = pl.program_id(0)
    last = pl.num_programs(0) - 1
    block = lower.shape[-1]
    for half in range(2):
        premultiply(depend, scale, lower, inverse, wide, acc, 0, 2 * step + half, half, keep)

    def emit(ref):
        for half in range(2):
            for d in range(SPAN):
                ref[half * EDGE + d] = keep[half, d]
            for chunk in range(CHUNKS):
                ref[half * EDGE + SPAN + chunk] = first[half, :, chunk * block : (chunk + 1) * block]

    odd = meta[1]
    at_low, at_high = step == 0, step == last

    @pl.when((at_low & (odd == 1)) | (at_high & (odd == 0)))
    def _():
        emit(even_out)

    @pl.when((at_low & (odd == 0)) | (at_high & (odd == 1)))
    def _():
        emit(odd_out)


def prepare_b_kernel(depend, scale, lower, inverse, right, wide, base, acc):
    step = pl.program_id(0)
    for half in range(2):
        premultiply(depend, scale, lower, inverse, wide, acc, 1, 2 * step + half, half)
        base[half] = dot(inverse[0, half], right[0, half])


def order_kernel(applies, meta, *refs):
    *pieces, edges = refs

    @pl.when(applies(meta[0]))
    def _():
        odd = meta[1]
        size = pieces[0].shape[0]
        for i in range(len(pieces) // 2):
            edges[1 - odd, i * size : (i + 1) * size] = pieces[2 * i][...]
            edges[odd, i * size : (i + 1) * size] = pieces[2 * i + 1][...]


def flat(ref, start, count, at=slice(None)):
    block = ref[start : start + count, :, at]
    return block.reshape(count * block.shape[1], block.shape[2])


def place(window, odd, even_in, odd_in, at=slice(None)):
    halo = even_in.shape[0]
    low, high = 0, window.shape[0] - halo
    window[pl.ds(jnp.where(odd == 1, low, high), halo)] = even_in[:, :, at]
    window[pl.ds(jnp.where(odd == 1, high, low), halo)] = odd_in[:, :, at]


def second_level(wide_b, base_b, level_a, solved, at):
    for p in range(wide_b.shape[0]):
        rows = dot(wide_b[p], flat(level_a, 2 * p, SPAN + 1)) + flat(base_b, 2 * p, 2, at)
        solved[2 * p : 2 * p + 2] = rows.astype(solved.dtype).reshape(2, *solved.shape[1:])


def emit_sends(odd, solved, sends):
    half = solved.shape[0] // 2
    if sends:
        by_parity(odd, lambda: solved[:half], lambda: solved[half:], *sends)


def store(first_level, second, out, at, sems):
    copies = [
        pltpu.make_async_copy(source, out.at[level, :, :, at], sems.at[level])
        for level, source in ((0, first_level), (1, second))
    ]
    for copy in copies:
        copy.start()
    for copy in copies:
        copy.wait()


def ride(turn, meta, even_w, odd_w, sends):
    size = sends[0].shape[0]

    @pl.when(meta[0] > 2)
    def _():
        for send, source in zip(sends, (even_w, odd_w)):
            send[...] = source[turn * size : (turn + 1) * size]


def first_step(chunk, meta, first, even_in, odd_in, wide_b, base_b, even_w, odd_w, *rest):
    solved, even_out, odd_out, level_a = rest[-4:]

    @pl.when(meta[0] == 0)
    def _():
        cases = solved.shape[-1]
        at = slice(chunk * cases, (chunk + 1) * cases)
        count = first.shape[0]
        level_a[REACH : REACH + count] = first[:, :, at]
        place(level_a, meta[1], even_in, odd_in, at)
        second_level(wide_b, base_b, level_a, solved, at)
        emit_sends(meta[1], solved, (even_out, odd_out))

    ride(chunk, meta, even_w, odd_w, (even_out, odd_out))


def later_step(group, chunk, final, aliased, meta, centre, even_in, odd_in, edges, first, wide_a, wide_b, base_b, old_a, old_b, even_w, odd_w, *rest):
    rest = rest[1:] if aliased else rest
    out, solved, solved_a, *sends, window, level_a, sems = rest
    cases = solved.shape[-1]
    at = slice(chunk * cases, (chunk + 1) * cases)
    on_out = pl.ds(chunk * cases, cases)
    count = first.shape[0]

    @pl.when(meta[0] == group)
    def _():
        odd = meta[1]
        halo = 2 * REACH
        window[halo : halo + count] = centre[...]
        place(window, odd, even_in, odd_in)
        for p in range(wide_a.shape[0]):
            rows = dot(wide_a[p], flat(window, REACH + 2 * p, SPAN + 1)) + flat(first, 2 * p, 2, at).astype(jnp.float32)
            level_a[REACH + 2 * p : REACH + 2 * p + 2] = rows.astype(level_a.dtype).reshape(2, *level_a.shape[1:])
        for side in range(2):
            for i in range(REACH):
                put = side * (count + REACH) + i
                base = edges[side, i * EDGE + SPAN + chunk]
                blocks = jnp.concatenate([edges[side, i * EDGE + d] for d in range(SPAN)], axis=1)
                row = dot(blocks, flat(window, put, SPAN)) + base.astype(jnp.float32)
                level_a[put] = row.astype(level_a.dtype)
        second_level(wide_b, base_b, level_a, solved, at)
        emit_sends(odd, solved, sends)
        if final:
            store(level_a.at[pl.ds(REACH, count)], solved, out, on_out, sems)
        else:
            solved_a[...] = level_a[REACH : REACH + count]

    @pl.when(meta[0] == group - 1)
    def _():
        if group == 1:
            store(old_a.at[:, :, on_out], old_b, out, on_out, sems)
        else:
            store(old_a, old_b, out, on_out, sems)

    if group == 1 and not final:
        ride(CHUNKS + chunk, meta, even_w, odd_w, sends)


def shaped(shape, dtype=jnp.bfloat16):
    return jax.ShapeDtypeStruct(shape, dtype)


def params(**more):
    return pltpu.CompilerParams(vmem_limit_bytes=24 * 1024 * 1024, **more)


def in_hbm(value):
    return pltpu.with_memory_space_constraint(value, pltpu.HBM)


def after(values, *earlier):
    return lax.optimization_barrier((values, earlier))[0]


def per_device(chain, rows, right_side, lower_blocks, block_scale, diag_inverse, depend_rows):
    _, count, block, cases = right_side.shape
    terms = lower_blocks.shape[2]
    width = SPAN * block
    part = cases // CHUNKS
    row = lax.axis_index("rows")
    meta = jnp.stack([lax.axis_index("chain"), row % 2]).astype(jnp.int32)
    offset = depend_rows - (row * count + jnp.arange(count, dtype=jnp.int32))[None, :, None] + REACH
    offset = jnp.clip(offset, 0, SPAN - 1)
    right_side, lower_blocks, diag_inverse = in_hbm(right_side), in_hbm(lower_blocks), in_hbm(diag_inverse)
    mates = (even_mate, odd_mate)

    first, *sides = pl.pallas_call(
        first_kernel,
        in_specs=[SMEM, HBM, HBM],
        out_specs=[VMEM] * 3,
        out_shape=[shaped((count, block, cases))] + [shaped((REACH, block, cases))] * 2,
        scratch_shapes=[
            pltpu.VMEM((count, block, block), jnp.bfloat16),
            pltpu.VMEM((count, block, cases), jnp.bfloat16),
            pltpu.SemaphoreType.DMA((2, 2)),
        ],
        compiler_params=params(),
        name="first_level",
    )(meta, diag_inverse, right_side)
    sides = [lax.ppermute(side, AXES, first_pairs(mate, chain, rows)) for side, mate in zip(sides, mates)]

    pairs = count // 2
    wide_shape = shaped((pairs, 2 * block, width + block))
    wide_spec = pl.BlockSpec((1, 2 * block, width + block), lambda i: (i, 0, 0))
    halo = 2 * REACH
    pieces = 2 * CHUNKS * halo
    edge_shape = shaped((pieces, block, block))
    edge_spec = pl.BlockSpec((pieces, block, block), lambda i: (0, 0, 0))

    def of_level(level):
        return [
            pl.BlockSpec((1, 2, terms, block, block), lambda i: (level, i, 0, 0, 0)),
            pl.BlockSpec((1, 2, block, block), lambda i: (level, i, 0, 0)),
        ]

    def ordered(applies, moved):
        return pl.pallas_call(
            functools.partial(order_kernel, applies),
            in_specs=[SMEM] + [VMEM] * len(moved),
            out_specs=VMEM,
            out_shape=shaped((2, *edge_shape.shape)),
            compiler_params=params(),
            name="order",
        )(meta, *moved)

    acc = pltpu.VMEM((SPAN, block, block), jnp.float32)
    wide_a, *edge_w = pl.pallas_call(
        prepare_a_kernel,
        grid=(pairs,),
        in_specs=[SMEM, SMEM, SMEM, *of_level(0), pl.BlockSpec((2, block, cases), lambda i: (i, 0, 0))],
        out_specs=[wide_spec, edge_spec, edge_spec],
        out_shape=[wide_shape, edge_shape, edge_shape],
        scratch_shapes=[acc, pltpu.VMEM((2, SPAN, block, block), jnp.bfloat16)],
        compiler_params=params(),
        name="prepare_a",
    )(meta, offset, block_scale, lower_blocks, diag_inverse, first)
    moved_w = [lax.ppermute(value, AXES, inner_pairs(mate, chain, rows)) for value, mate in zip(edge_w, mates)]
    wide_b, base_b = pl.pallas_call(
        prepare_b_kernel,
        grid=(pairs,),
        in_specs=[SMEM, SMEM, *of_level(1), pl.BlockSpec((1, 2, block, cases), lambda i: (1, i, 0, 0))],
        out_specs=[wide_spec, pl.BlockSpec((2, block, cases), lambda i: (i, 0, 0))],
        out_shape=[wide_shape, shaped((count, block, cases), jnp.float32)],
        scratch_shapes=[acc],
        compiler_params=params(),
        name="prepare_b",
    )(offset, block_scale, lower_blocks, diag_inverse, right_side)

    level_a = pltpu.VMEM((count + 2 * REACH, block, part), jnp.bfloat16)
    solved_shape = shaped((count, block, part))
    send_shape = shaped((halo, block, part))

    sent, made_a = [], [first] * CHUNKS
    for chunk in range(CHUNKS):
        sent.append(
            pl.pallas_call(
                functools.partial(first_step, chunk),
                in_specs=[SMEM] + [VMEM] * 7 + [ANY] * chunk,
                out_specs=[VMEM] * 3,
                out_shape=[solved_shape, send_shape, send_shape],
                scratch_shapes=[level_a],
                compiler_params=params(),
                name=f"step_0_{chunk}",
            )(meta, first, *sides, wide_b, base_b, *edge_w, *(values[0] for values in sent))
        )
    edges = ordered(lambda group: (group == 1) | (group == 2), moved_w)

    def travel(group, chunk, before_sides, before_centre):
        solved, *halves = sent[chunk]
        halves = after(halves, before_sides)
        side = [
            lax.ppermute(value, AXES, hop_pairs(group, mate, chain, rows, True))
            for value, mate in zip(halves, mates)
        ]
        centre = lax.ppermute(
            after(solved, before_centre), AXES, hop_pairs(group, same_row, chain, rows, False)
        )
        return [centre, *side]

    out = None
    flying = None
    ridden = []
    for group in range(1, chain):
        final = group == chain - 1
        arrived = [travel(group - 1, 0, [], [])]
        wait = moved_w if group == 1 else []
        arrived.append(travel(group - 1, 1, wait, wait))
        flying = arrived[1][0]
        if group < 3:
            ridden += [side for chunk in range(CHUNKS) for side in arrived[chunk][1:]]
        if group == 3:
            edges = ordered(lambda group: group > 2, after(ridden, sent))
        made = []
        for chunk in range(CHUNKS):
            outs = [solved_shape, solved_shape] + ([] if final else [send_shape] * 2)
            aliased = out is not None
            out, solved, level, *sends = pl.pallas_call(
                functools.partial(later_step, group, chunk, final, aliased),
                in_specs=[SMEM] + [VMEM] * 12 + [ANY] * aliased,
                out_specs=[ANY] + [VMEM] * len(outs),
                out_shape=[shaped(right_side.shape), *outs],
                scratch_shapes=[
                    pltpu.VMEM((count + 2 * halo, block, part), jnp.bfloat16),
                    level_a,
                    pltpu.SemaphoreType.DMA((2,)),
                ],
                input_output_aliases={13: 0} if aliased else {},
                compiler_params=params(),
                name=f"step_{group}_{chunk}",
            )(
                meta,
                *arrived[chunk],
                edges,
                first,
                wide_a,
                wide_b,
                base_b,
                made_a[chunk],
                sent[chunk][0],
                *edge_w,
                *([out] if aliased else []),
            )
            made.append(((solved, *sends), level))
        sent, made_a = [values[0] for values in made], [values[1] for values in made]
    return out


def solution(mesh):
    placed = (
        P("chain", "rows", None, None),
        P("chain", "rows", None, None, None),
        P("chain", "rows", None),
        P("chain", "rows", None, None),
        P("chain", "rows", None),
    )
    return jax.shard_map(
        functools.partial(per_device, mesh.shape["chain"], mesh.shape["rows"]),
        mesh=mesh,
        in_specs=placed,
        out_specs=P("chain", "rows", None, None),
        check_vma=False,
    )
```

```python
import functools

import jax
import jax.numpy as jnp
from jax import lax
from jax.experimental import pallas as pl
from jax.experimental.pallas import tpu as pltpu
from jax.sharding import PartitionSpec as P

REACH = 2
SPAN = 2 * REACH + 1
CHUNKS = 2
EDGE = SPAN + CHUNKS
AXES = ("chain", "rows")
VMEM = pl.BlockSpec(memory_space=pltpu.VMEM)
SMEM = pl.BlockSpec(memory_space=pltpu.SMEM)
ANY = pl.BlockSpec(memory_space=pl.ANY)
HBM = pl.BlockSpec(memory_space=pltpu.HBM)


def even_mate(row, rows):
    return row ^ 1


def odd_mate(row, rows):
    mate = row + 1 if row % 2 else row - 1
    return mate if 0 <= mate < rows else row


def same_row(row, rows):
    return row


def swap_groups(chain, taken=()):
    return {g: g ^ 1 for g in range(chain) if g not in taken}


def hop_pairs(group, mate, chain, rows):
    if group % 2 == 0:
        moves = swap_groups(chain)
    else:
        moves = swap_groups(chain, range(group - 1, group + 3))
        moves.update({group: group + 1, group - 1: group, group + 1: group + 2, group + 2: group - 1})
    return [
        (source * rows + r, target * rows + (mate(r, rows) if source == group else r))
        for source, target in moves.items()
        for r in range(rows)
    ]


def inner_pairs(groups, mate, chain, rows):
    pairs = []
    for r in range(rows):
        target = mate(r, rows)
        if target == r:
            moves = swap_groups(chain)
        else:
            pairs += [(g * rows + r, g * rows + target) for g in groups]
            others = [g for g in range(min(chain, 4)) if g not in groups]
            moves = dict(zip(others, others[1:] + others[:1]))
            moves.update(swap_groups(chain, [*range(4), *groups]))
        pairs += [(a * rows + r, b * rows + r) for a, b in moves.items()]
    return pairs


def dot(a, b):
    return jnp.dot(a, b, preferred_element_type=jnp.float32)


def by_parity(odd, low_value, high_value, even_ref, odd_ref):
    @pl.when(odd == 0)
    def _():
        even_ref[...] = high_value()
        odd_ref[...] = low_value()

    @pl.when(odd == 1)
    def _():
        even_ref[...] = low_value()
        odd_ref[...] = high_value()


def first_kernel(meta, inverse_hbm, right_hbm, solved, *rest):
    *sends, inverse, right, sems = rest
    count = inverse.shape[0]
    parts = 2
    size = count // parts
    loads = []
    for part in range(parts):
        rows = pl.ds(part * size, size)
        loads.append(
            (
                pltpu.make_async_copy(inverse_hbm.at[0, rows], inverse.at[rows], sems.at[0, part]),
                pltpu.make_async_copy(right_hbm.at[0, rows], right.at[rows], sems.at[1, part]),
            )
        )
    for pair in loads:
        for load in pair:
            load.start()
    for part in range(parts):
        for load in loads[part]:
            load.wait()
        for q in range(part * size, (part + 1) * size):
            solved[q] = dot(inverse[q], right[q]).astype(solved.dtype)
    by_parity(meta[1], lambda: solved[:REACH], lambda: solved[count - REACH :], *sends)


def premultiply(meta, depend, scale, lower, inverse, wide, acc, level, q, half, keep=None):
    block = lower.shape[-1]
    terms = lower.shape[2]
    acc[...] = jnp.zeros_like(acc)
    beside = jnp.concatenate([lower[level, half, k] for k in range(terms)], axis=1)
    products = dot(inverse[level, half], beside)
    for k in range(terms):
        column = jnp.clip(depend[k, level, q] - (meta[2] + q) + REACH, 0, SPAN - 1)
        acc[column] += scale[k, level, q] * products[:, k * block : (k + 1) * block]
    at = slice(half * block, (half + 1) * block)
    for d in range(SPAN):
        value = (-acc[d]).astype(wide.dtype)
        wide[0, at, (d + half) * block : (d + half + 1) * block] = value
        if keep is not None:
            keep[half, d] = value
    other = 0 if half else SPAN
    wide[0, at, other * block : (other + 1) * block] = jnp.zeros((block, block), wide.dtype)


def prepare_kernel(meta, depend, scale, lower, inverse, right, first, wide_a, wide_b, base, even_out, odd_out, acc, keep):
    step = pl.program_id(0)
    last = pl.num_programs(0) - 1
    block = lower.shape[-1]
    for half in range(2):
        for level, wide in ((0, wide_a), (1, wide_b)):
            premultiply(meta, depend, scale, lower, inverse, wide, acc, level, 2 * step + half, half, None if level else keep)
        base[half] = dot(inverse[1, half], right[0, half])

    def emit(ref):
        for half in range(2):
            for d in range(SPAN):
                ref[half * EDGE + d] = keep[half, d]
            for chunk in range(CHUNKS):
                ref[half * EDGE + SPAN + chunk] = first[half, :, chunk * block : (chunk + 1) * block]

    odd = meta[1]
    at_low, at_high = step == 0, step == last

    @pl.when((at_low & (odd == 1)) | (at_high & (odd == 0)))
    def _():
        emit(even_out)

    @pl.when((at_low & (odd == 0)) | (at_high & (odd == 1)))
    def _():
        emit(odd_out)


def order_kernel(meta, even_in, odd_in, edges):
    @pl.when(meta[0] > 1)
    def _():
        odd = meta[1]
        edges[1 - odd] = even_in[...]
        edges[odd] = odd_in[...]


def flat(ref, start, count, at=slice(None)):
    block = ref[start : start + count, :, at]
    return block.reshape(count * block.shape[1], block.shape[2])


def place(window, odd, even_in, odd_in, at=slice(None)):
    halo = even_in.shape[0]
    low, high = 0, window.shape[0] - halo
    window[pl.ds(jnp.where(odd == 1, low, high), halo)] = even_in[:, :, at]
    window[pl.ds(jnp.where(odd == 1, high, low), halo)] = odd_in[:, :, at]


def columns(chunk, cases):
    return slice(None) if chunk is None else slice(chunk * cases, (chunk + 1) * cases)


def first_of_group(wide_a, first, window, level_a, put, at):
    for p in range(wide_a.shape[0]):
        rows = dot(wide_a[p], flat(window, 2 * p, SPAN + 1)) + flat(first, 2 * p, 2, at).astype(jnp.float32)
        level_a[put + 2 * p : put + 2 * p + 2] = rows.astype(level_a.dtype).reshape(2, *level_a.shape[1:])


def second_of_group(wide_b, base_b, level_a, solved, at, ready=None):
    for p in range(wide_b.shape[0]):
        rows = dot(wide_b[p], flat(level_a, 2 * p, SPAN + 1)) + flat(base_b, 2 * p, 2, at)
        solved[2 * p : 2 * p + 2] = rows.astype(solved.dtype).reshape(2, *solved.shape[1:])
        if ready is not None:
            ready[p].start()


def emit_sends(odd, solved, sends):
    if sends:
        size = sends[0].shape[0]
        count = solved.shape[0]
        by_parity(odd, lambda: solved[:size], lambda: solved[count - size :], *sends)


def store(level_a, solved, out, at, sems):
    copies = [
        pltpu.make_async_copy(source, out.at[level, :, :, at], sems.at[level])
        for level, source in ((0, level_a), (1, solved))
    ]
    for copy in copies:
        copy.start()
    for copy in copies:
        copy.wait()


def exchanged_step(group, chunk, meta, own, even_in, odd_in, wide_b, base_b, solved, even_out, odd_out, level_a):
    @pl.when(meta[0] == group)
    def _():
        at = columns(chunk, solved.shape[-1])
        count = own.shape[0]
        level_a[REACH : REACH + count] = own[:, :, at]
        place(level_a, meta[1], even_in, odd_in, at)
        second_of_group(wide_b, base_b, level_a, solved, at)
        emit_sends(meta[1], solved, (even_out, odd_out))


def level_step(group, meta, centre, even_in, odd_in, first, wide_a, old_b, out, solved, even_out, odd_out, window, sems):
    count = first.shape[0]

    @pl.when(meta[0] == group)
    def _():
        window[REACH : REACH + count] = centre[...]
        place(window, meta[1], even_in, odd_in)
        first_of_group(wide_a, first, window, solved, 0, slice(None))
        emit_sends(meta[1], solved, (even_out, odd_out))

    @pl.when(meta[0] == group - 1)
    def _():
        store(first, old_b, out, slice(None), sems)


def later_step(group, chunk, final, meta, centre, even_in, odd_in, edges, first, wide_a, wide_b, base_b, old_a, old_b, out_in, out, solved, solved_a, *rest):
    *sends, window, level_a, sems = rest
    cases = solved.shape[-1]
    at = columns(chunk, cases)
    on_out = pl.ds(chunk * cases, cases)
    count = first.shape[0]

    @pl.when(meta[0] == group)
    def _():
        odd = meta[1]
        halo = 2 * REACH
        window[halo : halo + count] = centre[...]
        place(window, odd, even_in, odd_in)
        first_of_group(wide_a, first, window.at[pl.ds(REACH, count + halo)], level_a, REACH, at)
        copy_a, copies_b = None, None
        if final:
            copy_a = pltpu.make_async_copy(level_a.at[pl.ds(REACH, count)], out.at[0, :, :, on_out], sems.at[0])
            copies_b = [
                pltpu.make_async_copy(solved.at[pl.ds(p, 2)], out.at[1, pl.ds(p, 2), :, on_out], sems.at[1 + p // 2])
                for p in range(0, count, 2)
            ]
            copy_a.start()
        for side in range(2):
            for i in range(REACH):
                put = side * (count + REACH) + i
                base = edges[side, i * EDGE + SPAN + chunk]
                blocks = jnp.concatenate([edges[side, i * EDGE + d] for d in range(SPAN)], axis=1)
                row = dot(blocks, flat(window, put, SPAN)) + base.astype(jnp.float32)
                level_a[put] = row.astype(level_a.dtype)
        second_of_group(wide_b, base_b, level_a, solved, at, copies_b)
        emit_sends(odd, solved, sends)
        if final:
            copy_a.wait()
            for copy in copies_b:
                copy.wait()
        else:
            solved_a[...] = level_a[REACH : REACH + count]

    @pl.when(meta[0] == group - 1)
    def _():
        store(old_a.at[:, :, at] if old_a.shape[-1] > cases else old_a, old_b, out, on_out, sems)


def shaped(shape, dtype=jnp.bfloat16):
    return jax.ShapeDtypeStruct(shape, dtype)


def params(**more):
    return pltpu.CompilerParams(vmem_limit_bytes=24 * 1024 * 1024, **more)


def in_hbm(value):
    return pltpu.with_memory_space_constraint(value, pltpu.HBM)


def after(values, *earlier):
    return lax.optimization_barrier((values, earlier))[0]


def per_device(chain, rows, right_side, lower_blocks, block_scale, diag_inverse, depend_rows):
    _, count, block, cases = right_side.shape
    terms = lower_blocks.shape[2]
    width = SPAN * block
    part = cases // CHUNKS
    halo = 2 * REACH
    row = lax.axis_index("rows")
    meta = jnp.stack([lax.axis_index("chain"), row % 2, row * count]).astype(jnp.int32)
    depend = depend_rows.transpose(2, 0, 1)
    scale = block_scale.transpose(2, 0, 1)
    right_side, lower_blocks, diag_inverse = in_hbm(right_side), in_hbm(lower_blocks), in_hbm(diag_inverse)
    mates = (even_mate, odd_mate)

    def exchange(groups, values):
        return [lax.ppermute(value, AXES, inner_pairs(groups, mate, chain, rows)) for value, mate in zip(values, mates)]

    def travel(group, centre, sides):
        return [
            lax.ppermute(value, AXES, hop_pairs(group, mate, chain, rows))
            for value, mate in zip((centre, *sides), (same_row, *mates))
        ]

    def call(kernel, name, in_specs, out_shape, out_specs=None, **more):
        return pl.pallas_call(
            kernel,
            in_specs=in_specs,
            out_specs=out_specs or [VMEM] * len(out_shape),
            out_shape=out_shape,
            compiler_params=params(),
            name=name,
            **more,
        )

    whole, half = shaped((count, block, cases)), shaped((count, block, part))
    whole_edge, half_edge = shaped((REACH, block, cases)), shaped((halo, block, part))

    first, *sides = call(
        first_kernel,
        "first_level",
        [SMEM, HBM, HBM],
        [whole, whole_edge, whole_edge],
        scratch_shapes=[
            pltpu.VMEM((count, block, block), jnp.bfloat16),
            pltpu.VMEM(whole.shape, jnp.bfloat16),
            pltpu.SemaphoreType.DMA((2, 2)),
        ],
    )(meta, diag_inverse, right_side)
    sides = exchange([0], sides)

    pairs = count // 2
    wide_shape = shaped((pairs, 2 * block, width + block))
    wide_spec = pl.BlockSpec((1, 2 * block, width + block), lambda i: (i, 0, 0))
    edge_shape = shaped((REACH * EDGE, block, block))
    edge_spec = pl.BlockSpec(edge_shape.shape, lambda i: (0, 0, 0))

    wide_a, wide_b, base_b, *edge_w = call(
        prepare_kernel,
        "prepare",
        [
            SMEM,
            SMEM,
            SMEM,
            pl.BlockSpec((2, 2, terms, block, block), lambda i: (0, i, 0, 0, 0)),
            pl.BlockSpec((2, 2, block, block), lambda i: (0, i, 0, 0)),
            pl.BlockSpec((1, 2, block, cases), lambda i: (1, i, 0, 0)),
            pl.BlockSpec((2, block, cases), lambda i: (i, 0, 0)),
        ],
        [wide_shape, wide_shape, shaped((count, block, cases), jnp.float32), edge_shape, edge_shape],
        [wide_spec, wide_spec, pl.BlockSpec((2, block, cases), lambda i: (i, 0, 0)), edge_spec, edge_spec],
        grid=(pairs,),
        scratch_shapes=[pltpu.VMEM((SPAN, block, block), jnp.float32), pltpu.VMEM((2, SPAN, block, block), jnp.bfloat16)],
    )(meta, depend, scale, lower_blocks, diag_inverse, right_side, first)

    padded = pltpu.VMEM((count + halo, block, cases), jnp.bfloat16)
    padded_half = pltpu.VMEM((count + halo, block, part), jnp.bfloat16)
    solved, *sends = call(
        functools.partial(exchanged_step, 0, None),
        "step_0",
        [SMEM] + [VMEM] * 5,
        [whole, whole_edge, whole_edge],
        scratch_shapes=[padded],
    )(meta, first, *sides, wide_b, base_b)
    arrived = travel(0, solved, sends)

    edge_w = exchange(range(2, chain), after(edge_w, sides))
    edges, = call(order_kernel, "order", [SMEM, VMEM, VMEM], [shaped((2, *edge_shape.shape))])(meta, *edge_w)

    out, own, *sides = call(
        functools.partial(level_step, 1),
        "step_1",
        [SMEM] + [VMEM] * 6,
        [shaped(right_side.shape), whole, whole_edge, whole_edge],
        [ANY] + [VMEM] * 3,
        scratch_shapes=[padded, pltpu.SemaphoreType.DMA((2,))],
    )(meta, *arrived, first, wide_a, solved)
    sides = exchange([1], sides)
    made_a = [own] * CHUNKS
    sent = []
    for chunk in range(CHUNKS):
        sent.append(
            call(
                functools.partial(exchanged_step, 1, chunk),
                f"step_1_{chunk}",
                [SMEM] + [VMEM] * 5,
                [half, half_edge, half_edge],
                scratch_shapes=[padded_half],
            )(meta, own, *sides, wide_b, base_b)
        )

    for group in range(2, chain):
        final = group == chain - 1
        arrived = [travel(group - 1, solved, sends) for solved, *sends in sent]
        made = []
        for chunk in range(CHUNKS):
            outs = [half, half] + ([] if final else [half_edge] * 2)
            out, solved, level, *sends = call(
                functools.partial(later_step, group, chunk, final),
                f"step_{group}_{chunk}",
                [SMEM] + [VMEM] * 10 + [ANY],
                [shaped(right_side.shape), *outs],
                [ANY] + [VMEM] * len(outs),
                scratch_shapes=[
                    pltpu.VMEM((count + 2 * halo, block, part), jnp.bfloat16),
                    padded_half,
                    pltpu.SemaphoreType.DMA((1 + pairs,)),
                ],
                input_output_aliases={11: 0},
            )(meta, *arrived[chunk], edges, first, wide_a, wide_b, base_b, made_a[chunk], sent[chunk][0], out)
            made.append(((solved, *sends), level))
        sent, made_a = [values[0] for values in made], [values[1] for values in made]
    return out


def solution(mesh):
    placed = (
        P("chain", "rows", None, None),
        P("chain", "rows", None, None, None),
        P("chain", "rows", None),
        P("chain", "rows", None, None),
        P("chain", "rows", None),
    )
    return jax.shard_map(
        functools.partial(per_device, mesh.shape["chain"], mesh.shape["rows"]),
        mesh=mesh,
        in_specs=placed,
        out_specs=P("chain", "rows", None, None),
        check_vma=False,
    )
```

```python
import functools

import jax
import jax.numpy as jnp
from jax import lax
from jax.experimental import pallas as pl
from jax.experimental.pallas import tpu as pltpu
from jax.sharding import PartitionSpec as P

REACH = 2
SPAN = 2 * REACH + 1
CHUNKS = 2
EDGE = SPAN + CHUNKS
AXES = ("chain", "rows")
VMEM = pl.BlockSpec(memory_space=pltpu.VMEM)
SMEM = pl.BlockSpec(memory_space=pltpu.SMEM)
ANY = pl.BlockSpec(memory_space=pl.ANY)
HBM = pl.BlockSpec(memory_space=pltpu.HBM)


def even_mate(row, rows):
    return row ^ 1


def odd_mate(row, rows):
    mate = row + 1 if row % 2 else row - 1
    return mate if 0 <= mate < rows else row


def same_row(row, rows):
    return row


def swap_groups(chain, taken=()):
    return {g: g ^ 1 for g in range(chain) if g not in taken}


def hop_pairs(group, mate, chain, rows):
    if group % 2 == 0:
        moves = swap_groups(chain)
    else:
        moves = swap_groups(chain, range(group - 1, group + 3))
        moves.update({group: group + 1, group - 1: group, group + 1: group + 2, group + 2: group - 1})
    return [
        (source * rows + r, target * rows + (mate(r, rows) if source == group else r))
        for source, target in moves.items()
        for r in range(rows)
    ]


def inner_pairs(groups, mate, chain, rows, idle=None):
    pairs = []
    paired = [r for r in range(rows) if mate(r, rows) != r]
    for r in range(rows):
        if r not in paired:
            moves = swap_groups(chain)
        else:
            pairs += [(g * rows + r, g * rows + mate(r, rows)) for g in groups]
            if idle is None:
                others = [g for g in range(min(chain, 4)) if g not in groups]
                moves = dict(zip(others, others[1:] + others[:1]))
                moves.update(swap_groups(chain, [*range(4), *groups]))
            else:
                alike = [q for q in paired if q % 2 == r % 2]
                pairs.append((idle * rows + r, idle * rows + alike[(alike.index(r) + 1) % len(alike)]))
                moves = swap_groups(chain, [idle, *groups])
        pairs += [(a * rows + r, b * rows + r) for a, b in moves.items()]
    return pairs


def side_pairs(group, mate, chain, rows):
    return [
        (group * rows + r, (group + 1) * rows + mate(r, rows))
        for r in range(rows)
        if mate(r, rows) != r
    ]


def dot(a, b):
    return jnp.dot(a, b, preferred_element_type=jnp.float32)


def by_parity(odd, low_value, high_value, even_ref, odd_ref):
    @pl.when(odd == 0)
    def _():
        even_ref[...] = high_value()
        odd_ref[...] = low_value()

    @pl.when(odd == 1)
    def _():
        even_ref[...] = low_value()
        odd_ref[...] = high_value()


def first_kernel(meta, inverse_hbm, right_hbm, solved, *rest):
    *sends, inverse, right, sems = rest
    count = inverse.shape[0]
    parts = 2
    size = count // parts
    loads = []
    for part in range(parts):
        rows = pl.ds(part * size, size)
        loads.append(
            (
                pltpu.make_async_copy(inverse_hbm.at[0, rows], inverse.at[rows], sems.at[0, part]),
                pltpu.make_async_copy(right_hbm.at[0, rows], right.at[rows], sems.at[1, part]),
            )
        )
    for pair in loads:
        for load in pair:
            load.start()
    for part in range(parts):
        for load in loads[part]:
            load.wait()
        for q in range(part * size, (part + 1) * size):
            solved[q] = dot(inverse[q], right[q]).astype(solved.dtype)
    by_parity(meta[1], lambda: solved[:REACH], lambda: solved[count - REACH :], *sends)


def premultiply(meta, depend, scale, lower, inverse, wide, acc, level, q, half, keep=None):
    block = lower.shape[-1]
    terms = lower.shape[2]
    acc[...] = jnp.zeros_like(acc)
    beside = jnp.concatenate([lower[level, half, k] for k in range(terms)], axis=1)
    products = dot(inverse[level, half], beside)
    for k in range(terms):
        column = jnp.clip(depend[k, level, q] - (meta[2] + q) + REACH, 0, SPAN - 1)
        acc[column] += scale[k, level, q] * products[:, k * block : (k + 1) * block]
    at = slice(half * block, (half + 1) * block)
    for d in range(SPAN):
        value = (-acc[d]).astype(wide.dtype)
        wide[0, at, (d + half) * block : (d + half + 1) * block] = value
        if keep is not None:
            keep[half, d] = value
    other = 0 if half else SPAN
    wide[0, at, other * block : (other + 1) * block] = jnp.zeros((block, block), wide.dtype)


def prepare_kernel(meta, depend, scale, lower, inverse, right, first, wide_a, wide_b, base, even_out, odd_out, acc, keep):
    step = pl.program_id(0)
    last = pl.num_programs(0) - 1
    block = lower.shape[-1]

    @pl.when(meta[0] > 0)
    def _():
        for half in range(2):
            premultiply(meta, depend, scale, lower, inverse, wide_a, acc, 0, 2 * step + half, half, keep)

    for half in range(2):
        premultiply(meta, depend, scale, lower, inverse, wide_b, acc, 1, 2 * step + half, half)
        base[half] = dot(inverse[1, half], right[0, half])

    def emit(ref):
        for half in range(2):
            for d in range(SPAN):
                ref[half * EDGE + d] = keep[half, d]
            for chunk in range(CHUNKS):
                ref[half * EDGE + SPAN + chunk] = first[half, :, chunk * block : (chunk + 1) * block]

    odd = meta[1]
    at_low, at_high = step == 0, step == last

    @pl.when((at_low & (odd == 1)) | (at_high & (odd == 0)))
    def _():
        emit(even_out)

    @pl.when((at_low & (odd == 0)) | (at_high & (odd == 1)))
    def _():
        emit(odd_out)


def order_kernel(applies, meta, even_in, odd_in, edges):
    @pl.when(applies(meta[0]))
    def _():
        odd = meta[1]
        edges[1 - odd] = even_in[...]
        edges[odd] = odd_in[...]


def flat(ref, start, count, at=slice(None)):
    block = ref[start : start + count, :, at]
    return block.reshape(count * block.shape[1], block.shape[2])


def place(window, odd, even_in, odd_in, at=slice(None)):
    halo = even_in.shape[0]
    low, high = 0, window.shape[0] - halo
    window[pl.ds(jnp.where(odd == 1, low, high), halo)] = even_in[:, :, at]
    window[pl.ds(jnp.where(odd == 1, high, low), halo)] = odd_in[:, :, at]


def columns(chunk, cases):
    return slice(None) if chunk is None else slice(chunk * cases, (chunk + 1) * cases)


def first_of_group(wide_a, first, window, level_a, put, at):
    for p in range(wide_a.shape[0]):
        rows = dot(wide_a[p], flat(window, 2 * p, SPAN + 1)) + flat(first, 2 * p, 2, at).astype(jnp.float32)
        level_a[put + 2 * p : put + 2 * p + 2] = rows.astype(level_a.dtype).reshape(2, *level_a.shape[1:])


def second_of_group(wide_b, base_b, level_a, solved, at, done=None):
    for p in range(wide_b.shape[0]):
        rows = dot(wide_b[p], flat(level_a, 2 * p, SPAN + 1)) + flat(base_b, 2 * p, 2, at)
        solved[2 * p : 2 * p + 2] = rows.astype(solved.dtype).reshape(2, *solved.shape[1:])
        if done is not None:
            done(p)


def emit_sends(odd, solved, sends):
    if sends:
        size = sends[0].shape[0]
        count = solved.shape[0]
        by_parity(odd, lambda: solved[:size], lambda: solved[count - size :], *sends)


def store(level_a, solved, out, at, sems):
    copies = [
        pltpu.make_async_copy(source, out.at[level, :, :, at], sems.at[level])
        for level, source in ((0, level_a), (1, solved))
    ]
    for copy in copies:
        copy.start()
    for copy in copies:
        copy.wait()


def exchanged_step(group, chunk, meta, own, even_in, odd_in, wide_b, base_b, solved, even_out, odd_out, level_a):
    @pl.when(meta[0] == group)
    def _():
        at = columns(chunk, solved.shape[-1])
        count = own.shape[0]
        level_a[REACH : REACH + count] = own[:, :, at]
        place(level_a, meta[1], even_in, odd_in, at)
        second_of_group(wide_b, base_b, level_a, solved, at)
        emit_sends(meta[1], solved, (even_out, odd_out))


def level_step(group, meta, centre, even_in, odd_in, first, wide_a, old_b, out, solved, even_out, odd_out, window, sems):
    count = first.shape[0]

    @pl.when(meta[0] == group)
    def _():
        window[REACH : REACH + count] = centre[...]
        place(window, meta[1], even_in, odd_in)
        first_of_group(wide_a, first, window, solved, 0, slice(None))
        emit_sends(meta[1], solved, (even_out, odd_out))

    @pl.when(meta[0] == group - 1)
    def _():
        store(first, old_b, out, slice(None), sems)


def later_step(group, chunk, final, meta, centre, even_in, odd_in, edges, first, wide_a, wide_b, base_b, old_a, old_b, *rest):
    stages = final and chunk == CHUNKS - 1
    if stages:
        made_a, made_b, _, out, solved, solved_a, window, level_a, stage, sems = rest
    else:
        _, out, solved, solved_a, *sends, window, level_a, sems = rest
    cases = solved.shape[-1]
    at = columns(chunk, cases)
    on_out = pl.ds(chunk * cases, cases)
    count = first.shape[0]

    @pl.when(meta[0] == group)
    def _():
        odd = meta[1]
        halo = 2 * REACH
        window[halo : halo + count] = centre[...]
        place(window, odd, even_in, odd_in)
        first_of_group(wide_a, first, window.at[pl.ds(REACH, count + halo)], level_a, REACH, at)
        done, copies = None, []
        if stages:
            copies = [
                pltpu.make_async_copy(stage.at[level, pl.ds(2 * p, 2)], out.at[level, pl.ds(2 * p, 2)], sems.at[level, p])
                for level in range(2)
                for p in range(count // 2)
            ]
            before = slice(0, chunk * cases)
            stage[0, :, :, before] = made_a[...]
            stage[1, :, :, before] = made_b[...]
            stage[0, :, :, at] = level_a[REACH : REACH + count]
            for copy in copies[: count // 2]:
                copy.start()

            def done(p):
                stage[1, 2 * p : 2 * p + 2, :, at] = solved[2 * p : 2 * p + 2]
                copies[count // 2 + p].start()

        for side in range(2):
            for i in range(REACH):
                put = side * (count + REACH) + i
                base = edges[side, i * EDGE + SPAN + chunk]
                blocks = jnp.concatenate([edges[side, i * EDGE + d] for d in range(SPAN)], axis=1)
                row = dot(blocks, flat(window, put, SPAN)) + base.astype(jnp.float32)
                level_a[put] = row.astype(level_a.dtype)
        second_of_group(wide_b, base_b, level_a, solved, at, done)
        if stages:
            for copy in copies:
                copy.wait()
        else:
            emit_sends(odd, solved, sends)
            solved_a[...] = level_a[REACH : REACH + count]

    @pl.when(meta[0] == group - 1)
    def _():
        store(old_a.at[:, :, at] if old_a.shape[-1] > cases else old_a, old_b, out, on_out, *([sems.at[0]] if stages else [sems]))


def shaped(shape, dtype=jnp.bfloat16):
    return jax.ShapeDtypeStruct(shape, dtype)


def params(**more):
    return pltpu.CompilerParams(vmem_limit_bytes=24 * 1024 * 1024, **more)


def in_hbm(value):
    return pltpu.with_memory_space_constraint(value, pltpu.HBM)


def after(values, *earlier):
    return lax.optimization_barrier((values, earlier))[0]


def per_device(chain, rows, right_side, lower_blocks, block_scale, diag_inverse, depend_rows):
    _, count, block, cases = right_side.shape
    terms = lower_blocks.shape[2]
    width = SPAN * block
    part = cases // CHUNKS
    halo = 2 * REACH
    row = lax.axis_index("rows")
    meta = jnp.stack([lax.axis_index("chain"), row % 2, row * count]).astype(jnp.int32)
    depend = depend_rows.transpose(2, 0, 1)
    scale = block_scale.transpose(2, 0, 1)
    right_side, lower_blocks, diag_inverse = in_hbm(right_side), in_hbm(lower_blocks), in_hbm(diag_inverse)
    mates = (even_mate, odd_mate)

    def exchange(groups, values, idle=None):
        return [
            lax.ppermute(value, AXES, inner_pairs(groups, mate, chain, rows, idle))
            for value, mate in zip(values, mates)
        ]

    def travel(group, centre, sides):
        side_table = hop_pairs if group else side_pairs
        return [lax.ppermute(centre, AXES, hop_pairs(group, same_row, chain, rows))] + [
            lax.ppermute(value, AXES, side_table(group, mate, chain, rows)) for value, mate in zip(sides, mates)
        ]

    def call(kernel, name, in_specs, out_shape, out_specs=None, **more):
        return pl.pallas_call(
            kernel,
            in_specs=in_specs,
            out_specs=out_specs or [VMEM] * len(out_shape),
            out_shape=out_shape,
            compiler_params=params(),
            name=name,
            **more,
        )

    whole, half = shaped((count, block, cases)), shaped((count, block, part))
    whole_edge, half_edge = shaped((REACH, block, cases)), shaped((halo, block, part))

    first, *sides = call(
        first_kernel,
        "first_level",
        [SMEM, HBM, HBM],
        [whole, whole_edge, whole_edge],
        scratch_shapes=[
            pltpu.VMEM((count, block, block), jnp.bfloat16),
            pltpu.VMEM(whole.shape, jnp.bfloat16),
            pltpu.SemaphoreType.DMA((2, 2)),
        ],
    )(meta, diag_inverse, right_side)
    sides = exchange([0], sides)

    pairs = count // 2
    wide_shape = shaped((pairs, 2 * block, width + block))
    wide_spec = pl.BlockSpec((1, 2 * block, width + block), lambda i: (i, 0, 0))
    edge_shape = shaped((REACH * EDGE, block, block))
    edge_spec = pl.BlockSpec(edge_shape.shape, lambda i: (0, 0, 0))

    wide_a, wide_b, base_b, *edge_w = call(
        prepare_kernel,
        "prepare",
        [
            SMEM,
            SMEM,
            SMEM,
            pl.BlockSpec((2, 2, terms, block, block), lambda i: (0, i, 0, 0, 0)),
            pl.BlockSpec((2, 2, block, block), lambda i: (0, i, 0, 0)),
            pl.BlockSpec((1, 2, block, cases), lambda i: (1, i, 0, 0)),
            pl.BlockSpec((2, block, cases), lambda i: (i, 0, 0)),
        ],
        [wide_shape, wide_shape, shaped((count, block, cases), jnp.float32), edge_shape, edge_shape],
        [wide_spec, wide_spec, pl.BlockSpec((2, block, cases), lambda i: (i, 0, 0)), edge_spec, edge_spec],
        grid=(pairs,),
        scratch_shapes=[pltpu.VMEM((SPAN, block, block), jnp.float32), pltpu.VMEM((2, SPAN, block, block), jnp.bfloat16)],
    )(meta, depend, scale, lower_blocks, diag_inverse, right_side, first)

    padded = pltpu.VMEM((count + halo, block, cases), jnp.bfloat16)
    padded_half = pltpu.VMEM((count + halo, block, part), jnp.bfloat16)
    solved, *sends = call(
        functools.partial(exchanged_step, 0, None),
        "step_0",
        [SMEM] + [VMEM] * 5,
        [whole, whole_edge, whole_edge],
        scratch_shapes=[padded],
    )(meta, first, *sides, wide_b, base_b)
    arrived = travel(0, solved, sends)

    def ordered(applies, moved):
        kernel = functools.partial(order_kernel, applies)
        return call(kernel, "order", [SMEM, VMEM, VMEM], [shaped((2, *edge_shape.shape))])(meta, *moved)[0]

    early = exchange([2], after(edge_w, sides), 3)
    edges = [ordered(lambda group: group == 2, early)]
    if chain > 3:
        late = exchange(range(3, chain), after(edge_w, early), 2)
        edges.append(ordered(lambda group: group > 2, late))

    out, own, *sides = call(
        functools.partial(level_step, 1),
        "step_1",
        [SMEM] + [VMEM] * 6,
        [shaped(right_side.shape), whole, whole_edge, whole_edge],
        [ANY] + [VMEM] * 3,
        scratch_shapes=[padded, pltpu.SemaphoreType.DMA((2,))],
    )(meta, *arrived, first, wide_a, solved)
    sides = after(exchange([1], sides), early)
    made_a = [own] * CHUNKS
    sent = []
    for chunk in range(CHUNKS):
        sent.append(
            call(
                functools.partial(exchanged_step, 1, chunk),
                f"step_1_{chunk}",
                [SMEM] + [VMEM] * 5,
                [half, half_edge, half_edge],
                scratch_shapes=[padded_half],
            )(meta, own, *sides, wide_b, base_b)
        )

    for group in range(2, chain):
        final = group == chain - 1
        arrived = [travel(group - 1, solved, sends) for solved, *sends in sent]
        made = []
        for chunk in range(CHUNKS):
            outs = [half, half] + ([] if final else [half_edge] * 2)
            stages = final and chunk == CHUNKS - 1
            extra = [made[0][1], made[0][0][0]] if stages else []
            sems = (2, pairs) if stages else (2,)
            out, solved, level, *sends = call(
                functools.partial(later_step, group, chunk, final),
                f"step_{group}_{chunk}",
                [SMEM] + [VMEM] * (10 + len(extra)) + [ANY],
                [shaped(right_side.shape), *outs],
                [ANY] + [VMEM] * len(outs),
                scratch_shapes=[
                    pltpu.VMEM((count + 2 * halo, block, part), jnp.bfloat16),
                    padded_half,
                    *([pltpu.VMEM((2, count, block, cases), jnp.bfloat16)] if stages else []),
                    pltpu.SemaphoreType.DMA(sems),
                ],
                input_output_aliases={11 + len(extra): 0},
            )(
                meta,
                *arrived[chunk],
                edges[min(group, 3) - 2],
                first,
                wide_a,
                wide_b,
                base_b,
                made_a[chunk],
                sent[chunk][0],
                *extra,
                out,
            )
            made.append(((solved, *sends), level))
        sent, made_a = [values[0] for values in made], [values[1] for values in made]
    return out


def solution(mesh):
    placed = (
        P("chain", "rows", None, None),
        P("chain", "rows", None, None, None),
        P("chain", "rows", None),
        P("chain", "rows", None, None),
        P("chain", "rows", None),
    )
    return jax.shard_map(
        functools.partial(per_device, mesh.shape["chain"], mesh.shape["rows"]),
        mesh=mesh,
        in_specs=placed,
        out_specs=P("chain", "rows", None, None),
        check_vma=False,
    )
```

```python
import functools

import jax
import jax.numpy as jnp
from jax import lax
from jax.experimental import pallas as pl
from jax.experimental.pallas import tpu as pltpu
from jax.sharding import PartitionSpec as P

REACH = 2
SPAN = 2 * REACH + 1
AXES = ("chain", "rows")
VMEM = pl.BlockSpec(memory_space=pltpu.VMEM)
SMEM = pl.BlockSpec(memory_space=pltpu.SMEM)
ANY = pl.BlockSpec(memory_space=pl.ANY)
HBM = pl.BlockSpec(memory_space=pltpu.HBM)


def even_mate(row, rows):
    return row ^ 1


def odd_mate(row, rows):
    mate = row + 1 if row % 2 else row - 1
    return mate if 0 <= mate < rows else row


def same_row(row, rows):
    return row


def swap_groups(chain, taken=()):
    return {g: g ^ 1 for g in range(chain) if g not in taken}


def hop_pairs(group, mate, chain, rows):
    if group % 2 == 0:
        moves = swap_groups(chain)
    else:
        moves = swap_groups(chain, range(group - 1, group + 3))
        moves.update({group: group + 1, group - 1: group, group + 1: group + 2, group + 2: group - 1})
    return [
        (source * rows + r, target * rows + (mate(r, rows) if source == group else r))
        for source, target in moves.items()
        for r in range(rows)
    ]


def inner_pairs(groups, mate, chain, rows):
    pairs = []
    for r in range(rows):
        target = mate(r, rows)
        if target == r:
            moves = swap_groups(chain)
        else:
            pairs += [(g * rows + r, g * rows + target) for g in groups]
            others = [g for g in range(min(chain, 4)) if g not in groups]
            moves = dict(zip(others, others[1:] + others[:1]))
            moves.update(swap_groups(chain, [*range(4), *groups]))
        pairs += [(a * rows + r, b * rows + r) for a, b in moves.items()]
    return pairs


def dot(a, b):
    return jnp.dot(a, b, preferred_element_type=jnp.float32)


def by_parity(odd, low_value, high_value, even_ref, odd_ref):
    @pl.when(odd == 0)
    def _():
        even_ref[...] = high_value()
        odd_ref[...] = low_value()

    @pl.when(odd == 1)
    def _():
        even_ref[...] = low_value()
        odd_ref[...] = high_value()


def first_kernel(meta, inverse_hbm, right_hbm, solved, *rest):
    *sends, inverse, right, sems = rest
    count = inverse.shape[0]
    parts = 2
    size = count // parts
    loads = []
    for part in range(parts):
        rows = pl.ds(part * size, size)
        loads.append(
            (
                pltpu.make_async_copy(inverse_hbm.at[0, rows], inverse.at[rows], sems.at[0, part]),
                pltpu.make_async_copy(right_hbm.at[0, rows], right.at[rows], sems.at[1, part]),
            )
        )
    for pair in loads:
        for load in pair:
            load.start()
    for part in range(parts):
        for load in loads[part]:
            load.wait()
        for q in range(part * size, (part + 1) * size):
            solved[q] = dot(inverse[q], right[q]).astype(solved.dtype)
    by_parity(meta[1], lambda: solved[:REACH], lambda: solved[count - REACH :], *sends)


def premultiply(meta, depend, scale, lower, inverse, wide, acc, level, q, half, keep=None):
    block = lower.shape[-1]
    terms = lower.shape[2]
    acc[...] = jnp.zeros_like(acc)
    beside = jnp.concatenate([lower[0, half, k] for k in range(terms)], axis=1)
    products = dot(inverse[0, half], beside)
    for k in range(terms):
        column = jnp.clip(depend[k, level, q] - (meta[2] + q) + REACH, 0, SPAN - 1)
        acc[column] += scale[k, level, q] * products[:, k * block : (k + 1) * block]
    at = slice(half * block, (half + 1) * block)
    for d in range(SPAN):
        value = (-acc[d]).astype(wide.dtype)
        wide[0, at, (d + half) * block : (d + half + 1) * block] = value
        if keep is not None:
            keep[half, d] = value
    other = 0 if half else SPAN
    wide[0, at, other * block : (other + 1) * block] = jnp.zeros((block, block), wide.dtype)


def prepare_kernel(meta, depend, scale, lower, inverse, right, first, wide_b, wide_a, base, even_out, odd_out, acc, keep):
    step = pl.program_id(0)
    pairs = pl.num_programs(0) // 2
    block = lower.shape[-1]

    @pl.when(step < pairs)
    def _():
        for half in range(2):
            premultiply(meta, depend, scale, lower, inverse, wide_b, acc, 1, 2 * step + half, half)
            base[half] = dot(inverse[0, half], right[0, half])

    @pl.when((step >= pairs) & (meta[0] > 0))
    def _():
        for half in range(2):
            premultiply(meta, depend, scale, lower, inverse, wide_a, acc, 0, 2 * (step - pairs) + half, half, keep)

    def emit(ref):
        parts = first.shape[2] // block
        size = SPAN + parts
        for half in range(2):
            for d in range(SPAN):
                ref[half * size + d] = keep[half, d]
            for part in range(parts):
                ref[half * size + SPAN + part] = first[half, :, part * block : (part + 1) * block]

    odd = meta[1]
    at_low, at_high = step == pairs, step == 2 * pairs - 1

    @pl.when((meta[0] > 1) & ((at_low & (odd == 1)) | (at_high & (odd == 0))))
    def _():
        emit(even_out)

    @pl.when((meta[0] > 1) & ((at_low & (odd == 0)) | (at_high & (odd == 1))))
    def _():
        emit(odd_out)


def order_kernel(meta, even_in, odd_in, edges):
    @pl.when(meta[0] > 1)
    def _():
        odd = meta[1]
        size = edges.shape[1]
        edges[1 - odd] = even_in[:size]
        edges[odd] = odd_in[:size]


def flat(ref, start, count):
    block = ref[start : start + count]
    return block.reshape(count * block.shape[1], block.shape[2])


def place(window, odd, even_in, odd_in):
    halo = even_in.shape[0]
    low, high = 0, window.shape[0] - halo
    window[pl.ds(jnp.where(odd == 1, low, high), halo)] = even_in[...]
    window[pl.ds(jnp.where(odd == 1, high, low), halo)] = odd_in[...]


def level(wide, base, window, solved, put, done=None):
    for p in range(wide.shape[0]):
        rows = dot(wide[p], flat(window, 2 * p, SPAN + 1)) + flat(base, 2 * p, 2).astype(jnp.float32)
        solved[put + 2 * p : put + 2 * p + 2] = rows.astype(solved.dtype).reshape(2, *solved.shape[1:])
        if done is not None:
            done(p)


def emit_sends(odd, solved, sends):
    if sends:
        size = sends[0].shape[0]
        count = solved.shape[0]
        by_parity(odd, lambda: solved[:size], lambda: solved[count - size :], *sends)


def store(level_a, solved, out, sems):
    copies = [
        pltpu.make_async_copy(source, out.at[at], sems.at[at]) for at, source in ((0, level_a), (1, solved))
    ]
    for copy in copies:
        copy.start()
    for copy in copies:
        copy.wait()


def exchanged_step(group, meta, own, even_in, odd_in, wide_b, base_b, solved, even_out, odd_out, level_a):
    @pl.when(meta[0] == group)
    def _():
        level_a[REACH : REACH + own.shape[0]] = own[...]
        place(level_a, meta[1], even_in, odd_in)
        level(wide_b, base_b, level_a, solved, 0)
        emit_sends(meta[1], solved, (even_out, odd_out))


def level_step(group, meta, centre, even_in, odd_in, first, wide_a, old_b, out, solved, even_out, odd_out, window, sems):
    @pl.when(meta[0] == group)
    def _():
        window[REACH : REACH + first.shape[0]] = centre[...]
        place(window, meta[1], even_in, odd_in)
        level(wide_a, first, window, solved, 0)
        emit_sends(meta[1], solved, (even_out, odd_out))

    @pl.when(meta[0] == group - 1)
    def _():
        store(first, old_b, out, sems)


def later_step(group, final, meta, centre, even_in, odd_in, edges, first, wide_a, wide_b, base_b, old_a, old_b, _, out, solved, solved_a, *rest):
    *sends, window, level_a, sems = rest
    count, block, cases = first.shape

    @pl.when(meta[0] == group)
    def _():
        odd = meta[1]
        halo = 2 * REACH
        window[halo : halo + count] = centre[...]
        place(window, odd, even_in, odd_in)
        level(wide_a, first, window.at[pl.ds(REACH, count + halo)], level_a, REACH)
        done, copies = None, []
        if final:
            copies = [pltpu.make_async_copy(level_a.at[pl.ds(REACH, count)], out.at[0], sems.at[0])]
            copies += [
                pltpu.make_async_copy(solved.at[pl.ds(2 * p, 2)], out.at[1, pl.ds(2 * p, 2)], sems.at[1 + p])
                for p in range(count // 2)
            ]
            copies[0].start()

            def done(p):
                copies[1 + p].start()

        parts = cases // block
        size = SPAN + parts
        for side in range(2):
            for i in range(REACH):
                put = side * (count + REACH) + i
                base = jnp.concatenate([edges[side, i * size + SPAN + part] for part in range(parts)], axis=1)
                blocks = jnp.concatenate([edges[side, i * size + d] for d in range(SPAN)], axis=1)
                row = dot(blocks, flat(window, put, SPAN)) + base.astype(jnp.float32)
                level_a[put] = row.astype(level_a.dtype)
        level(wide_b, base_b, level_a, solved, 0, done)
        if final:
            for copy in copies:
                copy.wait()
        else:
            emit_sends(odd, solved, sends)
            solved_a[...] = level_a[REACH : REACH + count]

    @pl.when(meta[0] == group - 1)
    def _():
        store(old_a, old_b, out, sems)


def shaped(shape, dtype=jnp.bfloat16):
    return jax.ShapeDtypeStruct(shape, dtype)


def params(**more):
    return pltpu.CompilerParams(vmem_limit_bytes=24 * 1024 * 1024, **more)


def in_hbm(value):
    return pltpu.with_memory_space_constraint(value, pltpu.HBM)


def after(values, *earlier):
    return lax.optimization_barrier((values, earlier))[0]


def per_device(chain, rows, right_side, lower_blocks, block_scale, diag_inverse, depend_rows):
    _, count, block, cases = right_side.shape
    terms = lower_blocks.shape[2]
    width = SPAN * block
    halo = 2 * REACH
    row = lax.axis_index("rows")
    meta = jnp.stack([lax.axis_index("chain"), row % 2, row * count]).astype(jnp.int32)
    depend = depend_rows.transpose(2, 0, 1)
    scale = block_scale.transpose(2, 0, 1)
    right_side, lower_blocks, diag_inverse = in_hbm(right_side), in_hbm(lower_blocks), in_hbm(diag_inverse)
    mates = (even_mate, odd_mate)

    def exchange(groups, values):
        return [lax.ppermute(value, AXES, inner_pairs(groups, mate, chain, rows)) for value, mate in zip(values, mates)]

    def travel(group, centre, sides):
        return [
            lax.ppermute(value, AXES, hop_pairs(group, mate, chain, rows))
            for value, mate in zip((centre, *sides), (same_row, *mates))
        ]

    def call(kernel, name, in_specs, out_shape, out_specs=None, **more):
        return pl.pallas_call(
            kernel,
            in_specs=in_specs,
            out_specs=out_specs or [VMEM] * len(out_shape),
            out_shape=out_shape,
            compiler_params=params(),
            name=name,
            **more,
        )

    whole, edge, wide_edge = (shaped((size, block, cases)) for size in (count, REACH, halo))

    first, *sides = call(
        first_kernel,
        "first_level",
        [SMEM, HBM, HBM],
        [whole, edge, edge],
        scratch_shapes=[
            pltpu.VMEM((count, block, block), jnp.bfloat16),
            pltpu.VMEM(whole.shape, jnp.bfloat16),
            pltpu.SemaphoreType.DMA((2, 2)),
        ],
    )(meta, diag_inverse, right_side)
    sides = exchange([0], sides)

    pairs = count // 2
    wide_shape = shaped((pairs, 2 * block, width + block))
    parts = REACH * (SPAN + cases // block)
    even_shape = shaped((parts, block, block))
    odd_shape = shaped((max(parts, count * cases // block + 1), block, block))

    def stage(i, meta):
        stays = (meta[0] == 0) | (i < pairs)
        return jnp.where(stays, 1, 0), jnp.where(stays, jnp.minimum(i, pairs - 1), i - pairs)

    def early(i):
        return jnp.minimum(i, pairs - 1)

    def late(i):
        return jnp.maximum(i - pairs, 0)

    wide_b, wide_a, base_b, *edge_w = pl.pallas_call(
        prepare_kernel,
        grid_spec=pltpu.PrefetchScalarGridSpec(
            num_scalar_prefetch=1,
            grid=(2 * pairs,),
            in_specs=[
                SMEM,
                SMEM,
                pl.BlockSpec((1, 2, terms, block, block), lambda i, meta: (*stage(i, meta), 0, 0, 0)),
                pl.BlockSpec((1, 2, block, block), lambda i, meta: (*stage(i, meta), 0, 0)),
                pl.BlockSpec((1, 2, block, cases), lambda i, meta: (1, early(i), 0, 0)),
                pl.BlockSpec((2, block, cases), lambda i, meta: (late(i), 0, 0)),
            ],
            out_specs=[
                pl.BlockSpec((1, 2 * block, width + block), lambda i, meta: (early(i), 0, 0)),
                pl.BlockSpec((1, 2 * block, width + block), lambda i, meta: (late(i), 0, 0)),
                pl.BlockSpec((2, block, cases), lambda i, meta: (early(i), 0, 0)),
                pl.BlockSpec(even_shape.shape, lambda i, meta: (0, 0, 0)),
                pl.BlockSpec(odd_shape.shape, lambda i, meta: (0, 0, 0)),
            ],
            scratch_shapes=[
                pltpu.VMEM((SPAN, block, block), jnp.float32),
                pltpu.VMEM((2, SPAN, block, block), jnp.bfloat16),
            ],
        ),
        out_shape=[wide_shape, wide_shape, shaped(whole.shape, jnp.float32), even_shape, odd_shape],
        compiler_params=params(),
        name="prepare",
    )(meta, depend, scale, lower_blocks, diag_inverse, right_side, first)

    padded = pltpu.VMEM((count + halo, block, cases), jnp.bfloat16)
    solved, *sends = call(
        functools.partial(exchanged_step, 0),
        "step_0",
        [SMEM] + [VMEM] * 5,
        [whole, edge, edge],
        scratch_shapes=[padded],
    )(meta, first, *sides, wide_b, base_b)
    arrived = travel(0, solved, sends)

    even_w, odd_w = edge_w
    even_w = lax.ppermute(after(even_w, sides), AXES, inner_pairs(range(2, chain), even_mate, chain, rows))
    odd_w = lax.ppermute(after(odd_w, even_w), AXES, inner_pairs(range(2, chain), odd_mate, chain, rows))
    arrived = after(arrived, even_w)
    edges = call(
        order_kernel,
        "order",
        [SMEM, VMEM, VMEM],
        [shaped((2, *even_shape.shape))],
    )(meta, even_w, odd_w)[0]

    out, made_a, *sides = call(
        functools.partial(level_step, 1),
        "step_1_a",
        [SMEM] + [VMEM] * 6,
        [shaped(right_side.shape), whole, edge, edge],
        [ANY] + [VMEM] * 3,
        scratch_shapes=[padded, pltpu.SemaphoreType.DMA((2,))],
    )(meta, *arrived, first, wide_a, solved)
    solved, *sends = call(
        functools.partial(exchanged_step, 1),
        "step_1_b",
        [SMEM] + [VMEM] * 5,
        [whole, wide_edge, wide_edge],
        scratch_shapes=[padded],
    )(meta, made_a, *exchange([1], sides), wide_b, base_b)

    for group in range(2, chain):
        final = group == chain - 1
        outs = [whole, whole] + ([] if final else [wide_edge] * 2)
        out, *now = call(
            functools.partial(later_step, group, final),
            f"step_{group}",
            [SMEM] + [VMEM] * 10 + [ANY],
            [shaped(right_side.shape), *outs],
            [ANY] + [VMEM] * len(outs),
            scratch_shapes=[
                pltpu.VMEM((count + 2 * halo, block, cases), jnp.bfloat16),
                padded,
                pltpu.SemaphoreType.DMA((1 + pairs,)),
            ],
            input_output_aliases={11: 0},
        )(meta, *travel(group - 1, solved, sends), edges, first, wide_a, wide_b, base_b, made_a, solved, out)
        solved, made_a, *sends = now
    return out


def solution(mesh):
    placed = (
        P("chain", "rows", None, None),
        P("chain", "rows", None, None, None),
        P("chain", "rows", None),
        P("chain", "rows", None, None),
        P("chain", "rows", None),
    )
    return jax.shard_map(
        functools.partial(per_device, mesh.shape["chain"], mesh.shape["rows"]),
        mesh=mesh,
        in_specs=placed,
        out_specs=P("chain", "rows", None, None),
        check_vma=False,
    )
```

```python
import functools

import jax
import jax.numpy as jnp
from jax import lax
from jax.experimental import pallas as pl
from jax.experimental.pallas import tpu as pltpu
from jax.sharding import PartitionSpec as P

REACH = 2
SPAN = 2 * REACH + 1
AXES = ("chain", "rows")
VMEM = pl.BlockSpec(memory_space=pltpu.VMEM)
SMEM = pl.BlockSpec(memory_space=pltpu.SMEM)
ANY = pl.BlockSpec(memory_space=pl.ANY)
HBM = pl.BlockSpec(memory_space=pltpu.HBM)


def even_mate(row, rows):
    return row ^ 1


def odd_mate(row, rows):
    mate = row + 1 if row % 2 else row - 1
    return mate if 0 <= mate < rows else row


def same_row(row, rows):
    return row


def swap_groups(chain, taken=()):
    return {g: g ^ 1 for g in range(chain) if g not in taken}


def hop_pairs(group, mate, chain, rows):
    if group % 2 == 0:
        moves = swap_groups(chain)
    else:
        moves = swap_groups(chain, range(group - 1, group + 3))
        moves.update({group: group + 1, group - 1: group, group + 1: group + 2, group + 2: group - 1})
    return [
        (source * rows + r, target * rows + (mate(r, rows) if source == group else r))
        for source, target in moves.items()
        for r in range(rows)
    ]


def inner_pairs(groups, mate, chain, rows, idle=None):
    pairs = []
    paired = [r for r in range(rows) if mate(r, rows) != r]
    for r in range(rows):
        if r not in paired:
            moves = swap_groups(chain)
        else:
            moves = swap_groups(chain, [*groups, idle])
            pairs += [(g * rows + r, g * rows + mate(r, rows)) for g in groups]
            if idle is not None:
                alike = [q for q in paired if q % 2 == r % 2]
                pairs.append((idle * rows + r, idle * rows + alike[(alike.index(r) + 1) % len(alike)]))
        pairs += [(a * rows + r, b * rows + r) for a, b in moves.items()]
    return pairs


def dot(a, b):
    return jnp.dot(a, b, preferred_element_type=jnp.float32)


def by_parity(odd, low_value, high_value, even_ref, odd_ref):
    @pl.when(odd == 0)
    def _():
        even_ref[...] = high_value()
        odd_ref[...] = low_value()

    @pl.when(odd == 1)
    def _():
        even_ref[...] = low_value()
        odd_ref[...] = high_value()


def first_kernel(meta, inverse_hbm, right_hbm, solved, *rest):
    *sends, inverse, right, sems = rest
    count = inverse.shape[0]
    parts = 2
    size = count // parts
    loads = []
    for part in range(parts):
        rows = pl.ds(part * size, size)
        loads.append(
            (
                pltpu.make_async_copy(inverse_hbm.at[0, rows], inverse.at[rows], sems.at[0, part]),
                pltpu.make_async_copy(right_hbm.at[0, rows], right.at[rows], sems.at[1, part]),
            )
        )
    for pair in loads:
        for load in pair:
            load.start()
    for part in range(parts):
        for load in loads[part]:
            load.wait()
        for q in range(part * size, (part + 1) * size):
            solved[q] = dot(inverse[q], right[q]).astype(solved.dtype)
    by_parity(meta[1], lambda: solved[:REACH], lambda: solved[count - REACH :], *sends)


def premultiply(meta, depend, scale, lower, inverse, wide, acc, level, p, half):
    block = lower.shape[-1]
    terms = lower.shape[2]
    q = 2 * p + half
    acc[...] = jnp.zeros_like(acc)
    beside = jnp.concatenate([lower[level, q, k] for k in range(terms)], axis=1)
    products = dot(inverse[level, q], beside)
    for k in range(terms):
        column = jnp.clip(depend[k, level, q] - (meta[2] + q) + REACH, 0, SPAN - 1)
        acc[column] += scale[k, level, q] * products[:, k * block : (k + 1) * block]
    at = slice(half * block, (half + 1) * block)
    for d in range(SPAN):
        wide[p, at, (d + half) * block : (d + half + 1) * block] = (-acc[d]).astype(wide.dtype)
    other = 0 if half else SPAN
    wide[p, at, other * block : (other + 1) * block] = jnp.zeros((block, block), wide.dtype)


def prepare_kernel(meta, depend, scale, lower_hbm, inverse_hbm, right_hbm, first, wide_b, wide_a, base, even_out, odd_out, lower, inverse, right, acc, sems):
    pairs = wide_a.shape[0]
    block = lower.shape[-1]

    def loads(level, p):
        rows = pl.ds(2 * p, 2)
        copies = [
            pltpu.make_async_copy(lower_hbm.at[level, rows], lower.at[level, rows], sems.at[level, 0, p]),
            pltpu.make_async_copy(inverse_hbm.at[level, rows], inverse.at[level, rows], sems.at[level, 1, p]),
        ]
        if level:
            copies.append(pltpu.make_async_copy(right_hbm.at[1, rows], right.at[rows], sems.at[level, 2, p]))
        return copies

    def start(level):
        for p in range(pairs):
            for copy in loads(level, p):
                copy.start()

    start(1)

    @pl.when(meta[0] > 0)
    def _():
        start(0)

    @pl.loop(0, pairs)
    def _(p):
        for copy in loads(1, p):
            copy.wait()
        for half in range(2):
            premultiply(meta, depend, scale, lower, inverse, wide_b, acc.at[half], 1, p, half)
            base[2 * p + half] = dot(inverse[1, 2 * p + half], right[2 * p + half])

    @pl.when(meta[0] > 0)
    def _():
        @pl.loop(0, pairs)
        def _(p):
            for copy in loads(0, p):
                copy.wait()
            for half in range(2):
                premultiply(meta, depend, scale, lower, inverse, wide_a, acc.at[half], 0, p, half)

    def emit(ref, p):
        parts = first.shape[2] // block
        size = SPAN + parts
        for half in range(2):
            for d in range(SPAN):
                column = (d + half) * block
                ref[half * size + d] = wide_a[p, half * block : (half + 1) * block, column : column + block]
            for part in range(parts):
                ref[half * size + SPAN + part] = first[2 * p + half, :, part * block : (part + 1) * block]

    @pl.when((meta[0] > 1) & (meta[1] == 1))
    def _():
        emit(even_out, 0)
        emit(odd_out, pairs - 1)

    @pl.when((meta[0] > 1) & (meta[1] == 0))
    def _():
        emit(odd_out, 0)
        emit(even_out, pairs - 1)


def order_kernel(meta, even_in, odd_in, edges):
    @pl.when(meta[0] > 1)
    def _():
        odd = meta[1]
        size = edges.shape[1]
        edges[1 - odd] = even_in[:size]
        edges[odd] = odd_in[:size]


def flat(ref, start, count):
    block = ref[start : start + count]
    return block.reshape(count * block.shape[1], block.shape[2])


def place(window, odd, even_in, odd_in):
    halo = even_in.shape[0]
    low, high = 0, window.shape[0] - halo
    window[pl.ds(jnp.where(odd == 1, low, high), halo)] = even_in[...]
    window[pl.ds(jnp.where(odd == 1, high, low), halo)] = odd_in[...]


def level(wide, base, window, solved, put, done=None):
    for p in range(wide.shape[0]):
        rows = dot(wide[p], flat(window, 2 * p, SPAN + 1)) + flat(base, 2 * p, 2).astype(jnp.float32)
        solved[put + 2 * p : put + 2 * p + 2] = rows.astype(solved.dtype).reshape(2, *solved.shape[1:])
        if done is not None:
            done(p)


def emit_sends(odd, solved, sends):
    if sends:
        size = sends[0].shape[0]
        count = solved.shape[0]
        by_parity(odd, lambda: solved[:size], lambda: solved[count - size :], *sends)


def store(level_a, solved, out, sems):
    copies = [
        pltpu.make_async_copy(source, out.at[at], sems.at[at]) for at, source in ((0, level_a), (1, solved))
    ]
    for copy in copies:
        copy.start()
    for copy in copies:
        copy.wait()


def exchanged_step(group, meta, own, even_in, odd_in, wide_b, base_b, solved, even_out, odd_out, level_a):
    @pl.when(meta[0] == group)
    def _():
        level_a[REACH : REACH + own.shape[0]] = own[...]
        place(level_a, meta[1], even_in, odd_in)
        level(wide_b, base_b, level_a, solved, 0)
        emit_sends(meta[1], solved, (even_out, odd_out))


def level_step(group, meta, centre, even_in, odd_in, first, wide_a, old_b, out, solved, even_out, odd_out, window, sems):
    @pl.when(meta[0] == group)
    def _():
        window[REACH : REACH + first.shape[0]] = centre[...]
        place(window, meta[1], even_in, odd_in)
        level(wide_a, first, window, solved, 0)
        emit_sends(meta[1], solved, (even_out, odd_out))

    @pl.when(meta[0] == group - 1)
    def _():
        store(first, old_b, out, sems)


def later_step(group, final, meta, centre, even_in, odd_in, edges, first, wide_a, wide_b, base_b, old_a, old_b, _, out, solved, solved_a, *rest):
    *sends, window, level_a, sems = rest
    count, block, cases = first.shape

    @pl.when(meta[0] == group)
    def _():
        odd = meta[1]
        halo = 2 * REACH
        window[halo : halo + count] = centre[...]
        place(window, odd, even_in, odd_in)
        level(wide_a, first, window.at[pl.ds(REACH, count + halo)], level_a, REACH)
        done, copies = None, []
        if final:
            copies = [pltpu.make_async_copy(level_a.at[pl.ds(REACH, count)], out.at[0], sems.at[0])]
            copies += [
                pltpu.make_async_copy(solved.at[pl.ds(2 * p, 2)], out.at[1, pl.ds(2 * p, 2)], sems.at[1 + p])
                for p in range(count // 2)
            ]
            copies[0].start()

            def done(p):
                copies[1 + p].start()

        parts = cases // block
        size = SPAN + parts
        for side in range(2):
            for i in range(REACH):
                put = side * (count + REACH) + i
                base = jnp.concatenate([edges[side, i * size + SPAN + part] for part in range(parts)], axis=1)
                blocks = jnp.concatenate([edges[side, i * size + d] for d in range(SPAN)], axis=1)
                row = dot(blocks, flat(window, put, SPAN)) + base.astype(jnp.float32)
                level_a[put] = row.astype(level_a.dtype)
        level(wide_b, base_b, level_a, solved, 0, done)
        if final:
            for copy in copies:
                copy.wait()
        else:
            emit_sends(odd, solved, sends)
            solved_a[...] = level_a[REACH : REACH + count]

    @pl.when(meta[0] == group - 1)
    def _():
        store(old_a, old_b, out, sems)


def shaped(shape, dtype=jnp.bfloat16):
    return jax.ShapeDtypeStruct(shape, dtype)


def params(**more):
    return pltpu.CompilerParams(vmem_limit_bytes=24 * 1024 * 1024, **more)


def in_hbm(value):
    return pltpu.with_memory_space_constraint(value, pltpu.HBM)


def after(values, *earlier):
    return lax.optimization_barrier((values, earlier))[0]


def per_device(chain, rows, right_side, lower_blocks, block_scale, diag_inverse, depend_rows):
    _, count, block, cases = right_side.shape
    width = SPAN * block
    halo = 2 * REACH
    row = lax.axis_index("rows")
    meta = jnp.stack([lax.axis_index("chain"), row % 2, row * count]).astype(jnp.int32)
    depend = depend_rows.transpose(2, 0, 1)
    scale = block_scale.transpose(2, 0, 1)
    right_side, lower_blocks, diag_inverse = in_hbm(right_side), in_hbm(lower_blocks), in_hbm(diag_inverse)
    mates = (even_mate, odd_mate)

    def exchange(groups, values, idle):
        return [
            lax.ppermute(value, AXES, inner_pairs(groups, mate, chain, rows, idle))
            for value, mate in zip(values, mates)
        ]

    def travel(group, centre, sides):
        return [
            lax.ppermute(value, AXES, hop_pairs(group, mate, chain, rows))
            for value, mate in zip((centre, *sides), (same_row, *mates))
        ]

    def call(kernel, name, in_specs, out_shape, out_specs=None, **more):
        return pl.pallas_call(
            kernel,
            in_specs=in_specs,
            out_specs=out_specs or [VMEM] * len(out_shape),
            out_shape=out_shape,
            compiler_params=params(),
            name=name,
            **more,
        )

    whole, edge, wide_edge = (shaped((size, block, cases)) for size in (count, REACH, halo))

    first, *sides = call(
        first_kernel,
        "first_level",
        [SMEM, HBM, HBM],
        [whole, edge, edge],
        scratch_shapes=[
            pltpu.VMEM((count, block, block), jnp.bfloat16),
            pltpu.VMEM(whole.shape, jnp.bfloat16),
            pltpu.SemaphoreType.DMA((2, 2)),
        ],
    )(meta, diag_inverse, right_side)
    sides = exchange([0], sides, 1)

    pairs = count // 2
    wide_shape = shaped((pairs, 2 * block, width + block))
    parts = REACH * (SPAN + cases // block)
    even_shape = shaped((parts, block, block))
    odd_shape = shaped((max(parts, count * cases // block + 1), block, block))

    wide_b, wide_a, base_b, *edge_w = call(
        prepare_kernel,
        "prepare",
        [SMEM, SMEM, SMEM, HBM, HBM, HBM, VMEM],
        [wide_shape, wide_shape, shaped(whole.shape, jnp.float32), even_shape, odd_shape],
        scratch_shapes=[
            pltpu.VMEM(lower_blocks.shape, jnp.bfloat16),
            pltpu.VMEM(diag_inverse.shape, jnp.bfloat16),
            pltpu.VMEM(whole.shape, jnp.bfloat16),
            pltpu.VMEM((2, SPAN, block, block), jnp.float32),
            pltpu.SemaphoreType.DMA((2, 3, pairs)),
        ],
    )(meta, depend, scale, lower_blocks, diag_inverse, right_side, first)

    padded = pltpu.VMEM((count + halo, block, cases), jnp.bfloat16)
    solved, *sends = call(
        functools.partial(exchanged_step, 0),
        "step_0",
        [SMEM] + [VMEM] * 5,
        [whole, edge, edge],
        scratch_shapes=[padded],
    )(meta, first, *sides, wide_b, base_b)
    arrived = travel(0, solved, sends)

    even_w, odd_w = edge_w
    even_w = lax.ppermute(after(even_w, sides), AXES, inner_pairs(range(2, chain), even_mate, chain, rows))
    odd_w = lax.ppermute(after(odd_w, even_w), AXES, inner_pairs(range(2, chain), odd_mate, chain, rows))
    arrived = after(arrived, even_w)
    edges = call(
        order_kernel,
        "order",
        [SMEM, VMEM, VMEM],
        [shaped((2, *even_shape.shape))],
    )(meta, even_w, odd_w)[0]

    out, made_a, *sides = call(
        functools.partial(level_step, 1),
        "step_1_a",
        [SMEM] + [VMEM] * 6,
        [shaped(right_side.shape), whole, edge, edge],
        [ANY] + [VMEM] * 3,
        scratch_shapes=[padded, pltpu.SemaphoreType.DMA((2,))],
    )(meta, *arrived, first, wide_a, solved)
    solved, *sends = call(
        functools.partial(exchanged_step, 1),
        "step_1_b",
        [SMEM] + [VMEM] * 5,
        [whole, wide_edge, wide_edge],
        scratch_shapes=[padded],
    )(meta, made_a, *exchange([1], sides, 0), wide_b, base_b)

    for group in range(2, chain):
        final = group == chain - 1
        outs = [whole, whole] + ([] if final else [wide_edge] * 2)
        out, *now = call(
            functools.partial(later_step, group, final),
            f"step_{group}",
            [SMEM] + [VMEM] * 10 + [ANY],
            [shaped(right_side.shape), *outs],
            [ANY] + [VMEM] * len(outs),
            scratch_shapes=[
                pltpu.VMEM((count + 2 * halo, block, cases), jnp.bfloat16),
                padded,
                pltpu.SemaphoreType.DMA((1 + pairs,)),
            ],
            input_output_aliases={11: 0},
        )(meta, *travel(group - 1, solved, sends), edges, first, wide_a, wide_b, base_b, made_a, solved, out)
        solved, made_a, *sends = now
    return out


def solution(mesh):
    placed = (
        P("chain", "rows", None, None),
        P("chain", "rows", None, None, None),
        P("chain", "rows", None),
        P("chain", "rows", None, None),
        P("chain", "rows", None),
    )
    return jax.shard_map(
        functools.partial(per_device, mesh.shape["chain"], mesh.shape["rows"]),
        mesh=mesh,
        in_specs=placed,
        out_specs=P("chain", "rows", None, None),
        check_vma=False,
    )
```

```python
import functools

import jax
import jax.numpy as jnp
from jax import lax
from jax.experimental import pallas as pl
from jax.experimental.pallas import tpu as pltpu
from jax.sharding import PartitionSpec as P

REACH = 2
SPAN = 2 * REACH + 1
AXES = ("chain", "rows")
VMEM = pl.BlockSpec(memory_space=pltpu.VMEM)
SMEM = pl.BlockSpec(memory_space=pltpu.SMEM)
ANY = pl.BlockSpec(memory_space=pl.ANY)
HBM = pl.BlockSpec(memory_space=pltpu.HBM)


def even_mate(row, rows):
    return row ^ 1


def odd_mate(row, rows):
    mate = row + 1 if row % 2 else row - 1
    return mate if 0 <= mate < rows else row


def same_row(row, rows):
    return row


def swap_groups(chain, taken=()):
    return {g: g ^ 1 for g in range(chain) if g not in taken}


def hop_pairs(group, mate, chain, rows):
    if group % 2 == 0:
        moves = swap_groups(chain)
    else:
        moves = swap_groups(chain, range(group - 1, group + 3))
        moves.update({group: group + 1, group - 1: group, group + 1: group + 2, group + 2: group - 1})
    return [
        (source * rows + r, target * rows + (mate(r, rows) if source == group else r))
        for source, target in moves.items()
        for r in range(rows)
    ]


def inner_pairs(groups, mate, chain, rows, idle=None):
    pairs = []
    paired = [r for r in range(rows) if mate(r, rows) != r]
    for r in range(rows):
        if r not in paired:
            moves = swap_groups(chain)
        else:
            moves = swap_groups(chain, [*groups, idle])
            pairs += [(g * rows + r, g * rows + mate(r, rows)) for g in groups]
            if idle is not None:
                alike = [q for q in paired if q % 2 == r % 2]
                pairs.append((idle * rows + r, idle * rows + alike[(alike.index(r) + 1) % len(alike)]))
        pairs += [(a * rows + r, b * rows + r) for a, b in moves.items()]
    return pairs


def dot(a, b):
    return jnp.dot(a, b, preferred_element_type=jnp.float32)


def by_parity(odd, low_value, high_value, even_ref, odd_ref):
    @pl.when(odd == 0)
    def _():
        even_ref[...] = high_value()
        odd_ref[...] = low_value()

    @pl.when(odd == 1)
    def _():
        even_ref[...] = low_value()
        odd_ref[...] = high_value()


def first_kernel(meta, inverse_hbm, right_hbm, solved, *rest):
    *sends, inverse, right, sems = rest
    count = inverse.shape[0]
    parts = 2
    size = count // parts
    loads = []
    for part in range(parts):
        rows = pl.ds(part * size, size)
        loads.append(
            (
                pltpu.make_async_copy(inverse_hbm.at[0, rows], inverse.at[rows], sems.at[0, part]),
                pltpu.make_async_copy(right_hbm.at[0, rows], right.at[rows], sems.at[1, part]),
            )
        )
    for pair in loads:
        for load in pair:
            load.start()
    for part in range(parts):
        for load in loads[part]:
            load.wait()
        for q in range(part * size, (part + 1) * size):
            solved[q] = dot(inverse[q], right[q]).astype(solved.dtype)
    by_parity(meta[1], lambda: solved[:REACH], lambda: solved[count - REACH :], *sends)


def premultiply(meta, depend, scale, lower, inverse, wide, acc, level, p, half):
    block = lower.shape[-1]
    terms = lower.shape[2]
    q = 2 * p + half
    acc[...] = jnp.zeros_like(acc)
    for k in range(terms):
        column = jnp.clip(depend[k, level, q] - (meta[2] + q) + REACH, 0, SPAN - 1)
        acc[column] += scale[k, level, q] * dot(inverse[level, q], lower[level, q, k])
    at = slice(half * block, (half + 1) * block)
    for d in range(SPAN):
        wide[p, at, (d + half) * block : (d + half + 1) * block] = (-acc[d]).astype(wide.dtype)
    other = 0 if half else SPAN
    wide[p, at, other * block : (other + 1) * block] = jnp.zeros((block, block), wide.dtype)


def prepare_kernel(meta, depend, scale, lower_hbm, inverse_hbm, right_hbm, first, wide_b, wide_a, base, even_out, odd_out, lower, inverse, right, acc, sems):
    pairs = wide_a.shape[0]
    block = lower.shape[-1]

    def loads(level, p):
        rows = pl.ds(2 * p, 2)
        copies = [
            pltpu.make_async_copy(lower_hbm.at[level, rows], lower.at[level, rows], sems.at[level, 0, p]),
            pltpu.make_async_copy(inverse_hbm.at[level, rows], inverse.at[level, rows], sems.at[level, 1, p]),
        ]
        if level:
            copies.append(pltpu.make_async_copy(right_hbm.at[1, rows], right.at[rows], sems.at[level, 2, p]))
        return copies

    def start(level):
        for p in range(pairs):
            for copy in loads(level, p):
                copy.start()

    start(1)

    @pl.when(meta[0] > 0)
    def _():
        start(0)

    @pl.loop(0, pairs)
    def _(p):
        for copy in loads(1, p):
            copy.wait()
        for half in range(2):
            premultiply(meta, depend, scale, lower, inverse, wide_b, acc.at[half], 1, p, half)
            base[2 * p + half] = dot(inverse[1, 2 * p + half], right[2 * p + half])

    @pl.when(meta[0] > 0)
    def _():
        @pl.loop(0, pairs)
        def _(p):
            for copy in loads(0, p):
                copy.wait()
            for half in range(2):
                premultiply(meta, depend, scale, lower, inverse, wide_a, acc.at[half], 0, p, half)

    def emit(ref, p):
        parts = first.shape[2] // block
        size = SPAN + parts
        for half in range(2):
            for d in range(SPAN):
                column = (d + half) * block
                ref[half * size + d] = wide_a[p, half * block : (half + 1) * block, column : column + block]
            for part in range(parts):
                ref[half * size + SPAN + part] = first[2 * p + half, :, part * block : (part + 1) * block]

    @pl.when((meta[0] > 1) & (meta[1] == 1))
    def _():
        emit(even_out, 0)
        emit(odd_out, pairs - 1)

    @pl.when((meta[0] > 1) & (meta[1] == 0))
    def _():
        emit(odd_out, 0)
        emit(even_out, pairs - 1)


def order_kernel(meta, even_in, odd_in, edges):
    @pl.when(meta[0] > 1)
    def _():
        odd = meta[1]
        edges[1 - odd] = even_in[...]
        edges[odd] = odd_in[...]


def flat(ref, start, count):
    block = ref[start : start + count]
    return block.reshape(count * block.shape[1], block.shape[2])


def place(window, odd, even_in, odd_in):
    halo = even_in.shape[0]
    low, high = 0, window.shape[0] - halo
    window[pl.ds(jnp.where(odd == 1, low, high), halo)] = even_in[...]
    window[pl.ds(jnp.where(odd == 1, high, low), halo)] = odd_in[...]


def level(wide, base, window, solved, put, done=None):
    for p in range(wide.shape[0]):
        rows = dot(wide[p], flat(window, 2 * p, SPAN + 1)) + flat(base, 2 * p, 2).astype(jnp.float32)
        solved[put + 2 * p : put + 2 * p + 2] = rows.astype(solved.dtype).reshape(2, *solved.shape[1:])
        if done is not None:
            done(p)


def emit_sends(odd, solved, sends):
    if sends:
        size = sends[0].shape[0]
        count = solved.shape[0]
        by_parity(odd, lambda: solved[:size], lambda: solved[count - size :], *sends)


def store(level_a, solved, out, sems):
    copies = [
        pltpu.make_async_copy(source, out.at[at], sems.at[at]) for at, source in ((0, level_a), (1, solved))
    ]
    for copy in copies:
        copy.start()
    for copy in copies:
        copy.wait()


def exchanged_step(group, final, meta, own, even_in, odd_in, wide_b, base_b, *rest):
    if final:
        _, out, solved, level_a, sems = rest
    else:
        solved, even_out, odd_out, level_a = rest

    @pl.when(meta[0] == group)
    def _():
        done, copies = None, []
        if final:
            copies = [pltpu.make_async_copy(own, out.at[0], sems.at[0])]
            copies += [
                pltpu.make_async_copy(solved.at[pl.ds(2 * p, 2)], out.at[1, pl.ds(2 * p, 2)], sems.at[1 + p])
                for p in range(wide_b.shape[0])
            ]
            copies[0].start()

            def done(p):
                copies[1 + p].start()

        level_a[REACH : REACH + own.shape[0]] = own[...]
        place(level_a, meta[1], even_in, odd_in)
        level(wide_b, base_b, level_a, solved, 0, done)
        if final:
            for copy in copies:
                copy.wait()
        else:
            emit_sends(meta[1], solved, (even_out, odd_out))


def level_step(group, meta, centre, even_in, odd_in, first, wide_a, old_a, old_b, *rest):
    out, solved, even_out, odd_out, window, sems = rest[-6:]

    @pl.when(meta[0] == group)
    def _():
        window[REACH : REACH + first.shape[0]] = centre[...]
        place(window, meta[1], even_in, odd_in)
        level(wide_a, first, window, solved, 0)
        emit_sends(meta[1], solved, (even_out, odd_out))

    @pl.when(meta[0] == group - 1)
    def _():
        store(old_a, old_b, out, sems)


def later_step(group, meta, centre, even_in, odd_in, edges, first, wide_a, wide_b, base_b, old_a, old_b, _, out, solved, solved_a, *rest):
    *sends, window, level_a, sems = rest
    count, block, cases = first.shape

    @pl.when(meta[0] == group)
    def _():
        odd = meta[1]
        halo = 2 * REACH
        window[halo : halo + count] = centre[...]
        place(window, odd, even_in, odd_in)
        level(wide_a, first, window.at[pl.ds(REACH, count + halo)], level_a, REACH)
        parts = cases // block
        size = SPAN + parts
        for side in range(2):
            for i in range(REACH):
                put = side * (count + REACH) + i
                base = jnp.concatenate([edges[side, i * size + SPAN + part] for part in range(parts)], axis=1)
                blocks = jnp.concatenate([edges[side, i * size + d] for d in range(SPAN)], axis=1)
                row = dot(blocks, flat(window, put, SPAN)) + base.astype(jnp.float32)
                level_a[put] = row.astype(level_a.dtype)
        level(wide_b, base_b, level_a, solved, 0)
        emit_sends(odd, solved, sends)
        solved_a[...] = level_a[REACH : REACH + count]

    @pl.when(meta[0] == group - 1)
    def _():
        store(old_a, old_b, out, sems)


def shaped(shape, dtype=jnp.bfloat16):
    return jax.ShapeDtypeStruct(shape, dtype)


def params(**more):
    return pltpu.CompilerParams(vmem_limit_bytes=24 * 1024 * 1024, **more)


def in_hbm(value):
    return pltpu.with_memory_space_constraint(value, pltpu.HBM)


def after(values, *earlier):
    return lax.optimization_barrier((values, earlier))[0]


def per_device(chain, rows, right_side, lower_blocks, block_scale, diag_inverse, depend_rows):
    _, count, block, cases = right_side.shape
    width = SPAN * block
    halo = 2 * REACH
    row = lax.axis_index("rows")
    meta = jnp.stack([lax.axis_index("chain"), row % 2, row * count]).astype(jnp.int32)
    depend = depend_rows.transpose(2, 0, 1)
    scale = block_scale.transpose(2, 0, 1)
    right_side, lower_blocks, diag_inverse = in_hbm(right_side), in_hbm(lower_blocks), in_hbm(diag_inverse)
    mates = (even_mate, odd_mate)

    def exchange(groups, values, idle):
        return [
            lax.ppermute(value, AXES, inner_pairs(groups, mate, chain, rows, idle))
            for value, mate in zip(values, mates)
        ]

    def travel(group, centre, sides):
        return [
            lax.ppermute(value, AXES, hop_pairs(group, mate, chain, rows))
            for value, mate in zip((centre, *sides), (same_row, *mates))
        ]

    def call(kernel, name, in_specs, out_shape, out_specs=None, **more):
        return pl.pallas_call(
            kernel,
            in_specs=in_specs,
            out_specs=out_specs or [VMEM] * len(out_shape),
            out_shape=out_shape,
            compiler_params=params(),
            name=name,
            **more,
        )

    whole, edge, wide_edge = (shaped((size, block, cases)) for size in (count, REACH, halo))

    first, *sides = call(
        first_kernel,
        "first_level",
        [SMEM, HBM, HBM],
        [whole, edge, edge],
        scratch_shapes=[
            pltpu.VMEM((count, block, block), jnp.bfloat16),
            pltpu.VMEM(whole.shape, jnp.bfloat16),
            pltpu.SemaphoreType.DMA((2, 2)),
        ],
    )(meta, diag_inverse, right_side)
    sides = exchange([0], sides, 1)

    pairs = count // 2
    wide_shape = shaped((pairs, 2 * block, width + block))
    weight_edge = shaped((REACH * (SPAN + cases // block), block, block))

    wide_b, wide_a, base_b, *edge_w = call(
        prepare_kernel,
        "prepare",
        [SMEM, SMEM, SMEM, HBM, HBM, HBM, VMEM],
        [wide_shape, wide_shape, shaped(whole.shape, jnp.float32), weight_edge, weight_edge],
        scratch_shapes=[
            pltpu.VMEM(lower_blocks.shape, jnp.bfloat16),
            pltpu.VMEM(diag_inverse.shape, jnp.bfloat16),
            pltpu.VMEM(whole.shape, jnp.bfloat16),
            pltpu.VMEM((2, SPAN, block, block), jnp.float32),
            pltpu.SemaphoreType.DMA((2, 3, pairs)),
        ],
    )(meta, depend, scale, lower_blocks, diag_inverse, right_side, first)

    padded = pltpu.VMEM((count + halo, block, cases), jnp.bfloat16)
    def own_exchange(group, values, sides, final=False):
        sems = pltpu.SemaphoreType.DMA((1 + pairs,))
        sizes = [] if final else [edge if group in (0, chain - 2) else wide_edge] * 2
        return call(
            functools.partial(exchanged_step, group, final),
            f"step_{group}_b",
            [SMEM] + [VMEM] * 5 + [ANY] * final,
            [shaped(right_side.shape)] * final + [whole, *sizes],
            [ANY] * final + [VMEM] * (1 + len(sizes)),
            scratch_shapes=[padded] + [sems] * final,
            input_output_aliases={6: 0} if final else {},
        )(meta, values, *sides, wide_b, base_b, *([out] * final))

    def own_level(group, arrived, made_a, solved, out):
        aliased = out is not None
        return call(
            functools.partial(level_step, group),
            f"step_{group}_a",
            [SMEM] + [VMEM] * 7 + [ANY] * aliased,
            [shaped(right_side.shape), whole, edge, edge],
            [ANY] + [VMEM] * 3,
            scratch_shapes=[padded, pltpu.SemaphoreType.DMA((2,))],
            input_output_aliases={8: 0} if aliased else {},
        )(meta, *arrived, first, wide_a, made_a, solved, *([out] * aliased))

    out = None
    solved, *sends = own_exchange(0, first, sides)
    arrived = travel(0, solved, sends)

    between = range(2, chain - 1)
    moved = [
        lax.ppermute(after(value, sides), AXES, inner_pairs(between, mate, chain, rows, chain - 1))
        for value, mate in zip(edge_w, mates)
    ]
    edges = call(order_kernel, "order", [SMEM, VMEM, VMEM], [shaped((2, *weight_edge.shape))])(meta, *moved)[0]

    out, made_a, *sides = own_level(1, after(arrived, moved), first, solved, out)
    solved, *sends = own_exchange(1, made_a, exchange([1], sides, 0))
    for group in between:
        size = edge if group == chain - 2 else wide_edge
        out, *now = call(
            functools.partial(later_step, group),
            f"step_{group}",
            [SMEM] + [VMEM] * 10 + [ANY],
            [shaped(right_side.shape), whole, whole, size, size],
            [ANY] + [VMEM] * 4,
            scratch_shapes=[
                pltpu.VMEM((count + 2 * halo, block, cases), jnp.bfloat16),
                padded,
                pltpu.SemaphoreType.DMA((2,)),
            ],
            input_output_aliases={11: 0},
        )(meta, *travel(group - 1, solved, sends), edges, first, wide_a, wide_b, base_b, made_a, solved, out)
        solved, made_a, *sends = now
    last = chain - 1
    out, made_a, *sides = own_level(last, travel(last - 1, solved, sends), made_a, solved, out)
    return own_exchange(last, made_a, exchange([last], sides, last - 1), True)[0]


def solution(mesh):
    placed = (
        P("chain", "rows", None, None),
        P("chain", "rows", None, None, None),
        P("chain", "rows", None),
        P("chain", "rows", None, None),
        P("chain", "rows", None),
    )
    return jax.shard_map(
        functools.partial(per_device, mesh.shape["chain"], mesh.shape["rows"]),
        mesh=mesh,
        in_specs=placed,
        out_specs=P("chain", "rows", None, None),
        check_vma=False,
    )
```

```python
import functools

import jax
import jax.numpy as jnp
from jax import lax
from jax.experimental import pallas as pl
from jax.experimental.pallas import tpu as pltpu
from jax.sharding import PartitionSpec as P

REACH = 2
SPAN = 2 * REACH + 1
CHUNKS = 2
EDGE = SPAN + CHUNKS
AXES = ("chain", "rows")
VMEM = pl.BlockSpec(memory_space=pltpu.VMEM)
SMEM = pl.BlockSpec(memory_space=pltpu.SMEM)
ANY = pl.BlockSpec(memory_space=pl.ANY)
HBM = pl.BlockSpec(memory_space=pltpu.HBM)


def even_mate(row, rows):
    return row ^ 1


def odd_mate(row, rows):
    mate = row + 1 if row % 2 else row - 1
    return mate if 0 <= mate < rows else row


def same_row(row, rows):
    return row


def swap_groups(chain, taken=()):
    return {g: g ^ 1 for g in range(chain) if g not in taken}


def hop_pairs(group, mate, chain, rows):
    if group % 2 == 0:
        moves = swap_groups(chain)
    else:
        moves = swap_groups(chain, range(group - 1, group + 3))
        moves.update({group: group + 1, group - 1: group, group + 1: group + 2, group + 2: group - 1})
    return [
        (source * rows + r, target * rows + (mate(r, rows) if source == group else r))
        for source, target in moves.items()
        for r in range(rows)
    ]


def inner_pairs(groups, mate, chain, rows, idle=None):
    pairs = []
    paired = [r for r in range(rows) if mate(r, rows) != r]
    for r in range(rows):
        if r not in paired:
            moves = swap_groups(chain)
        else:
            moves = swap_groups(chain, [*groups, idle])
            pairs += [(g * rows + r, g * rows + mate(r, rows)) for g in groups]
            if idle is not None:
                alike = [q for q in paired if q % 2 == r % 2]
                pairs.append((idle * rows + r, idle * rows + alike[(alike.index(r) + 1) % len(alike)]))
        pairs += [(a * rows + r, b * rows + r) for a, b in moves.items()]
    return pairs


def dot(a, b):
    return jnp.dot(a, b, preferred_element_type=jnp.float32)


def by_parity(odd, low_value, high_value, even_ref, odd_ref):
    @pl.when(odd == 0)
    def _():
        even_ref[...] = high_value()
        odd_ref[...] = low_value()

    @pl.when(odd == 1)
    def _():
        even_ref[...] = low_value()
        odd_ref[...] = high_value()


def premultiplied(meta, depend, scale, lower, inverse, acc, level, q):
    acc[...] = jnp.zeros_like(acc)
    for k in range(len(lower)):
        column = jnp.clip(depend[k, level, q] - (meta[2] + q) + REACH, 0, SPAN - 1)
        acc[column] += scale[k, level, q] * dot(inverse, lower[k])


def first_kernel(meta, depend, scale, lower_hbm, inverse_hbm, right_hbm, solved, even_a, odd_a, even_b, odd_b, inverse, right, lower, acc, edges, sems):
    count = inverse.shape[0]
    block = inverse.shape[1]
    parts = right.shape[2] // block
    steps = 4
    size = count // steps
    loads = []
    for step in range(steps):
        rows = pl.ds(step * size, size)
        loads.append(
            (
                pltpu.make_async_copy(inverse_hbm.at[0, rows], inverse.at[rows], sems.at[0, step]),
                pltpu.make_async_copy(right_hbm.at[0, rows], right.at[rows], sems.at[1, step]),
            )
        )
    ends = (0, count - REACH)

    def edge_load(side):
        rows = pl.ds(ends[side], REACH)
        return pltpu.make_async_copy(lower_hbm.at[0, rows], lower.at[side], sems.at[2, side])

    for pair in loads:
        for load in pair:
            load.start()

    @pl.when(meta[0] > 1)
    def _():
        for side in range(2):
            edge_load(side).start()

    for step in range(steps):
        for load in loads[step]:
            load.wait()
        for q in range(step * size, (step + 1) * size):
            solved[q] = dot(inverse[q], right[q]).astype(solved.dtype)

    def row_parts(q):
        return [solved[q, :, part * block : (part + 1) * block] for part in range(parts)]

    @pl.when(meta[0] < 2)
    def _():
        for side in range(2):
            for i in range(REACH):
                for part, value in enumerate(row_parts(ends[side] + i)):
                    edges[side, i * parts + part] = value

    @pl.when(meta[0] > 1)
    def _():
        for side in range(2):
            edge_load(side).wait()
            for i in range(REACH):
                q = ends[side] + i
                blocks = [lower[side, i, k] for k in range(lower.shape[2])]
                premultiplied(meta, depend, scale, blocks, inverse[q], acc.at[i], 0, q)
                for d in range(SPAN):
                    edges[side, i * EDGE + d] = (-acc[i, d]).astype(edges.dtype)
                for part, value in enumerate(row_parts(q)):
                    edges[side, i * EDGE + SPAN + part] = value

    soon = even_a.shape[0]
    by_parity(meta[1], lambda: edges[0, :soon], lambda: edges[1, :soon], even_a, odd_a)

    @pl.when(meta[0] > 1)
    def _():
        by_parity(meta[1], lambda: edges[0, soon:], lambda: edges[1, soon:], even_b, odd_b)


def prepare_kernel(meta, depend, scale, lower_hbm, inverse_hbm, right_hbm, wide_b, wide_a, base, lower, inverse, right, acc, sems):
    pairs = wide_a.shape[0]
    block = lower.shape[-1]

    def loads(level, p):
        rows = pl.ds(2 * p, 2)
        copies = [
            pltpu.make_async_copy(lower_hbm.at[level, rows], lower.at[level, rows], sems.at[level, 0, p]),
            pltpu.make_async_copy(inverse_hbm.at[level, rows], inverse.at[level, rows], sems.at[level, 1, p]),
        ]
        if level:
            copies.append(pltpu.make_async_copy(right_hbm.at[1, rows], right.at[rows], sems.at[level, 2, p]))
        return copies

    def start(level):
        for p in range(pairs):
            for copy in loads(level, p):
                copy.start()

    def pair(level, p, wide):
        for copy in loads(level, p):
            copy.wait()
        for half in range(2):
            q = 2 * p + half
            blocks = [lower[level, q, k] for k in range(lower.shape[2])]
            premultiplied(meta, depend, scale, blocks, inverse[level, q], acc.at[half], level, q)
            at = slice(half * block, (half + 1) * block)
            for d in range(SPAN):
                wide[p, at, (d + half) * block : (d + half + 1) * block] = (-acc[half, d]).astype(wide.dtype)
            other = 0 if half else SPAN
            wide[p, at, other * block : (other + 1) * block] = jnp.zeros((block, block), wide.dtype)

    start(1)

    @pl.when(meta[0] > 0)
    def _():
        start(0)

    @pl.loop(0, pairs)
    def _(p):
        pair(1, p, wide_b)
        for half in range(2):
            base[2 * p + half] = dot(inverse[1, 2 * p + half], right[2 * p + half])

    @pl.when(meta[0] > 0)
    def _():
        @pl.loop(0, pairs)
        def _(p):
            pair(0, p, wide_a)


def order_kernel(meta, even_a, odd_a, even_b, odd_b, edges):
    @pl.when(meta[0] > 1)
    def _():
        odd = meta[1]
        soon = even_a.shape[0]
        edges[1 - odd, :soon] = even_a[...]
        edges[1 - odd, soon:] = even_b[...]
        edges[odd, :soon] = odd_a[...]
        edges[odd, soon:] = odd_b[...]


def flat(ref, start, count, at=slice(None)):
    block = ref[start : start + count, :, at]
    return block.reshape(count * block.shape[1], block.shape[2])


def place(window, odd, even_in, odd_in, at=slice(None)):
    halo = even_in.shape[0]
    low, high = 0, window.shape[0] - halo
    window[pl.ds(jnp.where(odd == 1, low, high), halo)] = even_in[:, :, at]
    window[pl.ds(jnp.where(odd == 1, high, low), halo)] = odd_in[:, :, at]


def columns(chunk, cases):
    return slice(None) if chunk is None else slice(chunk * cases, (chunk + 1) * cases)


def first_of_group(wide_a, first, window, level_a, put, at):
    for p in range(wide_a.shape[0]):
        rows = dot(wide_a[p], flat(window, 2 * p, SPAN + 1)) + flat(first, 2 * p, 2, at).astype(jnp.float32)
        level_a[put + 2 * p : put + 2 * p + 2] = rows.astype(level_a.dtype).reshape(2, *level_a.shape[1:])


def second_of_group(wide_b, base_b, level_a, solved, at, done=None):
    for p in range(wide_b.shape[0]):
        rows = dot(wide_b[p], flat(level_a, 2 * p, SPAN + 1)) + flat(base_b, 2 * p, 2, at)
        solved[2 * p : 2 * p + 2] = rows.astype(solved.dtype).reshape(2, *solved.shape[1:])
        if done is not None:
            done(p)


def emit_sends(odd, solved, sends):
    if sends:
        size = sends[0].shape[0]
        count = solved.shape[0]
        by_parity(odd, lambda: solved[:size], lambda: solved[count - size :], *sends)


def store(level_a, solved, out, at, sems):
    copies = [
        pltpu.make_async_copy(source, out.at[level, :, :, at], sems.at[level])
        for level, source in ((0, level_a), (1, solved))
    ]
    for copy in copies:
        copy.start()
    for copy in copies:
        copy.wait()


def exchanged_step(group, chunk, meta, own, even_in, odd_in, wide_b, base_b, solved, even_out, odd_out, level_a):
    @pl.when(meta[0] == group)
    def _():
        at = columns(chunk, solved.shape[-1])
        count, block = own.shape[0], own.shape[1]
        level_a[REACH : REACH + count] = own[:, :, at]
        if even_in.shape[0] == REACH:
            place(level_a, meta[1], even_in, odd_in, at)
        else:
            parts = even_in.shape[0] // REACH
            low, high = 0, count + REACH
            for i in range(REACH):
                for part in range(parts):
                    cols = slice(part * block, (part + 1) * block)
                    level_a[i + jnp.where(meta[1] == 1, low, high), :, cols] = even_in[i * parts + part]
                    level_a[i + jnp.where(meta[1] == 1, high, low), :, cols] = odd_in[i * parts + part]
        second_of_group(wide_b, base_b, level_a, solved, at)
        emit_sends(meta[1], solved, (even_out, odd_out))


def level_step(group, meta, centre, even_in, odd_in, first, wide_a, old_b, out, solved, even_out, odd_out, window, sems):
    count = first.shape[0]

    @pl.when(meta[0] == group)
    def _():
        window[REACH : REACH + count] = centre[...]
        place(window, meta[1], even_in, odd_in)
        first_of_group(wide_a, first, window, solved, 0, slice(None))
        emit_sends(meta[1], solved, (even_out, odd_out))

    @pl.when(meta[0] == group - 1)
    def _():
        store(first, old_b, out, slice(None), sems)


def later_step(group, chunk, final, meta, centre, even_in, odd_in, edges, first, wide_a, wide_b, base_b, old_a, old_b, *rest):
    stages = final and chunk == CHUNKS - 1
    if stages:
        made_a, made_b, _, out, solved, solved_a, window, level_a, stage, sems = rest
    else:
        _, out, solved, solved_a, *sends, window, level_a, sems = rest
    cases = solved.shape[-1]
    at = columns(chunk, cases)
    on_out = pl.ds(chunk * cases, cases)
    count = first.shape[0]

    @pl.when(meta[0] == group)
    def _():
        odd = meta[1]
        halo = 2 * REACH
        window[halo : halo + count] = centre[...]
        place(window, odd, even_in, odd_in)
        first_of_group(wide_a, first, window.at[pl.ds(REACH, count + halo)], level_a, REACH, at)
        done, copies = None, []
        if stages:
            copies = [
                pltpu.make_async_copy(stage.at[level, pl.ds(2 * p, 2)], out.at[level, pl.ds(2 * p, 2)], sems.at[level, p])
                for level in range(2)
                for p in range(count // 2)
            ]
            before = slice(0, chunk * cases)
            stage[0, :, :, before] = made_a[...]
            stage[1, :, :, before] = made_b[...]
            stage[0, :, :, at] = level_a[REACH : REACH + count]
            for copy in copies[: count // 2]:
                copy.start()

            def done(p):
                stage[1, 2 * p : 2 * p + 2, :, at] = solved[2 * p : 2 * p + 2]
                copies[count // 2 + p].start()

        for side in range(2):
            for i in range(REACH):
                put = side * (count + REACH) + i
                base = edges[side, i * EDGE + SPAN + chunk]
                blocks = jnp.concatenate([edges[side, i * EDGE + d] for d in range(SPAN)], axis=1)
                row = dot(blocks, flat(window, put, SPAN)) + base.astype(jnp.float32)
                level_a[put] = row.astype(level_a.dtype)
        second_of_group(wide_b, base_b, level_a, solved, at, done)
        if stages:
            for copy in copies:
                copy.wait()
        else:
            emit_sends(odd, solved, sends)
            solved_a[...] = level_a[REACH : REACH + count]

    @pl.when(meta[0] == group - 1)
    def _():
        store(old_a.at[:, :, at] if old_a.shape[-1] > cases else old_a, old_b, out, on_out, *([sems.at[0]] if stages else [sems]))


def shaped(shape, dtype=jnp.bfloat16):
    return jax.ShapeDtypeStruct(shape, dtype)


def params(**more):
    return pltpu.CompilerParams(vmem_limit_bytes=24 * 1024 * 1024, **more)


def in_hbm(value):
    return pltpu.with_memory_space_constraint(value, pltpu.HBM)


def after(values, *earlier):
    return lax.optimization_barrier((values, earlier))[0]


def per_device(chain, rows, right_side, lower_blocks, block_scale, diag_inverse, depend_rows):
    _, count, block, cases = right_side.shape
    terms = lower_blocks.shape[2]
    width = SPAN * block
    part = cases // CHUNKS
    halo = 2 * REACH
    row = lax.axis_index("rows")
    meta = jnp.stack([lax.axis_index("chain"), row % 2, row * count]).astype(jnp.int32)
    depend = depend_rows.transpose(2, 0, 1)
    scale = block_scale.transpose(2, 0, 1)
    right_side, lower_blocks, diag_inverse = in_hbm(right_side), in_hbm(lower_blocks), in_hbm(diag_inverse)
    mates = (even_mate, odd_mate)

    def exchange(groups, values, idle=None):
        return [
            lax.ppermute(value, AXES, inner_pairs(groups, mate, chain, rows, idle))
            for value, mate in zip(values, mates)
        ]

    def travel(group, centre, sides):
        return [lax.ppermute(centre, AXES, hop_pairs(group, same_row, chain, rows))] + [
            lax.ppermute(value, AXES, hop_pairs(group, mate, chain, rows)) for value, mate in zip(sides, mates)
        ]

    def call(kernel, name, in_specs, out_shape, out_specs=None, **more):
        return pl.pallas_call(
            kernel,
            in_specs=in_specs,
            out_specs=out_specs or [VMEM] * len(out_shape),
            out_shape=out_shape,
            compiler_params=params(),
            name=name,
            **more,
        )

    whole, half = shaped((count, block, cases)), shaped((count, block, part))
    whole_edge, half_edge = shaped((REACH, block, cases)), shaped((halo, block, part))

    total = REACH * EDGE
    soon = REACH * cases // block
    edge_shapes = [shaped((size, block, block)) for size in (soon, total - soon)]
    first, *edge_w = call(
        first_kernel,
        "first_level",
        [SMEM, SMEM, SMEM, HBM, HBM, HBM],
        [whole, *(shape for shape in edge_shapes for _ in range(2))],
        scratch_shapes=[
            pltpu.VMEM((count, block, block), jnp.bfloat16),
            pltpu.VMEM(whole.shape, jnp.bfloat16),
            pltpu.VMEM((2, REACH, terms, block, block), jnp.bfloat16),
            pltpu.VMEM((REACH, SPAN, block, block), jnp.float32),
            pltpu.VMEM((2, total, block, block), jnp.bfloat16),
            pltpu.SemaphoreType.DMA((3, 4)),
        ],
    )(meta, depend, scale, lower_blocks, diag_inverse, right_side)
    sides = exchange([0, *range(2, chain)], edge_w[:2], 1)

    pairs = count // 2
    wide_shape = shaped((pairs, 2 * block, width + block))
    wide_b, wide_a, base_b = call(
        prepare_kernel,
        "prepare",
        [SMEM, SMEM, SMEM, HBM, HBM, HBM],
        [wide_shape, wide_shape, shaped(whole.shape, jnp.float32)],
        scratch_shapes=[
            pltpu.VMEM(lower_blocks.shape, jnp.bfloat16),
            pltpu.VMEM(diag_inverse.shape, jnp.bfloat16),
            pltpu.VMEM(whole.shape, jnp.bfloat16),
            pltpu.VMEM((2, SPAN, block, block), jnp.float32),
            pltpu.SemaphoreType.DMA((2, 3, pairs)),
        ],
    )(meta, depend, scale, lower_blocks, diag_inverse, right_side)

    padded = pltpu.VMEM((count + halo, block, cases), jnp.bfloat16)
    padded_half = pltpu.VMEM((count + halo, block, part), jnp.bfloat16)
    solved, *sends = call(
        functools.partial(exchanged_step, 0, None),
        "step_0",
        [SMEM] + [VMEM] * 5,
        [whole, whole_edge, whole_edge],
        scratch_shapes=[padded],
    )(meta, first, *sides, wide_b, base_b)
    arrived = travel(0, solved, sends)

    later_w = exchange(range(2, chain), after(edge_w[2:], sides))
    edges, = call(
        order_kernel, "order", [SMEM] + [VMEM] * 4, [shaped((2, total, block, block))]
    )(meta, *sides, *later_w)

    out, own, *sides = call(
        functools.partial(level_step, 1),
        "step_1",
        [SMEM] + [VMEM] * 6,
        [shaped(right_side.shape), whole, whole_edge, whole_edge],
        [ANY] + [VMEM] * 3,
        scratch_shapes=[padded, pltpu.SemaphoreType.DMA((2,))],
    )(meta, *arrived, first, wide_a, solved)
    sides = exchange([1], sides, 0)
    made_a = [own] * CHUNKS
    sent = []
    for chunk in range(CHUNKS):
        sent.append(
            call(
                functools.partial(exchanged_step, 1, chunk),
                f"step_1_{chunk}",
                [SMEM] + [VMEM] * 5,
                [half, half_edge, half_edge],
                scratch_shapes=[padded_half],
            )(meta, own, *sides, wide_b, base_b)
        )

    for group in range(2, chain):
        final = group == chain - 1
        arrived = [travel(group - 1, solved, sends) for solved, *sends in sent]
        made = []
        for chunk in range(CHUNKS):
            outs = [half, half] + ([] if final else [half_edge] * 2)
            stages = final and chunk == CHUNKS - 1
            extra = [made[0][1], made[0][0][0]] if stages else []
            sems = (2, pairs) if stages else (2,)
            out, solved, level, *sends = call(
                functools.partial(later_step, group, chunk, final),
                f"step_{group}_{chunk}",
                [SMEM] + [VMEM] * (10 + len(extra)) + [ANY],
                [shaped(right_side.shape), *outs],
                [ANY] + [VMEM] * len(outs),
                scratch_shapes=[
                    pltpu.VMEM((count + 2 * halo, block, part), jnp.bfloat16),
                    padded_half,
                    *([pltpu.VMEM((2, count, block, cases), jnp.bfloat16)] if stages else []),
                    pltpu.SemaphoreType.DMA(sems),
                ],
                input_output_aliases={11 + len(extra): 0},
            )(
                meta,
                *arrived[chunk],
                edges,
                first,
                wide_a,
                wide_b,
                base_b,
                made_a[chunk],
                sent[chunk][0],
                *extra,
                out,
            )
            made.append(((solved, *sends), level))
        sent, made_a = [values[0] for values in made], [values[1] for values in made]
    return out


def solution(mesh):
    placed = (
        P("chain", "rows", None, None),
        P("chain", "rows", None, None, None),
        P("chain", "rows", None),
        P("chain", "rows", None, None),
        P("chain", "rows", None),
    )
    return jax.shard_map(
        functools.partial(per_device, mesh.shape["chain"], mesh.shape["rows"]),
        mesh=mesh,
        in_specs=placed,
        out_specs=P("chain", "rows", None, None),
        check_vma=False,
    )
```

```python
import functools

import jax
import jax.numpy as jnp
from jax import lax
from jax.experimental import pallas as pl
from jax.experimental.pallas import tpu as pltpu
from jax.sharding import PartitionSpec as P

REACH = 2
SPAN = 2 * REACH + 1
CHUNKS = 2
EDGE = SPAN + CHUNKS
AXES = ("chain", "rows")
VMEM = pl.BlockSpec(memory_space=pltpu.VMEM)
SMEM = pl.BlockSpec(memory_space=pltpu.SMEM)
ANY = pl.BlockSpec(memory_space=pl.ANY)
HBM = pl.BlockSpec(memory_space=pltpu.HBM)


def even_mate(row, rows):
    return row ^ 1


def odd_mate(row, rows):
    mate = row + 1 if row % 2 else row - 1
    return mate if 0 <= mate < rows else row


def same_row(row, rows):
    return row


def swap_groups(chain, taken=()):
    return {g: g ^ 1 for g in range(chain) if g not in taken}


def hop_pairs(group, mate, chain, rows):
    if group % 2 == 0:
        moves = swap_groups(chain)
    else:
        moves = swap_groups(chain, range(group - 1, group + 3))
        moves.update({group: group + 1, group - 1: group, group + 1: group + 2, group + 2: group - 1})
    return [
        (source * rows + r, target * rows + (mate(r, rows) if source == group else r))
        for source, target in moves.items()
        for r in range(rows)
    ]


def inner_pairs(groups, mate, chain, rows, idle=None):
    pairs = []
    paired = [r for r in range(rows) if mate(r, rows) != r]
    for r in range(rows):
        if r not in paired:
            moves = swap_groups(chain)
        else:
            moves = swap_groups(chain, [*groups, idle])
            pairs += [(g * rows + r, g * rows + mate(r, rows)) for g in groups]
            if idle is not None:
                alike = [q for q in paired if q % 2 == r % 2]
                pairs.append((idle * rows + r, idle * rows + alike[(alike.index(r) + 1) % len(alike)]))
        pairs += [(a * rows + r, b * rows + r) for a, b in moves.items()]
    return pairs


def dot(a, b):
    return jnp.dot(a, b, preferred_element_type=jnp.float32)


def by_parity(odd, low_value, high_value, even_ref, odd_ref):
    @pl.when(odd == 0)
    def _():
        even_ref[...] = high_value()
        odd_ref[...] = low_value()

    @pl.when(odd == 1)
    def _():
        even_ref[...] = low_value()
        odd_ref[...] = high_value()


def premultiplied(meta, depend, scale, lower, inverse, acc, level, q):
    acc[...] = jnp.zeros_like(acc)
    for k in range(len(lower)):
        column = jnp.clip(depend[k, level, q] - (meta[2] + q) + REACH, 0, SPAN - 1)
        acc[column] += scale[k, level, q] * dot(inverse, lower[k])


def first_kernel(meta, depend_hbm, scale_hbm, lower_hbm, inverse_hbm, right_hbm, solved, even_a, odd_a, even_b, odd_b, inverse, right, lower, depend, scale, acc, edges, sems):
    count = inverse.shape[0]
    block = inverse.shape[1]
    parts = right.shape[2] // block
    steps = 4
    size = count // steps
    loads = []
    for step in range(steps):
        rows = pl.ds(step * size, size)
        loads.append(
            (
                pltpu.make_async_copy(inverse_hbm.at[0, rows], inverse.at[rows], sems.at[0, step]),
                pltpu.make_async_copy(right_hbm.at[0, rows], right.at[rows], sems.at[1, step]),
            )
        )
    ends = (0, count - REACH)

    def edge_load(side):
        rows = pl.ds(ends[side], REACH)
        return pltpu.make_async_copy(lower_hbm.at[0, rows], lower.at[side], sems.at[2, side])

    tables = [
        pltpu.make_async_copy(source, target, sems.at[2, 2 + i])
        for i, (source, target) in enumerate(((depend_hbm, depend), (scale_hbm, scale)))
    ]

    for pair in loads:
        for load in pair:
            load.start()

    @pl.when(meta[0] > 1)
    def _():
        for load in (edge_load(0), edge_load(1), *tables):
            load.start()

    for step in range(steps):
        for load in loads[step]:
            load.wait()
        for q in range(step * size, (step + 1) * size):
            solved[q] = dot(inverse[q], right[q]).astype(solved.dtype)

    def row_parts(q):
        return [solved[q, :, part * block : (part + 1) * block] for part in range(parts)]

    @pl.when(meta[0] < 2)
    def _():
        for side in range(2):
            for i in range(REACH):
                for part, value in enumerate(row_parts(ends[side] + i)):
                    edges[side, i * parts + part] = value

    @pl.when(meta[0] > 1)
    def _():
        for table in tables:
            table.wait()
        for side in range(2):
            edge_load(side).wait()
            for i in range(REACH):
                q = ends[side] + i
                blocks = [lower[side, i, k] for k in range(lower.shape[2])]
                premultiplied(meta, depend, scale, blocks, inverse[q], acc.at[i], 0, q)
                for d in range(SPAN):
                    edges[side, i * EDGE + d] = (-acc[i, d]).astype(edges.dtype)
                for part, value in enumerate(row_parts(q)):
                    edges[side, i * EDGE + SPAN + part] = value

    soon = even_a.shape[0]
    by_parity(meta[1], lambda: edges[0, :soon], lambda: edges[1, :soon], even_a, odd_a)

    @pl.when(meta[0] > 1)
    def _():
        by_parity(meta[1], lambda: edges[0, soon:], lambda: edges[1, soon:], even_b, odd_b)


def prepare_kernel(turn, meta, depend_hbm, scale_hbm, lower_hbm, inverse_hbm, right_hbm, wide, base, lower, inverse, right, depend, scale, acc, sems):
    pairs = wide.shape[0]
    block = lower.shape[-1]
    level = jnp.where(meta[0] == 0, 1, turn)

    def loads(p):
        rows = pl.ds(2 * p, 2)
        return [
            pltpu.make_async_copy(source.at[level, rows], target.at[rows], sems.at[i, p])
            for i, (source, target) in enumerate(((lower_hbm, lower), (inverse_hbm, inverse), (right_hbm, right)))
        ]

    @pl.when((meta[0] > 0) | (turn == 0))
    def _():
        tables = [
            pltpu.make_async_copy(source, target, sems.at[3, i])
            for i, (source, target) in enumerate(((depend_hbm, depend), (scale_hbm, scale)))
        ]
        for table in tables:
            table.start()
        for p in range(pairs):
            for load in loads(p):
                load.start()
        for table in tables:
            table.wait()

        @pl.loop(0, pairs)
        def _(p):
            for load in loads(p):
                load.wait()
            for half in range(2):
                q = 2 * p + half
                blocks = [lower[q, k] for k in range(lower.shape[1])]
                premultiplied(meta, depend, scale, blocks, inverse[q], acc.at[half], level, q)
                at = slice(half * block, (half + 1) * block)
                for d in range(SPAN):
                    wide[p, at, (d + half) * block : (d + half + 1) * block] = (-acc[half, d]).astype(wide.dtype)
                other = 0 if half else SPAN
                wide[p, at, other * block : (other + 1) * block] = jnp.zeros((block, block), wide.dtype)
                base[q] = dot(inverse[q], right[q])


def order_kernel(meta, even_a, odd_a, even_b, odd_b, edges):
    @pl.when(meta[0] > 1)
    def _():
        odd = meta[1]
        soon = even_a.shape[0]
        edges[1 - odd, :soon] = even_a[...]
        edges[1 - odd, soon:] = even_b[...]
        edges[odd, :soon] = odd_a[...]
        edges[odd, soon:] = odd_b[...]


def flat(ref, start, count, at=slice(None)):
    block = ref[start : start + count, :, at]
    return block.reshape(count * block.shape[1], block.shape[2])


def place(window, odd, even_in, odd_in, at=slice(None)):
    halo = even_in.shape[0]
    low, high = 0, window.shape[0] - halo
    window[pl.ds(jnp.where(odd == 1, low, high), halo)] = even_in[:, :, at]
    window[pl.ds(jnp.where(odd == 1, high, low), halo)] = odd_in[:, :, at]


def columns(chunk, cases):
    return slice(None) if chunk is None else slice(chunk * cases, (chunk + 1) * cases)


def first_of_group(wide_a, first, window, level_a, put, at):
    for p in range(wide_a.shape[0]):
        rows = dot(wide_a[p], flat(window, 2 * p, SPAN + 1)) + flat(first, 2 * p, 2, at).astype(jnp.float32)
        level_a[put + 2 * p : put + 2 * p + 2] = rows.astype(level_a.dtype).reshape(2, *level_a.shape[1:])


def second_of_group(wide_b, base_b, level_a, solved, at, done=None):
    for p in range(wide_b.shape[0]):
        rows = dot(wide_b[p], flat(level_a, 2 * p, SPAN + 1)) + flat(base_b, 2 * p, 2, at)
        solved[2 * p : 2 * p + 2] = rows.astype(solved.dtype).reshape(2, *solved.shape[1:])
        if done is not None:
            done(p)


def emit_sends(odd, solved, sends):
    if sends:
        size = sends[0].shape[0]
        count = solved.shape[0]
        by_parity(odd, lambda: solved[:size], lambda: solved[count - size :], *sends)


def store(level_a, solved, out, at, sems):
    copies = [
        pltpu.make_async_copy(source, out.at[level, :, :, at], sems.at[level])
        for level, source in ((0, level_a), (1, solved))
    ]
    for copy in copies:
        copy.start()
    for copy in copies:
        copy.wait()


def exchanged_step(group, chunk, meta, own, even_in, odd_in, wide_b, base_b, solved, even_out, odd_out, level_a):
    @pl.when(meta[0] == group)
    def _():
        at = columns(chunk, solved.shape[-1])
        count, block = own.shape[0], own.shape[1]
        level_a[REACH : REACH + count] = own[:, :, at]
        if even_in.shape[0] == REACH:
            place(level_a, meta[1], even_in, odd_in, at)
        else:
            parts = even_in.shape[0] // REACH
            low, high = 0, count + REACH
            for i in range(REACH):
                for part in range(parts):
                    cols = slice(part * block, (part + 1) * block)
                    level_a[i + jnp.where(meta[1] == 1, low, high), :, cols] = even_in[i * parts + part]
                    level_a[i + jnp.where(meta[1] == 1, high, low), :, cols] = odd_in[i * parts + part]
        second_of_group(wide_b, base_b, level_a, solved, at)
        emit_sends(meta[1], solved, (even_out, odd_out))


def level_step(group, meta, centre, even_in, odd_in, first, wide_a, old_b, out, solved, even_out, odd_out, window, sems):
    count = first.shape[0]

    @pl.when(meta[0] == group)
    def _():
        window[REACH : REACH + count] = centre[...]
        place(window, meta[1], even_in, odd_in)
        first_of_group(wide_a, first, window, solved, 0, slice(None))
        emit_sends(meta[1], solved, (even_out, odd_out))

    @pl.when(meta[0] == group - 1)
    def _():
        store(first, old_b, out, slice(None), sems)


def later_step(group, chunk, final, meta, centre, even_in, odd_in, edges, first, wide_a, wide_b, base_b, old_a, old_b, *rest):
    stages = final and chunk == CHUNKS - 1
    if stages:
        made_a, made_b, _, out, window, level_a, solved, stage, sems = rest
    else:
        _, out, solved, solved_a, *sends, window, level_a, sems = rest
    cases = solved.shape[-1]
    at = columns(chunk, cases)
    on_out = pl.ds(chunk * cases, cases)
    count = first.shape[0]

    @pl.when(meta[0] == group)
    def _():
        odd = meta[1]
        halo = 2 * REACH
        window[halo : halo + count] = centre[...]
        place(window, odd, even_in, odd_in)
        first_of_group(wide_a, first, window.at[pl.ds(REACH, count + halo)], level_a, REACH, at)
        done, copies = None, []
        if stages:
            copies = [
                pltpu.make_async_copy(stage.at[level, pl.ds(2 * p, 2)], out.at[level, pl.ds(2 * p, 2)], sems.at[level, p])
                for level in range(2)
                for p in range(count // 2)
            ]
            before = slice(0, chunk * cases)
            stage[0, :, :, before] = made_a[...]
            stage[1, :, :, before] = made_b[...]
            stage[0, :, :, at] = level_a[REACH : REACH + count]
            for copy in copies[: count // 2]:
                copy.start()

            def done(p):
                stage[1, 2 * p : 2 * p + 2, :, at] = solved[2 * p : 2 * p + 2]
                copies[count // 2 + p].start()

        for side in range(2):
            for i in range(REACH):
                put = side * (count + REACH) + i
                base = edges[side, i * EDGE + SPAN + chunk]
                blocks = jnp.concatenate([edges[side, i * EDGE + d] for d in range(SPAN)], axis=1)
                row = dot(blocks, flat(window, put, SPAN)) + base.astype(jnp.float32)
                level_a[put] = row.astype(level_a.dtype)
        second_of_group(wide_b, base_b, level_a, solved, at, done)
        if stages:
            for copy in copies:
                copy.wait()
        else:
            emit_sends(odd, solved, sends)
            solved_a[...] = level_a[REACH : REACH + count]

    @pl.when(meta[0] == group - 1)
    def _():
        store(old_a.at[:, :, at] if old_a.shape[-1] > cases else old_a, old_b, out, on_out, *([sems.at[0]] if stages else [sems]))


def shaped(shape, dtype=jnp.bfloat16):
    return jax.ShapeDtypeStruct(shape, dtype)


def params(**more):
    return pltpu.CompilerParams(vmem_limit_bytes=24 * 1024 * 1024, **more)


def in_hbm(value):
    return pltpu.with_memory_space_constraint(value, pltpu.HBM)


def after(values, *earlier):
    return lax.optimization_barrier((values, earlier))[0]


def per_device(chain, rows, right_side, lower_blocks, block_scale, diag_inverse, depend_rows):
    _, count, block, cases = right_side.shape
    terms = lower_blocks.shape[2]
    width = SPAN * block
    part = cases // CHUNKS
    halo = 2 * REACH
    row = lax.axis_index("rows")
    meta = jnp.stack([lax.axis_index("chain"), row % 2, row * count]).astype(jnp.int32)
    depend = in_hbm(depend_rows.transpose(2, 0, 1))
    scale = in_hbm(block_scale.transpose(2, 0, 1))
    tables = [pltpu.SMEM(depend.shape, jnp.int32), pltpu.SMEM(scale.shape, jnp.float32)]
    right_side, lower_blocks, diag_inverse = in_hbm(right_side), in_hbm(lower_blocks), in_hbm(diag_inverse)
    mates = (even_mate, odd_mate)

    def exchange(groups, values, idle=None):
        return [
            lax.ppermute(value, AXES, inner_pairs(groups, mate, chain, rows, idle))
            for value, mate in zip(values, mates)
        ]

    def travel(group, centre, sides):
        return [lax.ppermute(centre, AXES, hop_pairs(group, same_row, chain, rows))] + [
            lax.ppermute(value, AXES, hop_pairs(group, mate, chain, rows)) for value, mate in zip(sides, mates)
        ]

    def call(kernel, name, in_specs, out_shape, out_specs=None, **more):
        return pl.pallas_call(
            kernel,
            in_specs=in_specs,
            out_specs=out_specs or [VMEM] * len(out_shape),
            out_shape=out_shape,
            compiler_params=params(),
            name=name,
            **more,
        )

    whole, half = shaped((count, block, cases)), shaped((count, block, part))
    whole_edge, half_edge = shaped((REACH, block, cases)), shaped((halo, block, part))

    total = REACH * EDGE
    soon = REACH * cases // block
    edge_shapes = [shaped((size, block, block)) for size in (soon, total - soon)]
    first, *edge_w = call(
        first_kernel,
        "first_level",
        [SMEM] + [HBM] * 5,
        [whole, *(shape for shape in edge_shapes for _ in range(2))],
        scratch_shapes=[
            pltpu.VMEM((count, block, block), jnp.bfloat16),
            pltpu.VMEM(whole.shape, jnp.bfloat16),
            pltpu.VMEM((2, REACH, terms, block, block), jnp.bfloat16),
            *tables,
            pltpu.VMEM((REACH, SPAN, block, block), jnp.float32),
            pltpu.VMEM((2, total, block, block), jnp.bfloat16),
            pltpu.SemaphoreType.DMA((3, 4)),
        ],
    )(meta, depend, scale, lower_blocks, diag_inverse, right_side)
    sides = exchange([0, *range(2, chain)], edge_w[:2], 1)

    pairs = count // 2
    wide_shape = shaped((pairs, 2 * block, width + block))

    def prepare(turn, meta):
        return call(
            functools.partial(prepare_kernel, turn),
            f"prepare_{turn}",
            [SMEM] + [HBM] * 5,
            [wide_shape, shaped(whole.shape, jnp.float32)],
            scratch_shapes=[
                pltpu.VMEM(lower_blocks.shape[1:], jnp.bfloat16),
                pltpu.VMEM(diag_inverse.shape[1:], jnp.bfloat16),
                pltpu.VMEM(whole.shape, jnp.bfloat16),
                *tables,
                pltpu.VMEM((2, SPAN, block, block), jnp.float32),
                pltpu.SemaphoreType.DMA((4, pairs)),
            ],
        )(meta, depend, scale, lower_blocks, diag_inverse, right_side)

    wide_a, base_0 = prepare(0, meta)

    padded = pltpu.VMEM((count + halo, block, cases), jnp.bfloat16)
    padded_half = pltpu.VMEM((count + halo, block, part), jnp.bfloat16)
    solved, *sends = call(
        functools.partial(exchanged_step, 0, None),
        "step_0",
        [SMEM] + [VMEM] * 5,
        [whole, whole_edge, whole_edge],
        scratch_shapes=[padded],
    )(meta, first, *sides, wide_a, base_0)
    wide_b, base_b = prepare(1, after(meta, solved))
    arrived = travel(0, solved, sends)

    later_w = exchange(range(2, chain), after(edge_w[2:], sides))
    edges, = call(
        order_kernel, "order", [SMEM] + [VMEM] * 4, [shaped((2, total, block, block))]
    )(meta, *sides, *later_w)

    out, own, *sides = call(
        functools.partial(level_step, 1),
        "step_1",
        [SMEM] + [VMEM] * 6,
        [shaped(right_side.shape), whole, whole_edge, whole_edge],
        [ANY] + [VMEM] * 3,
        scratch_shapes=[padded, pltpu.SemaphoreType.DMA((2,))],
    )(meta, *arrived, first, wide_a, solved)
    sides = exchange([1], sides, 0)
    made_a = [own] * CHUNKS
    sent = []
    for chunk in range(CHUNKS):
        sent.append(
            call(
                functools.partial(exchanged_step, 1, chunk),
                f"step_1_{chunk}",
                [SMEM] + [VMEM] * 5,
                [half, half_edge, half_edge],
                scratch_shapes=[padded_half],
            )(meta, own, *sides, wide_b, base_b)
        )

    for group in range(2, chain):
        final = group == chain - 1
        arrived = [travel(group - 1, solved, sends) for solved, *sends in sent]
        made = []
        for chunk in range(CHUNKS):
            stages = final and chunk == CHUNKS - 1
            outs = [] if stages else [half, half] + ([] if final else [half_edge] * 2)
            extra = [made[0][1], made[0][0][0]] if stages else []
            sems = (2, pairs) if stages else (2,)
            out, *now = call(
                functools.partial(later_step, group, chunk, final),
                f"step_{group}_{chunk}",
                [SMEM] + [VMEM] * (10 + len(extra)) + [ANY],
                [shaped(right_side.shape), *outs],
                [ANY] + [VMEM] * len(outs),
                scratch_shapes=[
                    pltpu.VMEM((count + 2 * halo, block, part), jnp.bfloat16),
                    padded_half,
                    *([pltpu.VMEM(shape, jnp.bfloat16) for shape in (half.shape, (2, *whole.shape))] if stages else []),
                    pltpu.SemaphoreType.DMA(sems),
                ],
                input_output_aliases={11 + len(extra): 0},
            )(
                meta,
                *arrived[chunk],
                edges,
                first,
                wide_a,
                wide_b,
                base_b,
                made_a[chunk],
                sent[chunk][0],
                *extra,
                out,
            )
            if now:
                solved, level, *sends = now
                made.append(((solved, *sends), level))
        sent, made_a = [values[0] for values in made], [values[1] for values in made]
    return out


def solution(mesh):
    placed = (
        P("chain", "rows", None, None),
        P("chain", "rows", None, None, None),
        P("chain", "rows", None),
        P("chain", "rows", None, None),
        P("chain", "rows", None),
    )
    return jax.shard_map(
        functools.partial(per_device, mesh.shape["chain"], mesh.shape["rows"]),
        mesh=mesh,
        in_specs=placed,
        out_specs=P("chain", "rows", None, None),
        check_vma=False,
    )
```

```python
import functools

import jax
import jax.numpy as jnp
from jax import lax
from jax.experimental import pallas as pl
from jax.experimental.pallas import tpu as pltpu
from jax.sharding import PartitionSpec as P

REACH = 2
SPAN = 2 * REACH + 1
CHUNKS = 2
EDGE = SPAN + CHUNKS
AXES = ("chain", "rows")
VMEM = pl.BlockSpec(memory_space=pltpu.VMEM)
SMEM = pl.BlockSpec(memory_space=pltpu.SMEM)
ANY = pl.BlockSpec(memory_space=pl.ANY)
HBM = pl.BlockSpec(memory_space=pltpu.HBM)


def even_mate(row, rows):
    return row ^ 1


def odd_mate(row, rows):
    mate = row + 1 if row % 2 else row - 1
    return mate if 0 <= mate < rows else row


def same_row(row, rows):
    return row


def swap_groups(chain, taken=()):
    return {g: g ^ 1 for g in range(chain) if g not in taken}


def hop_pairs(group, mate, chain, rows):
    if group % 2 == 0:
        moves = swap_groups(chain)
    else:
        moves = swap_groups(chain, range(group - 1, group + 3))
        moves.update({group: group + 1, group - 1: group, group + 1: group + 2, group + 2: group - 1})
    return [
        (source * rows + r, target * rows + (mate(r, rows) if source == group else r))
        for source, target in moves.items()
        for r in range(rows)
    ]


def inner_pairs(groups, mate, chain, rows, idle=None):
    pairs = []
    paired = [r for r in range(rows) if mate(r, rows) != r]
    for r in range(rows):
        if r not in paired:
            moves = swap_groups(chain)
        else:
            moves = swap_groups(chain, [*groups, idle])
            pairs += [(g * rows + r, g * rows + mate(r, rows)) for g in groups]
            if idle is not None:
                alike = [q for q in paired if q % 2 == r % 2]
                pairs.append((idle * rows + r, idle * rows + alike[(alike.index(r) + 1) % len(alike)]))
        pairs += [(a * rows + r, b * rows + r) for a, b in moves.items()]
    return pairs


def dot(a, b):
    return jnp.dot(a, b, preferred_element_type=jnp.float32)


def by_parity(odd, low_value, high_value, even_ref, odd_ref):
    @pl.when(odd == 0)
    def _():
        even_ref[...] = high_value()
        odd_ref[...] = low_value()

    @pl.when(odd == 1)
    def _():
        even_ref[...] = low_value()
        odd_ref[...] = high_value()


def premultiplied(meta, depend, scale, lower, inverse, acc, level, q):
    acc[...] = jnp.zeros_like(acc)
    for k in range(len(lower)):
        column = jnp.clip(depend[k, level, q] - (meta[2] + q) + REACH, 0, SPAN - 1)
        acc[column] += scale[k, level, q] * dot(inverse, lower[k])


def first_kernel(meta, depend_hbm, scale_hbm, lower_hbm, inverse_hbm, right_hbm, solved, even_a, odd_a, even_b, odd_b, inverse, right, lower, depend, scale, acc, edges, sems):
    count = inverse.shape[0]
    block = inverse.shape[1]
    parts = right.shape[2] // block
    steps = 4
    size = count // steps
    loads = []
    for step in range(steps):
        rows = pl.ds(step * size, size)
        loads.append(
            (
                pltpu.make_async_copy(inverse_hbm.at[0, rows], inverse.at[rows], sems.at[0, step]),
                pltpu.make_async_copy(right_hbm.at[0, rows], right.at[rows], sems.at[1, step]),
            )
        )
    ends = (0, count - REACH)

    def edge_load(side):
        rows = pl.ds(ends[side], REACH)
        return pltpu.make_async_copy(lower_hbm.at[0, rows], lower.at[side], sems.at[2, side])

    tables = [
        pltpu.make_async_copy(source, target, sems.at[2, 2 + i])
        for i, (source, target) in enumerate(((depend_hbm, depend), (scale_hbm, scale)))
    ]

    for pair in loads:
        for load in pair:
            load.start()

    @pl.when(meta[0] > 1)
    def _():
        for load in (edge_load(0), edge_load(1), *tables):
            load.start()

    for step in range(steps):
        for load in loads[step]:
            load.wait()
        for q in range(step * size, (step + 1) * size):
            solved[q] = dot(inverse[q], right[q]).astype(solved.dtype)

    def row_parts(q):
        return [solved[q, :, part * block : (part + 1) * block] for part in range(parts)]

    @pl.when(meta[0] < 2)
    def _():
        for side in range(2):
            for i in range(REACH):
                for part, value in enumerate(row_parts(ends[side] + i)):
                    edges[side, i * parts + part] = value

    @pl.when(meta[0] > 1)
    def _():
        for table in tables:
            table.wait()
        for side in range(2):
            edge_load(side).wait()
            for i in range(REACH):
                q = ends[side] + i
                blocks = [lower[side, i, k] for k in range(lower.shape[2])]
                premultiplied(meta, depend, scale, blocks, inverse[q], acc.at[i], 0, q)
                for d in range(SPAN):
                    edges[side, i * EDGE + d] = (-acc[i, d]).astype(edges.dtype)
                for part, value in enumerate(row_parts(q)):
                    edges[side, i * EDGE + SPAN + part] = value

    soon = even_a.shape[0]
    by_parity(meta[1], lambda: edges[0, :soon], lambda: edges[1, :soon], even_a, odd_a)

    @pl.when(meta[0] > 1)
    def _():
        by_parity(meta[1], lambda: edges[0, soon:], lambda: edges[1, soon:], even_b, odd_b)


def prepare_kernel(turn, meta, depend_hbm, scale_hbm, lower_hbm, inverse_hbm, right_hbm, wide, base, lower, inverse, right, depend, scale, acc, sems):
    pairs = wide.shape[0]
    block = lower.shape[-1]
    level = jnp.where(meta[0] == 0, 1, turn)

    def loads(p):
        rows = pl.ds(2 * p, 2)
        return [
            pltpu.make_async_copy(source.at[level, rows], target.at[rows], sems.at[i, p])
            for i, (source, target) in enumerate(((lower_hbm, lower), (inverse_hbm, inverse), (right_hbm, right)))
        ]

    @pl.when((meta[0] > 0) | (turn == 0))
    def _():
        tables = [
            pltpu.make_async_copy(source, target, sems.at[3, i])
            for i, (source, target) in enumerate(((depend_hbm, depend), (scale_hbm, scale)))
        ]
        for table in tables:
            table.start()
        for p in range(pairs):
            for load in loads(p):
                load.start()
        for table in tables:
            table.wait()

        @pl.loop(0, pairs)
        def _(p):
            for load in loads(p):
                load.wait()
            for half in range(2):
                q = 2 * p + half
                blocks = [lower[q, k] for k in range(lower.shape[1])]
                premultiplied(meta, depend, scale, blocks, inverse[q], acc.at[half], level, q)
                at = slice(half * block, (half + 1) * block)
                for d in range(SPAN):
                    wide[p, at, (d + half) * block : (d + half + 1) * block] = (-acc[half, d]).astype(wide.dtype)
                other = 0 if half else SPAN
                wide[p, at, other * block : (other + 1) * block] = jnp.zeros((block, block), wide.dtype)
                base[q] = dot(inverse[q], right[q])


def order_kernel(meta, even_a, odd_a, even_b, odd_b, edges):
    @pl.when(meta[0] > 1)
    def _():
        odd = meta[1]
        soon = even_a.shape[0]
        edges[1 - odd, :soon] = even_a[...]
        edges[1 - odd, soon:] = even_b[...]
        edges[odd, :soon] = odd_a[...]
        edges[odd, soon:] = odd_b[...]


def flat(ref, start, count, at=slice(None)):
    block = ref[start : start + count, :, at]
    return block.reshape(count * block.shape[1], block.shape[2])


def place(window, odd, even_in, odd_in, at=slice(None)):
    halo = even_in.shape[0]
    low, high = 0, window.shape[0] - halo
    window[pl.ds(jnp.where(odd == 1, low, high), halo)] = even_in[:, :, at]
    window[pl.ds(jnp.where(odd == 1, high, low), halo)] = odd_in[:, :, at]


def columns(chunk, cases):
    return slice(None) if chunk is None else slice(chunk * cases, (chunk + 1) * cases)


def first_of_group(wide_a, first, window, level_a, put, at):
    for p in range(wide_a.shape[0]):
        rows = dot(wide_a[p], flat(window, 2 * p, SPAN + 1)) + flat(first, 2 * p, 2, at).astype(jnp.float32)
        level_a[put + 2 * p : put + 2 * p + 2] = rows.astype(level_a.dtype).reshape(2, *level_a.shape[1:])


def second_of_group(wide_b, base_b, level_a, solved, at, done=None):
    for p in range(wide_b.shape[0]):
        rows = dot(wide_b[p], flat(level_a, 2 * p, SPAN + 1)) + flat(base_b, 2 * p, 2, at)
        solved[2 * p : 2 * p + 2] = rows.astype(solved.dtype).reshape(2, *solved.shape[1:])
        if done is not None:
            done(p)


def emit_sends(odd, solved, sends):
    if sends:
        size = sends[0].shape[0]
        count = solved.shape[0]
        by_parity(odd, lambda: solved[:size], lambda: solved[count - size :], *sends)


def store(level_a, solved, out, at, sems):
    copies = [
        pltpu.make_async_copy(source, out.at[level, :, :, at], sems.at[level])
        for level, source in ((0, level_a), (1, solved))
    ]
    for copy in copies:
        copy.start()
    for copy in copies:
        copy.wait()


def exchanged_step(group, meta, own, even_in, odd_in, wide_b, base_b, *rest):
    *parts_out, even_out, odd_out, level_a, solved = rest

    @pl.when(meta[0] == group)
    def _():
        count, block = own.shape[0], own.shape[1]
        level_a[REACH : REACH + count] = own[...]
        if even_in.shape[0] == REACH:
            place(level_a, meta[1], even_in, odd_in)
        else:
            parts = even_in.shape[0] // REACH
            low, high = 0, count + REACH
            for i in range(REACH):
                for part in range(parts):
                    cols = slice(part * block, (part + 1) * block)
                    level_a[i + jnp.where(meta[1] == 1, low, high), :, cols] = even_in[i * parts + part]
                    level_a[i + jnp.where(meta[1] == 1, high, low), :, cols] = odd_in[i * parts + part]
        second_of_group(wide_b, base_b, level_a, solved, slice(None))
        emit_sends(meta[1], solved, (even_out, odd_out))
        for i, part in enumerate(parts_out):
            part[...] = solved[:, :, columns(i, part.shape[-1])]


def level_step(group, meta, centre, even_in, odd_in, first, wide_a, old_b, out, solved, even_out, odd_out, window, sems):
    count = first.shape[0]

    @pl.when(meta[0] == group)
    def _():
        window[REACH : REACH + count] = centre[...]
        place(window, meta[1], even_in, odd_in)
        first_of_group(wide_a, first, window, solved, 0, slice(None))
        emit_sends(meta[1], solved, (even_out, odd_out))

    @pl.when(meta[0] == group - 1)
    def _():
        store(first, old_b, out, slice(None), sems)


def later_step(group, chunk, final, meta, centre, even_in, odd_in, edges, first, wide_a, wide_b, base_b, old_a, old_b, *rest):
    ends = chunk == CHUNKS - 1
    stages = final and ends
    if stages:
        made_a, made_b, _, out, window, level_a, solved, stage, sems = rest
    elif ends:
        made_b, _, out, joined, solved, solved_a, *sends, window, level_a, sems = rest
    else:
        _, out, solved, solved_a, *sends, window, level_a, sems = rest
    cases = solved.shape[-1]
    at = columns(chunk, cases)
    on_out = pl.ds(chunk * cases, cases)
    count = first.shape[0]

    @pl.when(meta[0] == group)
    def _():
        odd = meta[1]
        halo = 2 * REACH
        window[halo : halo + count] = centre[:, :, at if centre.shape[-1] > cases else slice(None)]
        place(window, odd, even_in, odd_in, at if even_in.shape[-1] > cases else slice(None))
        first_of_group(wide_a, first, window.at[pl.ds(REACH, count + halo)], level_a, REACH, at)
        done, copies = None, []
        if stages:
            copies = [
                pltpu.make_async_copy(stage.at[level, pl.ds(2 * p, 2)], out.at[level, pl.ds(2 * p, 2)], sems.at[level, p])
                for level in range(2)
                for p in range(count // 2)
            ]
            before = slice(0, chunk * cases)
            stage[0, :, :, before] = made_a[...]
            stage[1, :, :, before] = made_b[...]
            stage[0, :, :, at] = level_a[REACH : REACH + count]
            for copy in copies[: count // 2]:
                copy.start()

            def done(p):
                stage[1, 2 * p : 2 * p + 2, :, at] = solved[2 * p : 2 * p + 2]
                copies[count // 2 + p].start()

        for side in range(2):
            for i in range(REACH):
                put = side * (count + REACH) + i
                base = edges[side, i * EDGE + SPAN + chunk]
                blocks = jnp.concatenate([edges[side, i * EDGE + d] for d in range(SPAN)], axis=1)
                row = dot(blocks, flat(window, put, SPAN)) + base.astype(jnp.float32)
                level_a[put] = row.astype(level_a.dtype)
        second_of_group(wide_b, base_b, level_a, solved, at, done)
        if stages:
            for copy in copies:
                copy.wait()
        else:
            emit_sends(odd, solved, sends)
            solved_a[...] = level_a[REACH : REACH + count]
            if ends:
                joined[:, :, : chunk * cases] = made_b[...]
                joined[:, :, at] = solved[...]

    @pl.when(meta[0] == group - 1)
    def _():
        store(old_a.at[:, :, at] if old_a.shape[-1] > cases else old_a, old_b, out, on_out, *([sems.at[0]] if stages else [sems]))


def shaped(shape, dtype=jnp.bfloat16):
    return jax.ShapeDtypeStruct(shape, dtype)


def params(**more):
    return pltpu.CompilerParams(vmem_limit_bytes=24 * 1024 * 1024, **more)


def in_hbm(value):
    return pltpu.with_memory_space_constraint(value, pltpu.HBM)


def after(values, *earlier):
    return lax.optimization_barrier((values, earlier))[0]


def per_device(chain, rows, right_side, lower_blocks, block_scale, diag_inverse, depend_rows):
    _, count, block, cases = right_side.shape
    terms = lower_blocks.shape[2]
    width = SPAN * block
    part = cases // CHUNKS
    halo = 2 * REACH
    row = lax.axis_index("rows")
    meta = jnp.stack([lax.axis_index("chain"), row % 2, row * count]).astype(jnp.int32)
    depend = in_hbm(depend_rows.transpose(2, 0, 1))
    scale = in_hbm(block_scale.transpose(2, 0, 1))
    tables = [pltpu.SMEM(depend.shape, jnp.int32), pltpu.SMEM(scale.shape, jnp.float32)]
    right_side, lower_blocks, diag_inverse = in_hbm(right_side), in_hbm(lower_blocks), in_hbm(diag_inverse)
    mates = (even_mate, odd_mate)

    def exchange(groups, values, idle=None):
        return [
            lax.ppermute(value, AXES, inner_pairs(groups, mate, chain, rows, idle))
            for value, mate in zip(values, mates)
        ]

    def travel_centre(group, value):
        return lax.ppermute(value, AXES, hop_pairs(group, same_row, chain, rows))

    def travel_sides(group, values):
        return [lax.ppermute(value, AXES, hop_pairs(group, mate, chain, rows)) for value, mate in zip(values, mates)]

    def call(kernel, name, in_specs, out_shape, out_specs=None, **more):
        return pl.pallas_call(
            kernel,
            in_specs=in_specs,
            out_specs=out_specs or [VMEM] * len(out_shape),
            out_shape=out_shape,
            compiler_params=params(),
            name=name,
            **more,
        )

    whole, half = shaped((count, block, cases)), shaped((count, block, part))
    whole_edge, half_edge = shaped((REACH, block, cases)), shaped((halo, block, part))

    total = REACH * EDGE
    soon = REACH * cases // block
    edge_shapes = [shaped((size, block, block)) for size in (soon, total - soon)]
    first, *edge_w = call(
        first_kernel,
        "first_level",
        [SMEM] + [HBM] * 5,
        [whole, *(shape for shape in edge_shapes for _ in range(2))],
        scratch_shapes=[
            pltpu.VMEM((count, block, block), jnp.bfloat16),
            pltpu.VMEM(whole.shape, jnp.bfloat16),
            pltpu.VMEM((2, REACH, terms, block, block), jnp.bfloat16),
            *tables,
            pltpu.VMEM((REACH, SPAN, block, block), jnp.float32),
            pltpu.VMEM((2, total, block, block), jnp.bfloat16),
            pltpu.SemaphoreType.DMA((3, 4)),
        ],
    )(meta, depend, scale, lower_blocks, diag_inverse, right_side)
    sides = exchange([0, *range(2, chain)], edge_w[:2], 1)

    pairs = count // 2
    wide_shape = shaped((pairs, 2 * block, width + block))

    def prepare(turn, meta):
        return call(
            functools.partial(prepare_kernel, turn),
            f"prepare_{turn}",
            [SMEM] + [HBM] * 5,
            [wide_shape, shaped(whole.shape, jnp.float32)],
            scratch_shapes=[
                pltpu.VMEM(lower_blocks.shape[1:], jnp.bfloat16),
                pltpu.VMEM(diag_inverse.shape[1:], jnp.bfloat16),
                pltpu.VMEM(whole.shape, jnp.bfloat16),
                *tables,
                pltpu.VMEM((2, SPAN, block, block), jnp.float32),
                pltpu.SemaphoreType.DMA((4, pairs)),
            ],
        )(meta, depend, scale, lower_blocks, diag_inverse, right_side)

    wide_a, base_0 = prepare(0, meta)

    padded = pltpu.VMEM((count + halo, block, cases), jnp.bfloat16)
    padded_half = pltpu.VMEM((count + halo, block, part), jnp.bfloat16)
    solved, *sends = call(
        functools.partial(exchanged_step, 0),
        "step_0",
        [SMEM] + [VMEM] * 5,
        [whole, whole_edge, whole_edge],
        scratch_shapes=[padded, pltpu.VMEM(whole.shape, jnp.bfloat16)],
    )(meta, first, *sides, wide_a, base_0)
    wide_b, base_b = prepare(1, after(meta, solved))
    arrived = [travel_centre(0, solved), *travel_sides(0, sends)]

    later_w = exchange(range(2, chain), after(edge_w[2:], sides))
    edges, = call(
        order_kernel, "order", [SMEM] + [VMEM] * 4, [shaped((2, total, block, block))]
    )(meta, *sides, *later_w)

    out, own, *sides = call(
        functools.partial(level_step, 1),
        "step_1",
        [SMEM] + [VMEM] * 6,
        [shaped(right_side.shape), whole, whole_edge, whole_edge],
        [ANY] + [VMEM] * 3,
        scratch_shapes=[padded, pltpu.SemaphoreType.DMA((2,))],
    )(meta, *arrived, first, wide_a, solved)
    sides = exchange([1], sides, 0)
    made_a = [own] * CHUNKS
    wide_side = shaped((halo, block, cases))
    *sent, even_side, odd_side = call(
        functools.partial(exchanged_step, 1),
        "step_1_b",
        [SMEM] + [VMEM] * 5,
        [half] * CHUNKS + [wide_side] * 2,
        scratch_shapes=[padded, pltpu.VMEM(whole.shape, jnp.bfloat16)],
    )(meta, own, *sides, wide_b, base_b)
    sides = travel_sides(1, (even_side, odd_side))
    arrived = [
        [travel_centre(1, after(value, later_w) if chunk else value), *sides] for chunk, value in enumerate(sent)
    ]

    for group in range(2, chain):
        final = group == chain - 1
        made, sides = [], []
        for chunk in range(CHUNKS):
            ends = chunk == CHUNKS - 1
            stages = final and ends
            extra = [level for _, level in made] * stages + [value for value, _ in made] * ends
            outs = [whole] * (ends and not final) + [half, half] * (not stages) + [half_edge] * (2 * (not final))
            out, *now = call(
                functools.partial(later_step, group, chunk, final),
                f"step_{group}_{chunk}",
                [SMEM] + [VMEM] * (10 + len(extra)) + [ANY],
                [shaped(right_side.shape), *outs],
                [ANY] + [VMEM] * len(outs),
                scratch_shapes=[
                    pltpu.VMEM((count + 2 * halo, block, part), jnp.bfloat16),
                    padded_half,
                    *([pltpu.VMEM(shape, jnp.bfloat16) for shape in (half.shape, (2, *whole.shape))] if stages else []),
                    pltpu.SemaphoreType.DMA((2, pairs) if stages else (2,)),
                ],
                input_output_aliases={11 + len(extra): 0},
            )(
                meta,
                *arrived[chunk],
                edges,
                first,
                wide_a,
                wide_b,
                base_b,
                made_a[chunk],
                sent[chunk],
                *extra,
                out,
            )
            if not final:
                *joined, solved, level, even_side, odd_side = now
                made.append((solved, level))
                sides.append(travel_sides(group, (even_side, odd_side)))
            elif now:
                made.append(now)
        if not final:
            centre = travel_centre(group, joined[0])
            arrived = [[centre, *pair] for pair in sides]
            sent, made_a = [value for value, _ in made], [level for _, level in made]
    return out


def solution(mesh):
    placed = (
        P("chain", "rows", None, None),
        P("chain", "rows", None, None, None),
        P("chain", "rows", None),
        P("chain", "rows", None, None),
        P("chain", "rows", None),
    )
    return jax.shard_map(
        functools.partial(per_device, mesh.shape["chain"], mesh.shape["rows"]),
        mesh=mesh,
        in_specs=placed,
        out_specs=P("chain", "rows", None, None),
        check_vma=False,
    )
```

```python
import functools

import jax
import jax.numpy as jnp
from jax import lax
from jax.experimental import pallas as pl
from jax.experimental.pallas import tpu as pltpu
from jax.sharding import PartitionSpec as P

REACH = 2
SPAN = 2 * REACH + 1
CHUNKS = 2
EDGE = SPAN + CHUNKS
AXES = ("chain", "rows")
VMEM = pl.BlockSpec(memory_space=pltpu.VMEM)
SMEM = pl.BlockSpec(memory_space=pltpu.SMEM)
ANY = pl.BlockSpec(memory_space=pl.ANY)
HBM = pl.BlockSpec(memory_space=pltpu.HBM)


def even_mate(row, rows):
    return row ^ 1


def odd_mate(row, rows):
    mate = row + 1 if row % 2 else row - 1
    return mate if 0 <= mate < rows else row


def same_row(row, rows):
    return row


def swap_groups(chain, taken=()):
    return {g: g ^ 1 for g in range(chain) if g not in taken}


def hop_pairs(group, mate, chain, rows):
    if group % 2 == 0:
        moves = swap_groups(chain)
    else:
        moves = swap_groups(chain, range(group - 1, group + 3))
        moves.update({group: group + 1, group - 1: group, group + 1: group + 2, group + 2: group - 1})
    return [
        (source * rows + r, target * rows + (mate(r, rows) if source == group else r))
        for source, target in moves.items()
        for r in range(rows)
    ]


def inner_pairs(groups, mate, chain, rows, idle=None):
    pairs = []
    paired = [r for r in range(rows) if mate(r, rows) != r]
    for r in range(rows):
        if r not in paired:
            moves = swap_groups(chain)
        else:
            moves = swap_groups(chain, [*groups, idle])
            pairs += [(g * rows + r, g * rows + mate(r, rows)) for g in groups]
            if idle is not None:
                alike = [q for q in paired if q % 2 == r % 2]
                pairs.append((idle * rows + r, idle * rows + alike[(alike.index(r) + 1) % len(alike)]))
        pairs += [(a * rows + r, b * rows + r) for a, b in moves.items()]
    return pairs


def dot(a, b):
    return jnp.dot(a, b, preferred_element_type=jnp.float32)


def by_parity(odd, low_value, high_value, even_ref, odd_ref):
    @pl.when(odd == 0)
    def _():
        even_ref[...] = high_value()
        odd_ref[...] = low_value()

    @pl.when(odd == 1)
    def _():
        even_ref[...] = low_value()
        odd_ref[...] = high_value()


def premultiplied(meta, depend, scale, lower, inverse, acc, level, q):
    acc[...] = jnp.zeros_like(acc)
    for k in range(len(lower)):
        column = jnp.clip(depend[k, level, q] - (meta[2] + q) + REACH, 0, SPAN - 1)
        acc[column] += scale[k, level, q] * dot(inverse, lower[k])


def first_kernel(meta, depend_hbm, scale_hbm, lower_hbm, inverse_hbm, right_hbm, solved, even_a, odd_a, even_b, odd_b, inverse, right, lower, depend, scale, acc, edges, sems):
    count = inverse.shape[0]
    block = inverse.shape[1]
    parts = right.shape[2] // block
    steps = 4
    size = count // steps
    loads = []
    for step in range(steps):
        rows = pl.ds(step * size, size)
        loads.append(
            (
                pltpu.make_async_copy(inverse_hbm.at[0, rows], inverse.at[rows], sems.at[0, step]),
                pltpu.make_async_copy(right_hbm.at[0, rows], right.at[rows], sems.at[1, step]),
            )
        )
    ends = (0, count - REACH)

    def edge_load(side):
        rows = pl.ds(ends[side], REACH)
        return pltpu.make_async_copy(lower_hbm.at[0, rows], lower.at[side], sems.at[2, side])

    tables = [
        pltpu.make_async_copy(source, target, sems.at[2, 2 + i])
        for i, (source, target) in enumerate(((depend_hbm, depend), (scale_hbm, scale)))
    ]

    for pair in loads:
        for load in pair:
            load.start()

    @pl.when(meta[0] > 1)
    def _():
        for load in (edge_load(0), edge_load(1), *tables):
            load.start()

    for step in range(steps):
        for load in loads[step]:
            load.wait()
        for q in range(step * size, (step + 1) * size):
            solved[q] = dot(inverse[q], right[q]).astype(solved.dtype)

    def row_parts(q):
        return [solved[q, :, part * block : (part + 1) * block] for part in range(parts)]

    @pl.when(meta[0] < 2)
    def _():
        for side in range(2):
            for i in range(REACH):
                for part, value in enumerate(row_parts(ends[side] + i)):
                    edges[side, i * parts + part] = value

    @pl.when(meta[0] > 1)
    def _():
        for table in tables:
            table.wait()
        for side in range(2):
            edge_load(side).wait()
            for i in range(REACH):
                q = ends[side] + i
                blocks = [lower[side, i, k] for k in range(lower.shape[2])]
                premultiplied(meta, depend, scale, blocks, inverse[q], acc.at[i], 0, q)
                for d in range(SPAN):
                    edges[side, i * EDGE + d] = (-acc[i, d]).astype(edges.dtype)
                for part, value in enumerate(row_parts(q)):
                    edges[side, i * EDGE + SPAN + part] = value

    soon = even_a.shape[0]
    by_parity(meta[1], lambda: edges[0, :soon], lambda: edges[1, :soon], even_a, odd_a)

    @pl.when(meta[0] > 1)
    def _():
        by_parity(meta[1], lambda: edges[0, soon:], lambda: edges[1, soon:], even_b, odd_b)


def prepare_kernel(turn, meta, depend_hbm, scale_hbm, lower_hbm, inverse_hbm, right_hbm, wide, base, lower, inverse, right, depend, scale, acc, sems):
    pairs = wide.shape[0]
    block = lower.shape[-1]
    level = jnp.where(meta[0] == 0, 1, turn)

    def loads(p):
        rows = pl.ds(2 * p, 2)
        return [
            pltpu.make_async_copy(source.at[level, rows], target.at[rows], sems.at[i, p])
            for i, (source, target) in enumerate(((lower_hbm, lower), (inverse_hbm, inverse), (right_hbm, right)))
        ]

    @pl.when((meta[0] > 0) | (turn == 0))
    def _():
        tables = [
            pltpu.make_async_copy(source, target, sems.at[3, i])
            for i, (source, target) in enumerate(((depend_hbm, depend), (scale_hbm, scale)))
        ]
        for table in tables:
            table.start()
        for p in range(pairs):
            for load in loads(p):
                load.start()
        for table in tables:
            table.wait()

        @pl.loop(0, pairs)
        def _(p):
            for load in loads(p):
                load.wait()
            for half in range(2):
                q = 2 * p + half
                blocks = [lower[q, k] for k in range(lower.shape[1])]
                premultiplied(meta, depend, scale, blocks, inverse[q], acc.at[half], level, q)
                at = slice(half * block, (half + 1) * block)
                for d in range(SPAN):
                    wide[p, at, (d + half) * block : (d + half + 1) * block] = (-acc[half, d]).astype(wide.dtype)
                other = 0 if half else SPAN
                wide[p, at, other * block : (other + 1) * block] = jnp.zeros((block, block), wide.dtype)
                base[q] = dot(inverse[q], right[q])


def order_kernel(meta, even_a, odd_a, even_b, odd_b, edges):
    @pl.when(meta[0] > 1)
    def _():
        odd = meta[1]
        soon = even_a.shape[0]
        edges[1 - odd, :soon] = even_a[...]
        edges[1 - odd, soon:] = even_b[...]
        edges[odd, :soon] = odd_a[...]
        edges[odd, soon:] = odd_b[...]


def flat(ref, start, count, at=slice(None)):
    block = ref[start : start + count, :, at]
    return block.reshape(count * block.shape[1], block.shape[2])


def place(window, odd, even_in, odd_in, at=slice(None)):
    halo = even_in.shape[0]
    low, high = 0, window.shape[0] - halo
    window[pl.ds(jnp.where(odd == 1, low, high), halo)] = even_in[:, :, at]
    window[pl.ds(jnp.where(odd == 1, high, low), halo)] = odd_in[:, :, at]


def clear_beyond(meta, window, halo):
    for end in range(2):
        start = end * (window.shape[0] - halo)

        @pl.when(meta[3 + end] == 1)
        def _():
            window[start : start + halo] = jnp.zeros((halo, *window.shape[1:]), window.dtype)


def columns(chunk, cases):
    return slice(None) if chunk is None else slice(chunk * cases, (chunk + 1) * cases)


def first_of_group(wide_a, first, window, level_a, put, at):
    for p in range(wide_a.shape[0]):
        rows = dot(wide_a[p], flat(window, 2 * p, SPAN + 1)) + flat(first, 2 * p, 2, at).astype(jnp.float32)
        level_a[put + 2 * p : put + 2 * p + 2] = rows.astype(level_a.dtype).reshape(2, *level_a.shape[1:])


def second_of_group(wide_b, base_b, level_a, solved, at, done=None):
    for p in range(wide_b.shape[0]):
        rows = dot(wide_b[p], flat(level_a, 2 * p, SPAN + 1)) + flat(base_b, 2 * p, 2, at)
        solved[2 * p : 2 * p + 2] = rows.astype(solved.dtype).reshape(2, *solved.shape[1:])
        if done is not None:
            done(p)


def emit_sends(odd, solved, sends):
    if sends:
        size = sends[0].shape[0]
        count = solved.shape[0]
        by_parity(odd, lambda: solved[:size], lambda: solved[count - size :], *sends)


def store(level_a, solved, out, at, sems):
    copies = [
        pltpu.make_async_copy(source, out.at[level, :, :, at], sems.at[level])
        for level, source in ((0, level_a), (1, solved))
    ]
    for copy in copies:
        copy.start()
    for copy in copies:
        copy.wait()


def exchanged_step(group, chunk, meta, own, even_in, odd_in, wide_b, base_b, solved, even_out, odd_out, level_a):
    @pl.when(meta[0] == group)
    def _():
        at = columns(chunk, solved.shape[-1])
        count, block = own.shape[0], own.shape[1]
        level_a[REACH : REACH + count] = own[:, :, at]
        if even_in.shape[0] == REACH:
            place(level_a, meta[1], even_in, odd_in, at)
        else:
            parts = even_in.shape[0] // REACH
            low, high = 0, count + REACH
            for i in range(REACH):
                for part in range(parts):
                    cols = slice(part * block, (part + 1) * block)
                    level_a[i + jnp.where(meta[1] == 1, low, high), :, cols] = even_in[i * parts + part]
                    level_a[i + jnp.where(meta[1] == 1, high, low), :, cols] = odd_in[i * parts + part]
        clear_beyond(meta, level_a, REACH)
        second_of_group(wide_b, base_b, level_a, solved, at)
        emit_sends(meta[1], solved, (even_out, odd_out))


def level_step(group, meta, centre, even_in, odd_in, first, wide_a, old_b, out, solved, even_out, odd_out, window, sems):
    count = first.shape[0]

    @pl.when(meta[0] == group)
    def _():
        window[REACH : REACH + count] = centre[...]
        place(window, meta[1], even_in, odd_in)
        clear_beyond(meta, window, REACH)
        first_of_group(wide_a, first, window, solved, 0, slice(None))
        emit_sends(meta[1], solved, (even_out, odd_out))

    @pl.when(meta[0] == group - 1)
    def _():
        store(first, old_b, out, slice(None), sems)


def later_step(group, chunk, final, meta, *refs):
    stages = final and chunk == CHUNKS - 1
    if final and chunk == 0:
        even_in, odd_in, low, high, *rest = refs
        centre = [low, high]
    else:
        one, even_in, odd_in, *rest = refs
        centre = [one]
    edges, first, wide_a, wide_b, base_b, old_a, old_b, *rest = rest
    if stages:
        made_a, made_b, _, out, window, level_a, solved, stage, sems = rest
    else:
        _, out, solved, solved_a, *sends, window, level_a, sems = rest
    cases = solved.shape[-1]
    at = columns(chunk, cases)
    on_out = pl.ds(chunk * cases, cases)
    count = first.shape[0]

    @pl.when(meta[0] == group)
    def _():
        odd = meta[1]
        halo = 2 * REACH
        for i, part in enumerate(centre):
            window[halo + i * part.shape[0] : halo + (i + 1) * part.shape[0]] = part[...]
        place(window, odd, even_in, odd_in)
        clear_beyond(meta, window, halo)
        first_of_group(wide_a, first, window.at[pl.ds(REACH, count + halo)], level_a, REACH, at)
        done, copies = None, []
        if stages:
            copies = [
                pltpu.make_async_copy(stage.at[level, pl.ds(2 * p, 2)], out.at[level, pl.ds(2 * p, 2)], sems.at[level, p])
                for level in range(2)
                for p in range(count // 2)
            ]
            before = slice(0, chunk * cases)
            stage[0, :, :, before] = made_a[...]
            stage[1, :, :, before] = made_b[...]
            stage[0, :, :, at] = level_a[REACH : REACH + count]
            for copy in copies[: count // 2]:
                copy.start()

            def done(p):
                stage[1, 2 * p : 2 * p + 2, :, at] = solved[2 * p : 2 * p + 2]
                copies[count // 2 + p].start()

        for side in range(2):
            for i in range(REACH):
                put = side * (count + REACH) + i
                base = edges[side, i * EDGE + SPAN + chunk]
                blocks = jnp.concatenate([edges[side, i * EDGE + d] for d in range(SPAN)], axis=1)
                row = dot(blocks, flat(window, put, SPAN)) + base.astype(jnp.float32)
                level_a[put] = row.astype(level_a.dtype)
        clear_beyond(meta, level_a, REACH)
        second_of_group(wide_b, base_b, level_a, solved, at, done)
        if stages:
            for copy in copies:
                copy.wait()
        else:
            emit_sends(odd, solved, sends[:2])
            for i, part in enumerate(sends[2:]):
                part[...] = solved[i * part.shape[0] : (i + 1) * part.shape[0]]
            solved_a[...] = level_a[REACH : REACH + count]

    @pl.when(meta[0] == group - 1)
    def _():
        store(old_a.at[:, :, at] if old_a.shape[-1] > cases else old_a, old_b, out, on_out, *([sems.at[0]] if stages else [sems]))


def shaped(shape, dtype=jnp.bfloat16):
    return jax.ShapeDtypeStruct(shape, dtype)


def params(**more):
    return pltpu.CompilerParams(vmem_limit_bytes=24 * 1024 * 1024, **more)


def in_hbm(value):
    return pltpu.with_memory_space_constraint(value, pltpu.HBM)


def after(values, *earlier):
    return lax.optimization_barrier((values, earlier))[0]


def per_device(chain, rows, right_side, lower_blocks, block_scale, diag_inverse, depend_rows):
    _, count, block, cases = right_side.shape
    terms = lower_blocks.shape[2]
    width = SPAN * block
    part = cases // CHUNKS
    halo = 2 * REACH
    row = lax.axis_index("rows")
    ends = [row == 0, row == rows - 1]
    meta = jnp.stack([lax.axis_index("chain"), row % 2, row * count, *ends]).astype(jnp.int32)
    depend = in_hbm(depend_rows.transpose(2, 0, 1))
    scale = in_hbm(block_scale.transpose(2, 0, 1))
    tables = [pltpu.SMEM(depend.shape, jnp.int32), pltpu.SMEM(scale.shape, jnp.float32)]
    right_side, lower_blocks, diag_inverse = in_hbm(right_side), in_hbm(lower_blocks), in_hbm(diag_inverse)
    mates = (even_mate, odd_mate)

    def exchange(groups, values, idle=None):
        return [
            lax.ppermute(value, AXES, inner_pairs(groups, mate, chain, rows, idle))
            for value, mate in zip(values, mates)
        ]

    def travel(group, centre, sides):
        *sides, = sides
        centres = sides[2:] or [centre]
        kinds = [lax.ppermute(value, AXES, hop_pairs(group, same_row, chain, rows)) for value in centres]
        kinds += [lax.ppermute(value, AXES, hop_pairs(group, mate, chain, rows)) for value, mate in zip(sides, mates)]
        return [kinds[i] for i in (2, 3, 0, 1)] if len(kinds) > 3 else kinds

    def call(kernel, name, in_specs, out_shape, out_specs=None, **more):
        return pl.pallas_call(
            kernel,
            in_specs=in_specs,
            out_specs=out_specs or [VMEM] * len(out_shape),
            out_shape=out_shape,
            compiler_params=params(),
            name=name,
            **more,
        )

    whole, half = shaped((count, block, cases)), shaped((count, block, part))
    whole_edge, half_edge = shaped((REACH, block, cases)), shaped((halo, block, part))

    total = REACH * EDGE
    soon = REACH * cases // block
    edge_shapes = [shaped((size, block, block)) for size in (soon, total - soon)]
    first, *edge_w = call(
        first_kernel,
        "first_level",
        [SMEM] + [HBM] * 5,
        [whole, *(shape for shape in edge_shapes for _ in range(2))],
        scratch_shapes=[
            pltpu.VMEM((count, block, block), jnp.bfloat16),
            pltpu.VMEM(whole.shape, jnp.bfloat16),
            pltpu.VMEM((2, REACH, terms, block, block), jnp.bfloat16),
            *tables,
            pltpu.VMEM((REACH, SPAN, block, block), jnp.float32),
            pltpu.VMEM((2, total, block, block), jnp.bfloat16),
            pltpu.SemaphoreType.DMA((3, 4)),
        ],
    )(meta, depend, scale, lower_blocks, diag_inverse, right_side)
    sides = exchange([0, *range(2, chain)], edge_w[:2], 1)

    pairs = count // 2
    wide_shape = shaped((pairs, 2 * block, width + block))

    def prepare(turn, meta):
        return call(
            functools.partial(prepare_kernel, turn),
            f"prepare_{turn}",
            [SMEM] + [HBM] * 5,
            [wide_shape, shaped(whole.shape, jnp.float32)],
            scratch_shapes=[
                pltpu.VMEM(lower_blocks.shape[1:], jnp.bfloat16),
                pltpu.VMEM(diag_inverse.shape[1:], jnp.bfloat16),
                pltpu.VMEM(whole.shape, jnp.bfloat16),
                *tables,
                pltpu.VMEM((2, SPAN, block, block), jnp.float32),
                pltpu.SemaphoreType.DMA((4, pairs)),
            ],
        )(meta, depend, scale, lower_blocks, diag_inverse, right_side)

    wide_a, base_0 = prepare(0, meta)

    padded = pltpu.VMEM((count + halo, block, cases), jnp.bfloat16)
    padded_half = pltpu.VMEM((count + halo, block, part), jnp.bfloat16)
    solved, *sends = call(
        functools.partial(exchanged_step, 0, None),
        "step_0",
        [SMEM] + [VMEM] * 5,
        [whole, whole_edge, whole_edge],
        scratch_shapes=[padded],
    )(meta, first, *sides, wide_a, base_0)
    wide_b, base_b = prepare(1, after(meta, solved))
    arrived = travel(0, solved, sends)

    later_w = exchange(range(2, chain), after(edge_w[2:], sides))
    edges, = call(
        order_kernel, "order", [SMEM] + [VMEM] * 4, [shaped((2, total, block, block))]
    )(meta, *sides, *later_w)

    out, own, *sides = call(
        functools.partial(level_step, 1),
        "step_1",
        [SMEM] + [VMEM] * 6,
        [shaped(right_side.shape), whole, whole_edge, whole_edge],
        [ANY] + [VMEM] * 3,
        scratch_shapes=[padded, pltpu.SemaphoreType.DMA((2,))],
    )(meta, *arrived, first, wide_a, solved)
    sides = exchange([1], sides, 0)
    made_a = [own] * CHUNKS
    sent = []
    for chunk in range(CHUNKS):
        sent.append(
            call(
                functools.partial(exchanged_step, 1, chunk),
                f"step_1_{chunk}",
                [SMEM] + [VMEM] * 5,
                [half, half_edge, half_edge],
                scratch_shapes=[padded_half],
            )(meta, own, *sides, wide_b, base_b)
        )

    for group in range(2, chain):
        final = group == chain - 1
        arrived = [travel(group - 1, solved, sends) for solved, *sends in sent]
        made = []
        for chunk in range(CHUNKS):
            stages = final and chunk == CHUNKS - 1
            splits = group == chain - 2 and chunk == 0
            outs = [] if stages else [half, half] + ([] if final else [half_edge] * (4 if splits else 2))
            extra = [made[0][1], made[0][0][0]] if stages else []
            sems = (2, pairs) if stages else (2,)
            out, *now = call(
                functools.partial(later_step, group, chunk, final),
                f"step_{group}_{chunk}",
                [SMEM] + [VMEM] * (7 + len(arrived[chunk]) + len(extra)) + [ANY],
                [shaped(right_side.shape), *outs],
                [ANY] + [VMEM] * len(outs),
                scratch_shapes=[
                    pltpu.VMEM((count + 2 * halo, block, part), jnp.bfloat16),
                    padded_half,
                    *([pltpu.VMEM(shape, jnp.bfloat16) for shape in (half.shape, (2, *whole.shape))] if stages else []),
                    pltpu.SemaphoreType.DMA(sems),
                ],
                input_output_aliases={8 + len(arrived[chunk]) + len(extra): 0},
            )(
                meta,
                *arrived[chunk],
                edges,
                first,
                wide_a,
                wide_b,
                base_b,
                made_a[chunk],
                sent[chunk][0],
                *extra,
                out,
            )
            if now:
                solved, level, *sends = now
                made.append(((solved, *sends), level))
        sent, made_a = [values[0] for values in made], [values[1] for values in made]
    return out


def solution(mesh):
    placed = (
        P("chain", "rows", None, None),
        P("chain", "rows", None, None, None),
        P("chain", "rows", None),
        P("chain", "rows", None, None),
        P("chain", "rows", None),
    )
    return jax.shard_map(
        functools.partial(per_device, mesh.shape["chain"], mesh.shape["rows"]),
        mesh=mesh,
        in_specs=placed,
        out_specs=P("chain", "rows", None, None),
        check_vma=False,
    )
```

```python
import functools

import jax
import jax.numpy as jnp
from jax import lax
from jax.experimental import pallas as pl
from jax.experimental.pallas import tpu as pltpu
from jax.sharding import PartitionSpec as P

REACH = 2
SPAN = 2 * REACH + 1
CHUNKS = 2
EDGE = SPAN + CHUNKS
AXES = ("chain", "rows")
VMEM = pl.BlockSpec(memory_space=pltpu.VMEM)
SMEM = pl.BlockSpec(memory_space=pltpu.SMEM)
ANY = pl.BlockSpec(memory_space=pl.ANY)
HBM = pl.BlockSpec(memory_space=pltpu.HBM)


def even_mate(row, rows):
    return row ^ 1


def odd_mate(row, rows):
    mate = row + 1 if row % 2 else row - 1
    return mate if 0 <= mate < rows else row


def same_row(row, rows):
    return row


def swap_groups(chain, taken=()):
    return {g: g ^ 1 for g in range(chain) if g not in taken}


def hop_pairs(group, mate, chain, rows):
    if group % 2 == 0:
        moves = swap_groups(chain)
    else:
        moves = swap_groups(chain, range(group - 1, group + 3))
        moves.update({group: group + 1, group - 1: group, group + 1: group + 2, group + 2: group - 1})
    return [
        (source * rows + r, target * rows + (mate(r, rows) if source == group else r))
        for source, target in moves.items()
        for r in range(rows)
    ]


def inner_pairs(groups, mate, chain, rows, idle=None):
    pairs = []
    paired = [r for r in range(rows) if mate(r, rows) != r]
    for r in range(rows):
        if r not in paired:
            moves = swap_groups(chain)
        else:
            moves = swap_groups(chain, [*groups, idle])
            pairs += [(g * rows + r, g * rows + mate(r, rows)) for g in groups]
            if idle is not None:
                alike = [q for q in paired if q % 2 == r % 2]
                pairs.append((idle * rows + r, idle * rows + alike[(alike.index(r) + 1) % len(alike)]))
        pairs += [(a * rows + r, b * rows + r) for a, b in moves.items()]
    return pairs


def dot(a, b):
    return jnp.dot(a, b, preferred_element_type=jnp.float32)


def by_parity(odd, low_value, high_value, even_ref, odd_ref):
    @pl.when(odd == 0)
    def _():
        even_ref[...] = high_value()
        odd_ref[...] = low_value()

    @pl.when(odd == 1)
    def _():
        even_ref[...] = low_value()
        odd_ref[...] = high_value()


def premultiplied(meta, depend, scale, lower, inverse, acc, level, q):
    acc[...] = jnp.zeros_like(acc)
    for k in range(len(lower)):
        column = jnp.clip(depend[k, level, q] - (meta[2] + q) + REACH, 0, SPAN - 1)
        acc[column] += scale[k, level, q] * dot(inverse, lower[k])


def first_kernel(meta, depend_hbm, scale_hbm, lower_hbm, inverse_hbm, right_hbm, solved, even_a, odd_a, even_b, odd_b, inverse, right, lower, depend, scale, acc, edges, sems):
    count = inverse.shape[0]
    block = inverse.shape[1]
    parts = right.shape[2] // block
    steps = 4
    size = count // steps
    loads = []
    for step in range(steps):
        rows = pl.ds(step * size, size)
        loads.append(
            (
                pltpu.make_async_copy(inverse_hbm.at[0, rows], inverse.at[rows], sems.at[0, step]),
                pltpu.make_async_copy(right_hbm.at[0, rows], right.at[rows], sems.at[1, step]),
            )
        )
    ends = (0, count - REACH)

    def edge_load(side):
        rows = pl.ds(ends[side], REACH)
        return pltpu.make_async_copy(lower_hbm.at[0, rows], lower.at[side], sems.at[2, side])

    tables = [
        pltpu.make_async_copy(source, target, sems.at[2, 2 + i])
        for i, (source, target) in enumerate(((depend_hbm, depend), (scale_hbm, scale)))
    ]

    for pair in loads:
        for load in pair:
            load.start()

    @pl.when(meta[0] > 1)
    def _():
        for load in (edge_load(0), edge_load(1), *tables):
            load.start()

    for step in range(steps):
        for load in loads[step]:
            load.wait()
        for q in range(step * size, (step + 1) * size):
            solved[q] = dot(inverse[q], right[q]).astype(solved.dtype)

    def row_parts(q):
        return [solved[q, :, part * block : (part + 1) * block] for part in range(parts)]

    @pl.when(meta[0] < 2)
    def _():
        for side in range(2):
            for i in range(REACH):
                for part, value in enumerate(row_parts(ends[side] + i)):
                    edges[side, i * parts + part] = value

    @pl.when(meta[0] > 1)
    def _():
        for table in tables:
            table.wait()
        for side in range(2):
            edge_load(side).wait()
            for i in range(REACH):
                q = ends[side] + i
                blocks = [lower[side, i, k] for k in range(lower.shape[2])]
                premultiplied(meta, depend, scale, blocks, inverse[q], acc.at[i], 0, q)
                for d in range(SPAN):
                    edges[side, i * EDGE + d] = (-acc[i, d]).astype(edges.dtype)
                for part, value in enumerate(row_parts(q)):
                    edges[side, i * EDGE + SPAN + part] = value

    soon = even_a.shape[0]
    by_parity(meta[1], lambda: edges[0, :soon], lambda: edges[1, :soon], even_a, odd_a)

    @pl.when(meta[0] > 1)
    def _():
        by_parity(meta[1], lambda: edges[0, soon:], lambda: edges[1, soon:], even_b, odd_b)


def prepare_kernel(turn, meta, depend_hbm, scale_hbm, lower_hbm, inverse_hbm, right_hbm, wide, base, lower, inverse, right, depend, scale, acc, sems):
    pairs = wide.shape[0]
    block = lower.shape[-1]
    level = jnp.where(meta[0] == 0, 1, turn)

    def loads(p):
        rows = pl.ds(2 * p, 2)
        return [
            pltpu.make_async_copy(source.at[level, rows], target.at[rows], sems.at[i, p])
            for i, (source, target) in enumerate(((lower_hbm, lower), (inverse_hbm, inverse), (right_hbm, right)))
        ]

    @pl.when((meta[0] > 0) | (turn == 0))
    def _():
        tables = [
            pltpu.make_async_copy(source, target, sems.at[3, i])
            for i, (source, target) in enumerate(((depend_hbm, depend), (scale_hbm, scale)))
        ]
        for table in tables:
            table.start()
        for p in range(pairs):
            for load in loads(p):
                load.start()
        for table in tables:
            table.wait()

        @pl.loop(0, pairs)
        def _(p):
            for load in loads(p):
                load.wait()
            for half in range(2):
                q = 2 * p + half
                blocks = [lower[q, k] for k in range(lower.shape[1])]
                premultiplied(meta, depend, scale, blocks, inverse[q], acc.at[half], level, q)
                at = slice(half * block, (half + 1) * block)
                for d in range(SPAN):
                    wide[p, at, (d + half) * block : (d + half + 1) * block] = (-acc[half, d]).astype(wide.dtype)
                other = 0 if half else SPAN
                wide[p, at, other * block : (other + 1) * block] = jnp.zeros((block, block), wide.dtype)
                base[q] = dot(inverse[q], right[q])


def order_kernel(meta, even_a, odd_a, even_b, odd_b, edges):
    @pl.when(meta[0] > 1)
    def _():
        odd = meta[1]
        soon = even_a.shape[0]
        edges[1 - odd, :soon] = even_a[...]
        edges[1 - odd, soon:] = even_b[...]
        edges[odd, :soon] = odd_a[...]
        edges[odd, soon:] = odd_b[...]


def flat(ref, start, count, at=slice(None)):
    block = ref[start : start + count, :, at]
    return block.reshape(count * block.shape[1], block.shape[2])


def place(window, odd, even_in, odd_in, at=slice(None)):
    halo = even_in.shape[0]
    low, high = 0, window.shape[0] - halo
    window[pl.ds(jnp.where(odd == 1, low, high), halo)] = even_in[:, :, at]
    window[pl.ds(jnp.where(odd == 1, high, low), halo)] = odd_in[:, :, at]


def clear_beyond(meta, window, halo):
    for end in range(2):
        start = end * (window.shape[0] - halo)

        @pl.when(meta[3 + end] == 1)
        def _():
            window[start : start + halo] = jnp.zeros((halo, *window.shape[1:]), window.dtype)


def columns(chunk, cases):
    return slice(None) if chunk is None else slice(chunk * cases, (chunk + 1) * cases)


def first_of_group(wide_a, first, window, level_a, put, at):
    for p in range(wide_a.shape[0]):
        rows = dot(wide_a[p], flat(window, 2 * p, SPAN + 1)) + flat(first, 2 * p, 2, at).astype(jnp.float32)
        level_a[put + 2 * p : put + 2 * p + 2] = rows.astype(level_a.dtype).reshape(2, *level_a.shape[1:])


def second_of_group(wide_b, base_b, level_a, solved, at, done=None):
    for p in range(wide_b.shape[0]):
        rows = dot(wide_b[p], flat(level_a, 2 * p, SPAN + 1)) + flat(base_b, 2 * p, 2, at)
        solved[2 * p : 2 * p + 2] = rows.astype(solved.dtype).reshape(2, *solved.shape[1:])
        if done is not None:
            done(p)


def emit_sends(odd, solved, sends):
    if sends:
        size = sends[0].shape[0]
        count = solved.shape[0]
        by_parity(odd, lambda: solved[:size], lambda: solved[count - size :], *sends)


def store(level_a, solved, out, at, sems):
    copies = [
        pltpu.make_async_copy(source, out.at[level, :, :, at], sems.at[level])
        for level, source in ((0, level_a), (1, solved))
    ]
    for copy in copies:
        copy.start()
    for copy in copies:
        copy.wait()


def exchanged_step(group, chunk, meta, own, even_in, odd_in, wide_b, base_b, solved, even_out, odd_out, level_a):
    @pl.when(meta[0] == group)
    def _():
        at = columns(chunk, solved.shape[-1])
        count, block = own.shape[0], own.shape[1]
        level_a[REACH : REACH + count] = own[:, :, at]
        if even_in.shape[0] == REACH:
            place(level_a, meta[1], even_in, odd_in, at)
        else:
            parts = even_in.shape[0] // REACH
            low, high = 0, count + REACH
            for i in range(REACH):
                for part in range(parts):
                    cols = slice(part * block, (part + 1) * block)
                    level_a[i + jnp.where(meta[1] == 1, low, high), :, cols] = even_in[i * parts + part]
                    level_a[i + jnp.where(meta[1] == 1, high, low), :, cols] = odd_in[i * parts + part]
        clear_beyond(meta, level_a, REACH)
        second_of_group(wide_b, base_b, level_a, solved, at)
        emit_sends(meta[1], solved, (even_out, odd_out))


def level_step(group, meta, centre, even_in, odd_in, first, wide_a, old_b, out, solved, even_out, odd_out, window, sems):
    count = first.shape[0]

    @pl.when(meta[0] == group)
    def _():
        window[REACH : REACH + count] = centre[...]
        place(window, meta[1], even_in, odd_in)
        clear_beyond(meta, window, REACH)
        first_of_group(wide_a, first, window, solved, 0, slice(None))
        emit_sends(meta[1], solved, (even_out, odd_out))

    @pl.when(meta[0] == group - 1)
    def _():
        store(first, old_b, out, slice(None), sems)


def later_step(group, chunk, final, meta, *refs):
    stages = final and chunk == CHUNKS - 1
    if final:
        even_in, odd_in, low, high, *rest = refs
        centre = [low, high]
    else:
        one, even_in, odd_in, *rest = refs
        centre = [one]
    edges, first, wide_a, wide_b, base_b, old_a, old_b, *rest = rest
    joins = not final and len(rest) > 9
    if joins:
        made_b, *rest = rest
    if stages:
        made_a, made_b, _, out, window, level_a, solved, stage, sems = rest
    else:
        _, out, solved, solved_a, *sends, window, level_a, sems = rest
    cases = solved.shape[-1]
    at = columns(chunk, cases)
    on_out = pl.ds(chunk * cases, cases)
    count = first.shape[0]

    @pl.when(meta[0] == group)
    def _():
        odd = meta[1]
        halo = 2 * REACH
        for i, part in enumerate(centre):
            cut = at if part.shape[-1] > cases else slice(None)
            window[halo + i * part.shape[0] : halo + (i + 1) * part.shape[0]] = part[:, :, cut]
        place(window, odd, even_in, odd_in)
        clear_beyond(meta, window, halo)
        first_of_group(wide_a, first, window.at[pl.ds(REACH, count + halo)], level_a, REACH, at)
        done, copies = None, []
        if stages:
            copies = [
                pltpu.make_async_copy(stage.at[level, pl.ds(2 * p, 2)], out.at[level, pl.ds(2 * p, 2)], sems.at[level, p])
                for level in range(2)
                for p in range(count // 2)
            ]
            before = slice(0, chunk * cases)
            stage[0, :, :, before] = made_a[...]
            stage[1, :, :, before] = made_b[...]
            stage[0, :, :, at] = level_a[REACH : REACH + count]
            for copy in copies[: count // 2]:
                copy.start()

            def done(p):
                stage[1, 2 * p : 2 * p + 2, :, at] = solved[2 * p : 2 * p + 2]
                copies[count // 2 + p].start()

        for side in range(2):
            for i in range(REACH):
                put = side * (count + REACH) + i
                base = edges[side, i * EDGE + SPAN + chunk]
                blocks = jnp.concatenate([edges[side, i * EDGE + d] for d in range(SPAN)], axis=1)
                row = dot(blocks, flat(window, put, SPAN)) + base.astype(jnp.float32)
                level_a[put] = row.astype(level_a.dtype)
        clear_beyond(meta, level_a, REACH)
        second_of_group(wide_b, base_b, level_a, solved, at, done)
        if stages:
            for copy in copies:
                copy.wait()
        else:
            emit_sends(odd, solved, sends[:2])
            for i, part in enumerate(sends[2:]):
                rows = slice(i * part.shape[0], (i + 1) * part.shape[0])
                part[:, :, : chunk * cases] = made_b[rows]
                part[:, :, at] = solved[rows]
            solved_a[...] = level_a[REACH : REACH + count]

    @pl.when(meta[0] == group - 1)
    def _():
        store(old_a.at[:, :, at] if old_a.shape[-1] > cases else old_a, old_b, out, on_out, *([sems.at[0]] if stages else [sems]))


def shaped(shape, dtype=jnp.bfloat16):
    return jax.ShapeDtypeStruct(shape, dtype)


def params(**more):
    return pltpu.CompilerParams(vmem_limit_bytes=24 * 1024 * 1024, **more)


def in_hbm(value):
    return pltpu.with_memory_space_constraint(value, pltpu.HBM)


def after(values, *earlier):
    return lax.optimization_barrier((values, earlier))[0]


def per_device(chain, rows, right_side, lower_blocks, block_scale, diag_inverse, depend_rows):
    _, count, block, cases = right_side.shape
    terms = lower_blocks.shape[2]
    width = SPAN * block
    part = cases // CHUNKS
    halo = 2 * REACH
    row = lax.axis_index("rows")
    ends = [row == 0, row == rows - 1]
    meta = jnp.stack([lax.axis_index("chain"), row % 2, row * count, *ends]).astype(jnp.int32)
    depend = in_hbm(depend_rows.transpose(2, 0, 1))
    scale = in_hbm(block_scale.transpose(2, 0, 1))
    tables = [pltpu.SMEM(depend.shape, jnp.int32), pltpu.SMEM(scale.shape, jnp.float32)]
    right_side, lower_blocks, diag_inverse = in_hbm(right_side), in_hbm(lower_blocks), in_hbm(diag_inverse)
    mates = (even_mate, odd_mate)

    def exchange(groups, values, idle=None):
        return [
            lax.ppermute(value, AXES, inner_pairs(groups, mate, chain, rows, idle))
            for value, mate in zip(values, mates)
        ]

    def travel_centre(group, value):
        return lax.ppermute(value, AXES, hop_pairs(group, same_row, chain, rows))

    def travel_sides(group, values):
        return [lax.ppermute(value, AXES, hop_pairs(group, mate, chain, rows)) for value, mate in zip(values, mates)]

    def call(kernel, name, in_specs, out_shape, out_specs=None, **more):
        return pl.pallas_call(
            kernel,
            in_specs=in_specs,
            out_specs=out_specs or [VMEM] * len(out_shape),
            out_shape=out_shape,
            compiler_params=params(),
            name=name,
            **more,
        )

    whole, half = shaped((count, block, cases)), shaped((count, block, part))
    whole_edge, half_edge = shaped((REACH, block, cases)), shaped((halo, block, part))

    total = REACH * EDGE
    soon = REACH * cases // block
    edge_shapes = [shaped((size, block, block)) for size in (soon, total - soon)]
    first, *edge_w = call(
        first_kernel,
        "first_level",
        [SMEM] + [HBM] * 5,
        [whole, *(shape for shape in edge_shapes for _ in range(2))],
        scratch_shapes=[
            pltpu.VMEM((count, block, block), jnp.bfloat16),
            pltpu.VMEM(whole.shape, jnp.bfloat16),
            pltpu.VMEM((2, REACH, terms, block, block), jnp.bfloat16),
            *tables,
            pltpu.VMEM((REACH, SPAN, block, block), jnp.float32),
            pltpu.VMEM((2, total, block, block), jnp.bfloat16),
            pltpu.SemaphoreType.DMA((3, 4)),
        ],
    )(meta, depend, scale, lower_blocks, diag_inverse, right_side)
    sides = exchange([0, *range(2, chain)], edge_w[:2], 1)

    pairs = count // 2
    wide_shape = shaped((pairs, 2 * block, width + block))

    def prepare(turn, meta):
        return call(
            functools.partial(prepare_kernel, turn),
            f"prepare_{turn}",
            [SMEM] + [HBM] * 5,
            [wide_shape, shaped(whole.shape, jnp.float32)],
            scratch_shapes=[
                pltpu.VMEM(lower_blocks.shape[1:], jnp.bfloat16),
                pltpu.VMEM(diag_inverse.shape[1:], jnp.bfloat16),
                pltpu.VMEM(whole.shape, jnp.bfloat16),
                *tables,
                pltpu.VMEM((2, SPAN, block, block), jnp.float32),
                pltpu.SemaphoreType.DMA((4, pairs)),
            ],
        )(meta, depend, scale, lower_blocks, diag_inverse, right_side)

    wide_a, base_0 = prepare(0, meta)

    padded = pltpu.VMEM((count + halo, block, cases), jnp.bfloat16)
    padded_half = pltpu.VMEM((count + halo, block, part), jnp.bfloat16)
    solved, *sends = call(
        functools.partial(exchanged_step, 0, None),
        "step_0",
        [SMEM] + [VMEM] * 5,
        [whole, whole_edge, whole_edge],
        scratch_shapes=[padded],
    )(meta, first, *sides, wide_a, base_0)
    wide_b, base_b = prepare(1, after(meta, solved))
    arrived = [travel_centre(0, solved), *travel_sides(0, sends)]

    later_w = exchange(range(2, chain), after(edge_w[2:], sides))
    edges, = call(
        order_kernel, "order", [SMEM] + [VMEM] * 4, [shaped((2, total, block, block))]
    )(meta, *sides, *later_w)

    out, own, *sides = call(
        functools.partial(level_step, 1),
        "step_1",
        [SMEM] + [VMEM] * 6,
        [shaped(right_side.shape), whole, whole_edge, whole_edge],
        [ANY] + [VMEM] * 3,
        scratch_shapes=[padded, pltpu.SemaphoreType.DMA((2,))],
    )(meta, *arrived, first, wide_a, solved)
    sides = exchange([1], sides, 0)
    made_a = [own] * CHUNKS
    sent = []
    for chunk in range(CHUNKS):
        sent.append(
            call(
                functools.partial(exchanged_step, 1, chunk),
                f"step_1_{chunk}",
                [SMEM] + [VMEM] * 5,
                [half, half_edge, half_edge],
                scratch_shapes=[padded_half],
            )(meta, own, *sides, wide_b, base_b)
        )

    for group in range(2, chain):
        final = group == chain - 1
        if final:
            centres = [travel_centre(group - 1, value) for value in sent[-1][3:]]
            arrived = [[*travel_sides(group - 1, sends[:2]), *centres] for _, *sends in sent]
        else:
            arrived = [[travel_centre(group - 1, solved), *travel_sides(group - 1, sends)] for solved, *sends in sent]
        made = []
        for chunk in range(CHUNKS):
            stages = final and chunk == CHUNKS - 1
            joins = group == chain - 2 and chunk == CHUNKS - 1
            outs = [] if stages else [half, half] + ([] if final else [half_edge] * 2)
            outs += [shaped((count // 2, block, cases))] * (2 * joins)
            extra = [level for _, level in made] * stages + [values[0] for values, _ in made] * (stages or joins)
            sems = (2, pairs) if stages else (2,)
            out, *now = call(
                functools.partial(later_step, group, chunk, final),
                f"step_{group}_{chunk}",
                [SMEM] + [VMEM] * (7 + len(arrived[chunk]) + len(extra)) + [ANY],
                [shaped(right_side.shape), *outs],
                [ANY] + [VMEM] * len(outs),
                scratch_shapes=[
                    pltpu.VMEM((count + 2 * halo, block, part), jnp.bfloat16),
                    padded_half,
                    *([pltpu.VMEM(shape, jnp.bfloat16) for shape in (half.shape, (2, *whole.shape))] if stages else []),
                    pltpu.SemaphoreType.DMA(sems),
                ],
                input_output_aliases={8 + len(arrived[chunk]) + len(extra): 0},
            )(
                meta,
                *arrived[chunk],
                edges,
                first,
                wide_a,
                wide_b,
                base_b,
                made_a[chunk],
                sent[chunk][0],
                *extra,
                out,
            )
            if now:
                solved, level, *sends = now
                made.append(((solved, *sends), level))
        sent, made_a = [values[0] for values in made], [values[1] for values in made]
    return out


def solution(mesh):
    placed = (
        P("chain", "rows", None, None),
        P("chain", "rows", None, None, None),
        P("chain", "rows", None),
        P("chain", "rows", None, None),
        P("chain", "rows", None),
    )
    return jax.shard_map(
        functools.partial(per_device, mesh.shape["chain"], mesh.shape["rows"]),
        mesh=mesh,
        in_specs=placed,
        out_specs=P("chain", "rows", None, None),
        check_vma=False,
    )
```

```python
import functools

import jax
import jax.numpy as jnp
from jax import lax
from jax.experimental import pallas as pl
from jax.experimental.pallas import tpu as pltpu
from jax.sharding import PartitionSpec as P

REACH = 2
SPAN = 2 * REACH + 1
CHUNKS = 2
EDGE = SPAN + CHUNKS
AXES = ("chain", "rows")
VMEM = pl.BlockSpec(memory_space=pltpu.VMEM)
SMEM = pl.BlockSpec(memory_space=pltpu.SMEM)
ANY = pl.BlockSpec(memory_space=pl.ANY)
HBM = pl.BlockSpec(memory_space=pltpu.HBM)


def even_mate(row, rows):
    return row ^ 1


def odd_mate(row, rows):
    mate = row + 1 if row % 2 else row - 1
    return mate if 0 <= mate < rows else row


def same_row(row, rows):
    return row


def swap_groups(chain, taken=()):
    return {g: g ^ 1 for g in range(chain) if g not in taken}


def hop_pairs(group, mate, chain, rows):
    if group % 2 == 0:
        moves = swap_groups(chain)
    else:
        moves = swap_groups(chain, range(group - 1, group + 3))
        moves.update({group: group + 1, group - 1: group, group + 1: group + 2, group + 2: group - 1})
    return [
        (source * rows + r, target * rows + (mate(r, rows) if source == group else r))
        for source, target in moves.items()
        for r in range(rows)
    ]


def inner_pairs(groups, mate, chain, rows, idle=None):
    pairs = []
    paired = [r for r in range(rows) if mate(r, rows) != r]
    for r in range(rows):
        if r not in paired:
            moves = swap_groups(chain)
        else:
            moves = swap_groups(chain, [*groups, idle])
            pairs += [(g * rows + r, g * rows + mate(r, rows)) for g in groups]
            if idle is not None:
                alike = [q for q in paired if q % 2 == r % 2]
                pairs.append((idle * rows + r, idle * rows + alike[(alike.index(r) + 1) % len(alike)]))
        pairs += [(a * rows + r, b * rows + r) for a, b in moves.items()]
    return pairs


def dot(a, b):
    return jnp.dot(a, b, preferred_element_type=jnp.float32)


def by_parity(odd, low_value, high_value, even_ref, odd_ref):
    @pl.when(odd == 0)
    def _():
        even_ref[...] = high_value()
        odd_ref[...] = low_value()

    @pl.when(odd == 1)
    def _():
        even_ref[...] = low_value()
        odd_ref[...] = high_value()


def premultiplied(meta, depend, scale, lower, inverse, acc, level, q):
    acc[...] = jnp.zeros_like(acc)
    for k in range(len(lower)):
        column = jnp.clip(depend[k, level, q] - (meta[2] + q) + REACH, 0, SPAN - 1)
        acc[column] += scale[k, level, q] * dot(inverse, lower[k])


def first_kernel(meta, depend_hbm, scale_hbm, lower_hbm, inverse_hbm, right_hbm, solved, even_a, odd_a, even_b, odd_b, inverse, right, lower, depend, scale, acc, edges, sems):
    count = inverse.shape[0]
    block = inverse.shape[1]
    parts = right.shape[2] // block
    steps = 4
    size = count // steps
    loads = []
    for step in range(steps):
        rows = pl.ds(step * size, size)
        loads.append(
            (
                pltpu.make_async_copy(inverse_hbm.at[0, rows], inverse.at[rows], sems.at[0, step]),
                pltpu.make_async_copy(right_hbm.at[0, rows], right.at[rows], sems.at[1, step]),
            )
        )
    ends = (0, count - REACH)

    def edge_load(side):
        rows = pl.ds(ends[side], REACH)
        return pltpu.make_async_copy(lower_hbm.at[0, rows], lower.at[side], sems.at[2, side])

    tables = [
        pltpu.make_async_copy(source, target, sems.at[2, 2 + i])
        for i, (source, target) in enumerate(((depend_hbm, depend), (scale_hbm, scale)))
    ]

    for pair in loads:
        for load in pair:
            load.start()

    @pl.when(meta[0] > 1)
    def _():
        for load in (edge_load(0), edge_load(1), *tables):
            load.start()

    for step in range(steps):
        for load in loads[step]:
            load.wait()
        for q in range(step * size, (step + 1) * size):
            solved[q] = dot(inverse[q], right[q]).astype(solved.dtype)

    def row_parts(q):
        return [solved[q, :, part * block : (part + 1) * block] for part in range(parts)]

    @pl.when(meta[0] < 2)
    def _():
        for side in range(2):
            for i in range(REACH):
                for part, value in enumerate(row_parts(ends[side] + i)):
                    edges[side, i * parts + part] = value

    @pl.when(meta[0] > 1)
    def _():
        for table in tables:
            table.wait()
        for side in range(2):
            edge_load(side).wait()
            for i in range(REACH):
                q = ends[side] + i
                blocks = [lower[side, i, k] for k in range(lower.shape[2])]
                premultiplied(meta, depend, scale, blocks, inverse[q], acc.at[i], 0, q)
                for d in range(SPAN):
                    edges[side, i * EDGE + d] = (-acc[i, d]).astype(edges.dtype)
                for part, value in enumerate(row_parts(q)):
                    edges[side, i * EDGE + SPAN + part] = value

    soon = even_a.shape[0]
    by_parity(meta[1], lambda: edges[0, :soon], lambda: edges[1, :soon], even_a, odd_a)

    @pl.when(meta[0] > 1)
    def _():
        by_parity(meta[1], lambda: edges[0, soon:], lambda: edges[1, soon:], even_b, odd_b)


def prepare_kernel(turn, meta, depend_hbm, scale_hbm, lower_hbm, inverse_hbm, right_hbm, wide, base, lower, inverse, right, depend, scale, acc, sems):
    pairs = wide.shape[0]
    block = lower.shape[-1]
    level = jnp.where(meta[0] == 0, 1, turn)

    def loads(p):
        rows = pl.ds(2 * p, 2)
        return [
            pltpu.make_async_copy(source.at[level, rows], target.at[rows], sems.at[i, p])
            for i, (source, target) in enumerate(((lower_hbm, lower), (inverse_hbm, inverse), (right_hbm, right)))
        ]

    @pl.when((meta[0] > 0) | (turn == 0))
    def _():
        tables = [
            pltpu.make_async_copy(source, target, sems.at[3, i])
            for i, (source, target) in enumerate(((depend_hbm, depend), (scale_hbm, scale)))
        ]
        for table in tables:
            table.start()
        for p in range(pairs):
            for load in loads(p):
                load.start()
        for table in tables:
            table.wait()

        @pl.loop(0, pairs)
        def _(p):
            for load in loads(p):
                load.wait()
            for half in range(2):
                q = 2 * p + half
                blocks = [lower[q, k] for k in range(lower.shape[1])]
                premultiplied(meta, depend, scale, blocks, inverse[q], acc.at[half], level, q)
                at = slice(half * block, (half + 1) * block)
                for d in range(SPAN):
                    wide[p, at, (d + half) * block : (d + half + 1) * block] = (-acc[half, d]).astype(wide.dtype)
                other = 0 if half else SPAN
                wide[p, at, other * block : (other + 1) * block] = jnp.zeros((block, block), wide.dtype)
                base[q] = dot(inverse[q], right[q])


def order_kernel(meta, even_a, odd_a, even_b, odd_b, edges):
    @pl.when(meta[0] > 1)
    def _():
        odd = meta[1]
        soon = even_a.shape[0]
        edges[1 - odd, :soon] = even_a[...]
        edges[1 - odd, soon:] = even_b[...]
        edges[odd, :soon] = odd_a[...]
        edges[odd, soon:] = odd_b[...]


def flat(ref, start, count, at=slice(None)):
    block = ref[start : start + count, :, at]
    return block.reshape(count * block.shape[1], block.shape[2])


def place(window, odd, even_in, odd_in, at=slice(None)):
    halo = even_in.shape[0]
    low, high = 0, window.shape[0] - halo
    window[pl.ds(jnp.where(odd == 1, low, high), halo)] = even_in[:, :, at]
    window[pl.ds(jnp.where(odd == 1, high, low), halo)] = odd_in[:, :, at]


def clear_beyond(meta, window, halo):
    for end in range(2):
        start = end * (window.shape[0] - halo)

        @pl.when(meta[3 + end] == 1)
        def _():
            window[start : start + halo] = jnp.zeros((halo, *window.shape[1:]), window.dtype)


def columns(chunk, cases):
    return slice(None) if chunk is None else slice(chunk * cases, (chunk + 1) * cases)


def first_of_group(wide_a, first, window, level_a, put, at):
    for p in range(wide_a.shape[0]):
        rows = dot(wide_a[p], flat(window, 2 * p, SPAN + 1)) + flat(first, 2 * p, 2, at).astype(jnp.float32)
        level_a[put + 2 * p : put + 2 * p + 2] = rows.astype(level_a.dtype).reshape(2, *level_a.shape[1:])


def second_of_group(wide_b, base_b, level_a, solved, at, done=None):
    for p in range(wide_b.shape[0]):
        rows = dot(wide_b[p], flat(level_a, 2 * p, SPAN + 1)) + flat(base_b, 2 * p, 2, at)
        solved[2 * p : 2 * p + 2] = rows.astype(solved.dtype).reshape(2, *solved.shape[1:])
        if done is not None:
            done(p)


def emit_sends(odd, solved, sends):
    if sends:
        size = sends[0].shape[0]
        count = solved.shape[0]
        by_parity(odd, lambda: solved[:size], lambda: solved[count - size :], *sends)


def store(level_a, solved, out, at, sems):
    copies = [
        pltpu.make_async_copy(source, out.at[level, :, :, at], sems.at[level])
        for level, source in ((0, level_a), (1, solved))
    ]
    for copy in copies:
        copy.start()
    for copy in copies:
        copy.wait()


def exchanged_step(group, chunk, meta, own, even_in, odd_in, wide_b, base_b, solved, even_out, odd_out, level_a):
    @pl.when(meta[0] == group)
    def _():
        at = columns(chunk, solved.shape[-1])
        count, block = own.shape[0], own.shape[1]
        level_a[REACH : REACH + count] = own[:, :, at]
        if even_in.shape[0] == REACH:
            place(level_a, meta[1], even_in, odd_in, at)
        else:
            parts = even_in.shape[0] // REACH
            low, high = 0, count + REACH
            for i in range(REACH):
                for part in range(parts):
                    cols = slice(part * block, (part + 1) * block)
                    level_a[i + jnp.where(meta[1] == 1, low, high), :, cols] = even_in[i * parts + part]
                    level_a[i + jnp.where(meta[1] == 1, high, low), :, cols] = odd_in[i * parts + part]
        clear_beyond(meta, level_a, REACH)
        second_of_group(wide_b, base_b, level_a, solved, at)
        emit_sends(meta[1], solved, (even_out, odd_out))


def level_step(group, meta, centre, even_in, odd_in, first, wide_a, old_b, out, solved, even_out, odd_out, window, sems):
    count = first.shape[0]

    @pl.when(meta[0] == group)
    def _():
        window[REACH : REACH + count] = centre[...]
        place(window, meta[1], even_in, odd_in)
        clear_beyond(meta, window, REACH)
        first_of_group(wide_a, first, window, solved, 0, slice(None))
        emit_sends(meta[1], solved, (even_out, odd_out))

    @pl.when(meta[0] == group - 1)
    def _():
        store(first, old_b, out, slice(None), sems)


def later_step(group, chunk, final, meta, *refs):
    stages = final and chunk == CHUNKS - 1
    if final:
        even_in, odd_in, low, high, *rest = refs
        centre = [low, high]
    else:
        one, even_in, odd_in, *rest = refs
        centre = [one]
    edges, first, wide_a, wide_b, base_b, old_a, old_b, *rest = rest
    if stages:
        made_a, made_b, _, out, window, level_a, solved, stage, sems = rest
    else:
        _, out, solved, solved_a, *sends, window, level_a, sems = rest
    cases = solved.shape[-1]
    at = columns(chunk, cases)
    on_out = pl.ds(chunk * cases, cases)
    count = first.shape[0]

    @pl.when(meta[0] == group)
    def _():
        odd = meta[1]
        halo = 2 * REACH
        for i, part in enumerate(centre):
            window[halo + i * part.shape[0] : halo + (i + 1) * part.shape[0]] = part[...]
        place(window, odd, even_in, odd_in)
        clear_beyond(meta, window, halo)
        first_of_group(wide_a, first, window.at[pl.ds(REACH, count + halo)], level_a, REACH, at)
        done, copies = None, []
        if stages:
            copies = [
                pltpu.make_async_copy(stage.at[level, pl.ds(2 * p, 2)], out.at[level, pl.ds(2 * p, 2)], sems.at[level, p])
                for level in range(2)
                for p in range(count // 2)
            ]
            before = slice(0, chunk * cases)
            stage[0, :, :, before] = made_a[...]
            stage[1, :, :, before] = made_b[...]
            stage[0, :, :, at] = level_a[REACH : REACH + count]
            for copy in copies[: count // 2]:
                copy.start()

            def done(p):
                stage[1, 2 * p : 2 * p + 2, :, at] = solved[2 * p : 2 * p + 2]
                copies[count // 2 + p].start()

        for side in range(2):
            for i in range(REACH):
                put = side * (count + REACH) + i
                base = edges[side, i * EDGE + SPAN + chunk]
                blocks = jnp.concatenate([edges[side, i * EDGE + d] for d in range(SPAN)], axis=1)
                row = dot(blocks, flat(window, put, SPAN)) + base.astype(jnp.float32)
                level_a[put] = row.astype(level_a.dtype)
        clear_beyond(meta, level_a, REACH)
        second_of_group(wide_b, base_b, level_a, solved, at, done)
        if stages:
            for copy in copies:
                copy.wait()
        else:
            emit_sends(odd, solved, sends[:2])
            for i, part in enumerate(sends[2:]):
                part[...] = solved[i * part.shape[0] : (i + 1) * part.shape[0]]
            solved_a[...] = level_a[REACH : REACH + count]

    @pl.when(meta[0] == group - 1)
    def _():
        store(old_a.at[:, :, at] if old_a.shape[-1] > cases else old_a, old_b, out, on_out, *([sems.at[0]] if stages else [sems]))


def shaped(shape, dtype=jnp.bfloat16):
    return jax.ShapeDtypeStruct(shape, dtype)


def params(**more):
    return pltpu.CompilerParams(vmem_limit_bytes=24 * 1024 * 1024, **more)


def in_hbm(value):
    return pltpu.with_memory_space_constraint(value, pltpu.HBM)


def after(values, *earlier):
    return lax.optimization_barrier((values, earlier))[0]


def per_device(chain, rows, right_side, lower_blocks, block_scale, diag_inverse, depend_rows):
    _, count, block, cases = right_side.shape
    terms = lower_blocks.shape[2]
    width = SPAN * block
    part = cases // CHUNKS
    halo = 2 * REACH
    row = lax.axis_index("rows")
    ends = [row == 0, row == rows - 1]
    meta = jnp.stack([lax.axis_index("chain"), row % 2, row * count, *ends]).astype(jnp.int32)
    depend = in_hbm(depend_rows.transpose(2, 0, 1))
    scale = in_hbm(block_scale.transpose(2, 0, 1))
    tables = [pltpu.SMEM(depend.shape, jnp.int32), pltpu.SMEM(scale.shape, jnp.float32)]
    right_side, lower_blocks, diag_inverse = in_hbm(right_side), in_hbm(lower_blocks), in_hbm(diag_inverse)
    mates = (even_mate, odd_mate)

    def exchange(groups, values, idle=None):
        return [
            lax.ppermute(value, AXES, inner_pairs(groups, mate, chain, rows, idle))
            for value, mate in zip(values, mates)
        ]

    def travel(group, centre, sides):
        *sides, = sides
        centres = sides[2:] or [centre]
        kinds = [lax.ppermute(value, AXES, hop_pairs(group, same_row, chain, rows)) for value in centres]
        kinds += [lax.ppermute(value, AXES, hop_pairs(group, mate, chain, rows)) for value, mate in zip(sides, mates)]
        return [kinds[i] for i in (2, 3, 0, 1)] if len(kinds) > 3 else kinds

    def call(kernel, name, in_specs, out_shape, out_specs=None, **more):
        return pl.pallas_call(
            kernel,
            in_specs=in_specs,
            out_specs=out_specs or [VMEM] * len(out_shape),
            out_shape=out_shape,
            compiler_params=params(),
            name=name,
            **more,
        )

    whole, half = shaped((count, block, cases)), shaped((count, block, part))
    whole_edge, half_edge = shaped((REACH, block, cases)), shaped((halo, block, part))

    total = REACH * EDGE
    soon = REACH * cases // block
    edge_shapes = [shaped((size, block, block)) for size in (soon, total - soon)]
    first, *edge_w = call(
        first_kernel,
        "first_level",
        [SMEM] + [HBM] * 5,
        [whole, *(shape for shape in edge_shapes for _ in range(2))],
        scratch_shapes=[
            pltpu.VMEM((count, block, block), jnp.bfloat16),
            pltpu.VMEM(whole.shape, jnp.bfloat16),
            pltpu.VMEM((2, REACH, terms, block, block), jnp.bfloat16),
            *tables,
            pltpu.VMEM((REACH, SPAN, block, block), jnp.float32),
            pltpu.VMEM((2, total, block, block), jnp.bfloat16),
            pltpu.SemaphoreType.DMA((3, 4)),
        ],
    )(meta, depend, scale, lower_blocks, diag_inverse, right_side)
    sides = exchange([0, *range(2, chain)], edge_w[:2], 1)

    pairs = count // 2
    wide_shape = shaped((pairs, 2 * block, width + block))

    def prepare(turn, meta):
        return call(
            functools.partial(prepare_kernel, turn),
            f"prepare_{turn}",
            [SMEM] + [HBM] * 5,
            [wide_shape, shaped(whole.shape, jnp.float32)],
            scratch_shapes=[
                pltpu.VMEM(lower_blocks.shape[1:], jnp.bfloat16),
                pltpu.VMEM(diag_inverse.shape[1:], jnp.bfloat16),
                pltpu.VMEM(whole.shape, jnp.bfloat16),
                *tables,
                pltpu.VMEM((2, SPAN, block, block), jnp.float32),
                pltpu.SemaphoreType.DMA((4, pairs)),
            ],
        )(meta, depend, scale, lower_blocks, diag_inverse, right_side)

    wide_a, base_0 = prepare(0, meta)

    padded = pltpu.VMEM((count + halo, block, cases), jnp.bfloat16)
    padded_half = pltpu.VMEM((count + halo, block, part), jnp.bfloat16)
    solved, *sends = call(
        functools.partial(exchanged_step, 0, None),
        "step_0",
        [SMEM] + [VMEM] * 5,
        [whole, whole_edge, whole_edge],
        scratch_shapes=[padded],
    )(meta, first, *sides, wide_a, base_0)
    wide_b, base_b = prepare(1, after(meta, solved))
    arrived = travel(0, solved, sends)

    later_w = exchange(range(2, chain), after(edge_w[2:], sides))
    edges, = call(
        order_kernel, "order", [SMEM] + [VMEM] * 4, [shaped((2, total, block, block))]
    )(meta, *sides, *later_w)

    out, own, *sides = call(
        functools.partial(level_step, 1),
        "step_1",
        [SMEM] + [VMEM] * 6,
        [shaped(right_side.shape), whole, whole_edge, whole_edge],
        [ANY] + [VMEM] * 3,
        scratch_shapes=[padded, pltpu.SemaphoreType.DMA((2,))],
    )(meta, *arrived, first, wide_a, solved)
    sides = exchange([1], sides, 0)
    made_a = [own] * CHUNKS
    sent = []
    for chunk in range(CHUNKS):
        sent.append(
            call(
                functools.partial(exchanged_step, 1, chunk),
                f"step_1_{chunk}",
                [SMEM] + [VMEM] * 5,
                [half, half_edge, half_edge],
                scratch_shapes=[padded_half],
            )(meta, own, *sides, wide_b, base_b)
        )

    for group in range(2, chain):
        final = group == chain - 1
        arrived = [travel(group - 1, solved, sends) for solved, *sends in sent]
        made = []
        for chunk in range(CHUNKS):
            stages = final and chunk == CHUNKS - 1
            splits = group == chain - 2
            outs = [] if stages else [half, half] + ([] if final else [half_edge] * (4 if splits else 2))
            extra = [made[0][1], made[0][0][0]] if stages else []
            sems = (2, pairs) if stages else (2,)
            out, *now = call(
                functools.partial(later_step, group, chunk, final),
                f"step_{group}_{chunk}",
                [SMEM] + [VMEM] * (7 + len(arrived[chunk]) + len(extra)) + [ANY],
                [shaped(right_side.shape), *outs],
                [ANY] + [VMEM] * len(outs),
                scratch_shapes=[
                    pltpu.VMEM((count + 2 * halo, block, part), jnp.bfloat16),
                    padded_half,
                    *([pltpu.VMEM(shape, jnp.bfloat16) for shape in (half.shape, (2, *whole.shape))] if stages else []),
                    pltpu.SemaphoreType.DMA(sems),
                ],
                input_output_aliases={8 + len(arrived[chunk]) + len(extra): 0},
            )(
                meta,
                *arrived[chunk],
                edges,
                first,
                wide_a,
                wide_b,
                base_b,
                made_a[chunk],
                sent[chunk][0],
                *extra,
                out,
            )
            if now:
                solved, level, *sends = now
                made.append(((solved, *sends), level))
        sent, made_a = [values[0] for values in made], [values[1] for values in made]
    return out


def solution(mesh):
    placed = (
        P("chain", "rows", None, None),
        P("chain", "rows", None, None, None),
        P("chain", "rows", None),
        P("chain", "rows", None, None),
        P("chain", "rows", None),
    )
    return jax.shard_map(
        functools.partial(per_device, mesh.shape["chain"], mesh.shape["rows"]),
        mesh=mesh,
        in_specs=placed,
        out_specs=P("chain", "rows", None, None),
        check_vma=False,
    )
```

```python
import functools

import jax
import jax.numpy as jnp
from jax import lax
from jax.experimental import pallas as pl
from jax.experimental.pallas import tpu as pltpu
from jax.sharding import PartitionSpec as P

REACH = 2
SPAN = 2 * REACH + 1
CHUNKS = 2
EDGE = SPAN + CHUNKS
AXES = ("chain", "rows")
VMEM = pl.BlockSpec(memory_space=pltpu.VMEM)
SMEM = pl.BlockSpec(memory_space=pltpu.SMEM)
ANY = pl.BlockSpec(memory_space=pl.ANY)
HBM = pl.BlockSpec(memory_space=pltpu.HBM)


def even_mate(row, rows):
    return row ^ 1


def odd_mate(row, rows):
    mate = row + 1 if row % 2 else row - 1
    return mate if 0 <= mate < rows else row


def same_row(row, rows):
    return row


def swap_groups(chain, taken=()):
    return {g: g ^ 1 for g in range(chain) if g not in taken}


def hop_pairs(group, mate, chain, rows):
    if group % 2 == 0:
        moves = swap_groups(chain)
    else:
        moves = swap_groups(chain, range(group - 1, group + 3))
        moves.update({group: group + 1, group - 1: group, group + 1: group + 2, group + 2: group - 1})
    return [
        (source * rows + r, target * rows + (mate(r, rows) if source == group else r))
        for source, target in moves.items()
        for r in range(rows)
    ]


def inner_pairs(groups, mate, chain, rows, idle=None):
    pairs = []
    paired = [r for r in range(rows) if mate(r, rows) != r]
    for r in range(rows):
        if r not in paired:
            moves = swap_groups(chain)
        else:
            moves = swap_groups(chain, [*groups, idle])
            pairs += [(g * rows + r, g * rows + mate(r, rows)) for g in groups]
            if idle is not None:
                alike = [q for q in paired if q % 2 == r % 2]
                pairs.append((idle * rows + r, idle * rows + alike[(alike.index(r) + 1) % len(alike)]))
        pairs += [(a * rows + r, b * rows + r) for a, b in moves.items()]
    return pairs


def dot(a, b):
    return jnp.dot(a, b, preferred_element_type=jnp.float32)


def by_parity(odd, low_value, high_value, even_ref, odd_ref):
    @pl.when(odd == 0)
    def _():
        even_ref[...] = high_value()
        odd_ref[...] = low_value()

    @pl.when(odd == 1)
    def _():
        even_ref[...] = low_value()
        odd_ref[...] = high_value()


def premultiplied(meta, depend, scale, lower, inverse, acc, level, q):
    acc[...] = jnp.zeros_like(acc)
    for k in range(len(lower)):
        column = jnp.clip(depend[k, level, q] - (meta[2] + q) + REACH, 0, SPAN - 1)
        acc[column] += scale[k, level, q] * dot(inverse, lower[k])


def first_kernel(meta, depend_hbm, scale_hbm, lower_hbm, inverse_hbm, right_hbm, solved, even_a, odd_a, even_b, odd_b, inverse, right, lower, depend, scale, acc, edges, sems):
    count = inverse.shape[0]
    block = inverse.shape[1]
    parts = right.shape[2] // block
    steps = 4
    size = count // steps
    loads = []
    for step in range(steps):
        rows = pl.ds(step * size, size)
        loads.append(
            (
                pltpu.make_async_copy(inverse_hbm.at[0, rows], inverse.at[rows], sems.at[0, step]),
                pltpu.make_async_copy(right_hbm.at[0, rows], right.at[rows], sems.at[1, step]),
            )
        )
    ends = (0, count - REACH)

    def edge_load(side):
        rows = pl.ds(ends[side], REACH)
        return pltpu.make_async_copy(lower_hbm.at[0, rows], lower.at[side], sems.at[2, side])

    tables = [
        pltpu.make_async_copy(source, target, sems.at[2, 2 + i])
        for i, (source, target) in enumerate(((depend_hbm, depend), (scale_hbm, scale)))
    ]

    for pair in loads:
        for load in pair:
            load.start()

    @pl.when(meta[0] > 1)
    def _():
        for load in (edge_load(0), edge_load(1), *tables):
            load.start()

    for step in range(steps):
        for load in loads[step]:
            load.wait()
        for q in range(step * size, (step + 1) * size):
            solved[q] = dot(inverse[q], right[q]).astype(solved.dtype)

    def row_parts(q):
        return [solved[q, :, part * block : (part + 1) * block] for part in range(parts)]

    @pl.when(meta[0] < 2)
    def _():
        for side in range(2):
            for i in range(REACH):
                for part, value in enumerate(row_parts(ends[side] + i)):
                    edges[side, i * parts + part] = value

    @pl.when(meta[0] > 1)
    def _():
        for table in tables:
            table.wait()
        for side in range(2):
            edge_load(side).wait()
            for i in range(REACH):
                q = ends[side] + i
                blocks = [lower[side, i, k] for k in range(lower.shape[2])]
                premultiplied(meta, depend, scale, blocks, inverse[q], acc.at[i], 0, q)
                for d in range(SPAN):
                    edges[side, i * EDGE + d] = (-acc[i, d]).astype(edges.dtype)
                for part, value in enumerate(row_parts(q)):
                    edges[side, i * EDGE + SPAN + part] = value

    soon = even_a.shape[0]
    by_parity(meta[1], lambda: edges[0, :soon], lambda: edges[1, :soon], even_a, odd_a)

    @pl.when(meta[0] > 1)
    def _():
        by_parity(meta[1], lambda: edges[0, soon:], lambda: edges[1, soon:], even_b, odd_b)


def prepare_kernel(turn, meta, depend_hbm, scale_hbm, lower_hbm, inverse_hbm, right_hbm, wide, base, lower, inverse, right, depend, scale, acc, sems):
    pairs = wide.shape[0]
    block = lower.shape[-1]
    level = jnp.where(meta[0] == 0, 1, turn)

    def loads(p):
        rows = pl.ds(2 * p, 2)
        return [
            pltpu.make_async_copy(source.at[level, rows], target.at[rows], sems.at[i, p])
            for i, (source, target) in enumerate(((lower_hbm, lower), (inverse_hbm, inverse), (right_hbm, right)))
        ]

    @pl.when((meta[0] > 0) | (turn == 0))
    def _():
        tables = [
            pltpu.make_async_copy(source, target, sems.at[3, i])
            for i, (source, target) in enumerate(((depend_hbm, depend), (scale_hbm, scale)))
        ]
        for table in tables:
            table.start()
        for p in range(pairs):
            for load in loads(p):
                load.start()
        for table in tables:
            table.wait()

        @pl.loop(0, pairs)
        def _(p):
            for load in loads(p):
                load.wait()
            for half in range(2):
                q = 2 * p + half
                blocks = [lower[q, k] for k in range(lower.shape[1])]
                premultiplied(meta, depend, scale, blocks, inverse[q], acc.at[half], level, q)
                at = slice(half * block, (half + 1) * block)
                for d in range(SPAN):
                    wide[p, at, (d + half) * block : (d + half + 1) * block] = (-acc[half, d]).astype(wide.dtype)
                other = 0 if half else SPAN
                wide[p, at, other * block : (other + 1) * block] = jnp.zeros((block, block), wide.dtype)
                base[q] = dot(inverse[q], right[q])


def order_kernel(meta, even_a, odd_a, even_b, odd_b, edges):
    @pl.when(meta[0] > 1)
    def _():
        odd = meta[1]
        soon = even_a.shape[0]
        edges[1 - odd, :soon] = even_a[...]
        edges[1 - odd, soon:] = even_b[...]
        edges[odd, :soon] = odd_a[...]
        edges[odd, soon:] = odd_b[...]


def flat(ref, start, count, at=slice(None)):
    block = ref[start : start + count, :, at]
    return block.reshape(count * block.shape[1], block.shape[2])


def place(window, odd, even_in, odd_in, at=slice(None)):
    halo = even_in.shape[0]
    low, high = 0, window.shape[0] - halo
    window[pl.ds(jnp.where(odd == 1, low, high), halo)] = even_in[:, :, at]
    window[pl.ds(jnp.where(odd == 1, high, low), halo)] = odd_in[:, :, at]


def clear_beyond(meta, window, halo):
    for end in range(2):
        start = end * (window.shape[0] - halo)

        @pl.when(meta[3 + end] == 1)
        def _():
            window[start : start + halo] = jnp.zeros((halo, *window.shape[1:]), window.dtype)


def columns(chunk, cases):
    return slice(None) if chunk is None else slice(chunk * cases, (chunk + 1) * cases)


def first_of_group(wide_a, first, window, level_a, put, at):
    for p in range(wide_a.shape[0]):
        rows = dot(wide_a[p], flat(window, 2 * p, SPAN + 1)) + flat(first, 2 * p, 2, at).astype(jnp.float32)
        level_a[put + 2 * p : put + 2 * p + 2] = rows.astype(level_a.dtype).reshape(2, *level_a.shape[1:])


def second_of_group(wide_b, base_b, level_a, solved, at, done=None):
    for p in range(wide_b.shape[0]):
        rows = dot(wide_b[p], flat(level_a, 2 * p, SPAN + 1)) + flat(base_b, 2 * p, 2, at)
        solved[2 * p : 2 * p + 2] = rows.astype(solved.dtype).reshape(2, *solved.shape[1:])
        if done is not None:
            done(p)


def emit_sends(odd, solved, sends):
    if sends:
        size = sends[0].shape[0]
        count = solved.shape[0]
        by_parity(odd, lambda: solved[:size], lambda: solved[count - size :], *sends)


def store(level_a, solved, out, at, sems):
    copies = [
        pltpu.make_async_copy(source, out.at[level, :, :, at], sems.at[level])
        for level, source in ((0, level_a), (1, solved))
    ]
    for copy in copies:
        copy.start()
    for copy in copies:
        copy.wait()


def exchanged_step(group, chunk, meta, own, even_in, odd_in, wide_b, base_b, solved, even_out, odd_out, *rest):
    *halves, level_a = rest

    @pl.when(meta[0] == group)
    def _():
        at = columns(chunk, solved.shape[-1])
        count, block = own.shape[0], own.shape[1]
        level_a[REACH : REACH + count] = own[:, :, at]
        if even_in.shape[0] == REACH:
            place(level_a, meta[1], even_in, odd_in, at)
        else:
            parts = even_in.shape[0] // REACH
            low, high = 0, count + REACH
            for i in range(REACH):
                for part in range(parts):
                    cols = slice(part * block, (part + 1) * block)
                    level_a[i + jnp.where(meta[1] == 1, low, high), :, cols] = even_in[i * parts + part]
                    level_a[i + jnp.where(meta[1] == 1, high, low), :, cols] = odd_in[i * parts + part]
        clear_beyond(meta, level_a, REACH)
        second_of_group(wide_b, base_b, level_a, solved, at)
        emit_sends(meta[1], solved, (even_out, odd_out))
        for i, part in enumerate(halves):
            part[...] = solved[i * part.shape[0] : (i + 1) * part.shape[0]]


def level_step(group, meta, centre, even_in, odd_in, first, wide_a, old_b, out, solved, even_out, odd_out, window, sems):
    count = first.shape[0]

    @pl.when(meta[0] == group)
    def _():
        window[REACH : REACH + count] = centre[...]
        place(window, meta[1], even_in, odd_in)
        clear_beyond(meta, window, REACH)
        first_of_group(wide_a, first, window, solved, 0, slice(None))
        emit_sends(meta[1], solved, (even_out, odd_out))

    @pl.when(meta[0] == group - 1)
    def _():
        store(first, old_b, out, slice(None), sems)


def later_step(group, chunk, final, meta, *refs):
    stages = final and chunk == CHUNKS - 1
    if final or group == 2:
        even_in, odd_in, low, high, *rest = refs
        centre = [low, high]
    else:
        one, even_in, odd_in, *rest = refs
        centre = [one]
    edges, first, wide_a, wide_b, base_b, old_a, old_b, *rest = rest
    if stages:
        made_a, made_b, _, out, window, level_a, solved, stage, sems = rest
    else:
        _, out, solved, solved_a, *sends, window, level_a, sems = rest
    cases = solved.shape[-1]
    at = columns(chunk, cases)
    on_out = pl.ds(chunk * cases, cases)
    count = first.shape[0]

    @pl.when(meta[0] == group)
    def _():
        odd = meta[1]
        halo = 2 * REACH
        for i, part in enumerate(centre):
            window[halo + i * part.shape[0] : halo + (i + 1) * part.shape[0]] = part[...]
        place(window, odd, even_in, odd_in)
        clear_beyond(meta, window, halo)
        first_of_group(wide_a, first, window.at[pl.ds(REACH, count + halo)], level_a, REACH, at)
        done, copies = None, []
        if stages:
            copies = [
                pltpu.make_async_copy(stage.at[level, pl.ds(2 * p, 2)], out.at[level, pl.ds(2 * p, 2)], sems.at[level, p])
                for level in range(2)
                for p in range(count // 2)
            ]
            before = slice(0, chunk * cases)
            stage[0, :, :, before] = made_a[...]
            stage[1, :, :, before] = made_b[...]
            stage[0, :, :, at] = level_a[REACH : REACH + count]
            for copy in copies[: count // 2]:
                copy.start()

            def done(p):
                stage[1, 2 * p : 2 * p + 2, :, at] = solved[2 * p : 2 * p + 2]
                copies[count // 2 + p].start()

        for side in range(2):
            for i in range(REACH):
                put = side * (count + REACH) + i
                base = edges[side, i * EDGE + SPAN + chunk]
                blocks = jnp.concatenate([edges[side, i * EDGE + d] for d in range(SPAN)], axis=1)
                row = dot(blocks, flat(window, put, SPAN)) + base.astype(jnp.float32)
                level_a[put] = row.astype(level_a.dtype)
        clear_beyond(meta, level_a, REACH)
        second_of_group(wide_b, base_b, level_a, solved, at, done)
        if stages:
            for copy in copies:
                copy.wait()
        else:
            emit_sends(odd, solved, sends[:2])
            for i, part in enumerate(sends[2:]):
                part[...] = solved[i * part.shape[0] : (i + 1) * part.shape[0]]
            solved_a[...] = level_a[REACH : REACH + count]

    @pl.when(meta[0] == group - 1)
    def _():
        store(old_a.at[:, :, at] if old_a.shape[-1] > cases else old_a, old_b, out, on_out, *([sems.at[0]] if stages else [sems]))


def shaped(shape, dtype=jnp.bfloat16):
    return jax.ShapeDtypeStruct(shape, dtype)


def params(**more):
    return pltpu.CompilerParams(vmem_limit_bytes=24 * 1024 * 1024, **more)


def in_hbm(value):
    return pltpu.with_memory_space_constraint(value, pltpu.HBM)


def after(values, *earlier):
    return lax.optimization_barrier((values, earlier))[0]


def per_device(chain, rows, right_side, lower_blocks, block_scale, diag_inverse, depend_rows):
    _, count, block, cases = right_side.shape
    terms = lower_blocks.shape[2]
    width = SPAN * block
    part = cases // CHUNKS
    halo = 2 * REACH
    row = lax.axis_index("rows")
    ends = [row == 0, row == rows - 1]
    meta = jnp.stack([lax.axis_index("chain"), row % 2, row * count, *ends]).astype(jnp.int32)
    depend = in_hbm(depend_rows.transpose(2, 0, 1))
    scale = in_hbm(block_scale.transpose(2, 0, 1))
    tables = [pltpu.SMEM(depend.shape, jnp.int32), pltpu.SMEM(scale.shape, jnp.float32)]
    right_side, lower_blocks, diag_inverse = in_hbm(right_side), in_hbm(lower_blocks), in_hbm(diag_inverse)
    mates = (even_mate, odd_mate)

    def exchange(groups, values, idle=None):
        return [
            lax.ppermute(value, AXES, inner_pairs(groups, mate, chain, rows, idle))
            for value, mate in zip(values, mates)
        ]

    def travel(group, centre, sides):
        *sides, = sides
        centres = sides[2:] or [centre]
        kinds = [lax.ppermute(value, AXES, hop_pairs(group, same_row, chain, rows)) for value in centres]
        kinds += [lax.ppermute(value, AXES, hop_pairs(group, mate, chain, rows)) for value, mate in zip(sides, mates)]
        return [kinds[i] for i in (2, 3, 0, 1)] if len(kinds) > 3 else kinds

    def call(kernel, name, in_specs, out_shape, out_specs=None, **more):
        return pl.pallas_call(
            kernel,
            in_specs=in_specs,
            out_specs=out_specs or [VMEM] * len(out_shape),
            out_shape=out_shape,
            compiler_params=params(),
            name=name,
            **more,
        )

    whole, half = shaped((count, block, cases)), shaped((count, block, part))
    whole_edge, half_edge = shaped((REACH, block, cases)), shaped((halo, block, part))

    total = REACH * EDGE
    soon = REACH * cases // block
    edge_shapes = [shaped((size, block, block)) for size in (soon, total - soon)]
    first, *edge_w = call(
        first_kernel,
        "first_level",
        [SMEM] + [HBM] * 5,
        [whole, *(shape for shape in edge_shapes for _ in range(2))],
        scratch_shapes=[
            pltpu.VMEM((count, block, block), jnp.bfloat16),
            pltpu.VMEM(whole.shape, jnp.bfloat16),
            pltpu.VMEM((2, REACH, terms, block, block), jnp.bfloat16),
            *tables,
            pltpu.VMEM((REACH, SPAN, block, block), jnp.float32),
            pltpu.VMEM((2, total, block, block), jnp.bfloat16),
            pltpu.SemaphoreType.DMA((3, 4)),
        ],
    )(meta, depend, scale, lower_blocks, diag_inverse, right_side)
    sides = exchange([0, *range(2, chain)], edge_w[:2], 1)

    pairs = count // 2
    wide_shape = shaped((pairs, 2 * block, width + block))

    def prepare(turn, meta):
        return call(
            functools.partial(prepare_kernel, turn),
            f"prepare_{turn}",
            [SMEM] + [HBM] * 5,
            [wide_shape, shaped(whole.shape, jnp.float32)],
            scratch_shapes=[
                pltpu.VMEM(lower_blocks.shape[1:], jnp.bfloat16),
                pltpu.VMEM(diag_inverse.shape[1:], jnp.bfloat16),
                pltpu.VMEM(whole.shape, jnp.bfloat16),
                *tables,
                pltpu.VMEM((2, SPAN, block, block), jnp.float32),
                pltpu.SemaphoreType.DMA((4, pairs)),
            ],
        )(meta, depend, scale, lower_blocks, diag_inverse, right_side)

    wide_a, base_0 = prepare(0, meta)

    padded = pltpu.VMEM((count + halo, block, cases), jnp.bfloat16)
    padded_half = pltpu.VMEM((count + halo, block, part), jnp.bfloat16)
    solved, *sends = call(
        functools.partial(exchanged_step, 0, None),
        "step_0",
        [SMEM] + [VMEM] * 5,
        [whole, whole_edge, whole_edge],
        scratch_shapes=[padded],
    )(meta, first, *sides, wide_a, base_0)
    wide_b, base_b = prepare(1, after(meta, solved))
    arrived = travel(0, solved, sends)

    later_w = exchange(range(2, chain), after(edge_w[2:], sides))
    edges, = call(
        order_kernel, "order", [SMEM] + [VMEM] * 4, [shaped((2, total, block, block))]
    )(meta, *sides, *later_w)

    out, own, *sides = call(
        functools.partial(level_step, 1),
        "step_1",
        [SMEM] + [VMEM] * 6,
        [shaped(right_side.shape), whole, whole_edge, whole_edge],
        [ANY] + [VMEM] * 3,
        scratch_shapes=[padded, pltpu.SemaphoreType.DMA((2,))],
    )(meta, *arrived, first, wide_a, solved)
    sides = exchange([1], sides, 0)
    made_a = [own] * CHUNKS
    sent = []
    for chunk in range(CHUNKS):
        sent.append(
            call(
                functools.partial(exchanged_step, 1, chunk),
                f"step_1_{chunk}",
                [SMEM] + [VMEM] * 5,
                [half] + [half_edge] * 4,
                scratch_shapes=[padded_half],
            )(meta, own, *sides, wide_b, base_b)
        )

    for group in range(2, chain):
        final = group == chain - 1
        arrived = [travel(group - 1, solved, sends) for solved, *sends in sent]
        made = []
        for chunk in range(CHUNKS):
            stages = final and chunk == CHUNKS - 1
            splits = group == chain - 2
            outs = [] if stages else [half, half] + ([] if final else [half_edge] * (4 if splits else 2))
            extra = [made[0][1], made[0][0][0]] if stages else []
            sems = (2, pairs) if stages else (2,)
            out, *now = call(
                functools.partial(later_step, group, chunk, final),
                f"step_{group}_{chunk}",
                [SMEM] + [VMEM] * (7 + len(arrived[chunk]) + len(extra)) + [ANY],
                [shaped(right_side.shape), *outs],
                [ANY] + [VMEM] * len(outs),
                scratch_shapes=[
                    pltpu.VMEM((count + 2 * halo, block, part), jnp.bfloat16),
                    padded_half,
                    *([pltpu.VMEM(shape, jnp.bfloat16) for shape in (half.shape, (2, *whole.shape))] if stages else []),
                    pltpu.SemaphoreType.DMA(sems),
                ],
                input_output_aliases={8 + len(arrived[chunk]) + len(extra): 0},
            )(
                meta,
                *arrived[chunk],
                edges,
                first,
                wide_a,
                wide_b,
                base_b,
                made_a[chunk],
                sent[chunk][0],
                *extra,
                out,
            )
            if now:
                solved, level, *sends = now
                made.append(((solved, *sends), level))
        sent, made_a = [values[0] for values in made], [values[1] for values in made]
    return out


def solution(mesh):
    placed = (
        P("chain", "rows", None, None),
        P("chain", "rows", None, None, None),
        P("chain", "rows", None),
        P("chain", "rows", None, None),
        P("chain", "rows", None),
    )
    return jax.shard_map(
        functools.partial(per_device, mesh.shape["chain"], mesh.shape["rows"]),
        mesh=mesh,
        in_specs=placed,
        out_specs=P("chain", "rows", None, None),
        check_vma=False,
    )
```

```python
import functools

import jax
import jax.numpy as jnp
from jax import lax
from jax.experimental import pallas as pl
from jax.experimental.pallas import tpu as pltpu
from jax.sharding import PartitionSpec as P

REACH = 2
SPAN = 2 * REACH + 1
CHUNKS = 2
EDGE = SPAN + CHUNKS
AXES = ("chain", "rows")
VMEM = pl.BlockSpec(memory_space=pltpu.VMEM)
SMEM = pl.BlockSpec(memory_space=pltpu.SMEM)
ANY = pl.BlockSpec(memory_space=pl.ANY)
HBM = pl.BlockSpec(memory_space=pltpu.HBM)


def even_mate(row, rows):
    return row ^ 1


def odd_mate(row, rows):
    mate = row + 1 if row % 2 else row - 1
    return mate if 0 <= mate < rows else row


def same_row(row, rows):
    return row


def swap_groups(chain, taken=()):
    return {g: g ^ 1 for g in range(chain) if g not in taken}


def hop_pairs(group, mate, chain, rows):
    if group % 2 == 0:
        moves = swap_groups(chain)
        if group and mate is not same_row:
            moves.update({group + 1: group - 1, group - 1: group - 2, group - 2: group})
    else:
        moves = swap_groups(chain, range(group - 1, group + 3))
        moves.update({group: group + 1, group - 1: group, group + 1: group + 2, group + 2: group - 1})
    return [
        (source * rows + r, target * rows + (mate(r, rows) if source == group else r))
        for source, target in moves.items()
        for r in range(rows)
    ]


def inner_pairs(groups, mate, chain, rows, idle=None):
    pairs = []
    paired = [r for r in range(rows) if mate(r, rows) != r]
    for r in range(rows):
        if r not in paired:
            moves = swap_groups(chain)
        else:
            moves = swap_groups(chain, [*groups, idle])
            pairs += [(g * rows + r, g * rows + mate(r, rows)) for g in groups]
            if idle is not None:
                alike = [q for q in paired if q % 2 == r % 2]
                pairs.append((idle * rows + r, idle * rows + alike[(alike.index(r) + 1) % len(alike)]))
        pairs += [(a * rows + r, b * rows + r) for a, b in moves.items()]
    return pairs


def dot(a, b):
    return jnp.dot(a, b, preferred_element_type=jnp.float32)


def by_parity(odd, low_value, high_value, even_ref, odd_ref):
    @pl.when(odd == 0)
    def _():
        even_ref[...] = high_value()
        odd_ref[...] = low_value()

    @pl.when(odd == 1)
    def _():
        even_ref[...] = low_value()
        odd_ref[...] = high_value()


def premultiplied(meta, depend, scale, lower, inverse, acc, level, q):
    acc[...] = jnp.zeros_like(acc)
    for k in range(len(lower)):
        column = jnp.clip(depend[k, level, q] - (meta[2] + q) + REACH, 0, SPAN - 1)
        acc[column] += scale[k, level, q] * dot(inverse, lower[k])


def first_kernel(meta, depend_hbm, scale_hbm, lower_hbm, inverse_hbm, right_hbm, solved, even_a, odd_a, even_b, odd_b, inverse, right, lower, depend, scale, acc, edges, sems):
    count = inverse.shape[0]
    block = inverse.shape[1]
    parts = right.shape[2] // block
    steps = 4
    size = count // steps
    loads = []
    for step in range(steps):
        rows = pl.ds(step * size, size)
        loads.append(
            (
                pltpu.make_async_copy(inverse_hbm.at[0, rows], inverse.at[rows], sems.at[0, step]),
                pltpu.make_async_copy(right_hbm.at[0, rows], right.at[rows], sems.at[1, step]),
            )
        )
    ends = (0, count - REACH)

    def edge_load(side):
        rows = pl.ds(ends[side], REACH)
        return pltpu.make_async_copy(lower_hbm.at[0, rows], lower.at[side], sems.at[2, side])

    tables = [
        pltpu.make_async_copy(source, target, sems.at[2, 2 + i])
        for i, (source, target) in enumerate(((depend_hbm, depend), (scale_hbm, scale)))
    ]

    for pair in loads:
        for load in pair:
            load.start()

    @pl.when(meta[0] > 1)
    def _():
        for load in (edge_load(0), edge_load(1), *tables):
            load.start()

    for step in range(steps):
        for load in loads[step]:
            load.wait()
        for q in range(step * size, (step + 1) * size):
            solved[q] = dot(inverse[q], right[q]).astype(solved.dtype)

    def row_parts(q):
        return [solved[q, :, part * block : (part + 1) * block] for part in range(parts)]

    @pl.when(meta[0] < 2)
    def _():
        for side in range(2):
            for i in range(REACH):
                for part, value in enumerate(row_parts(ends[side] + i)):
                    edges[side, i * parts + part] = value

    @pl.when(meta[0] > 1)
    def _():
        for table in tables:
            table.wait()
        for side in range(2):
            edge_load(side).wait()
            for i in range(REACH):
                q = ends[side] + i
                blocks = [lower[side, i, k] for k in range(lower.shape[2])]
                premultiplied(meta, depend, scale, blocks, inverse[q], acc.at[i], 0, q)
                for d in range(SPAN):
                    edges[side, i * EDGE + d] = (-acc[i, d]).astype(edges.dtype)
                for part, value in enumerate(row_parts(q)):
                    edges[side, i * EDGE + SPAN + part] = value

    soon = even_a.shape[0]
    by_parity(meta[1], lambda: edges[0, :soon], lambda: edges[1, :soon], even_a, odd_a)

    @pl.when(meta[0] > 1)
    def _():
        by_parity(meta[1], lambda: edges[0, soon:], lambda: edges[1, soon:], even_b, odd_b)


def prepare_kernel(turn, meta, depend_hbm, scale_hbm, lower_hbm, inverse_hbm, right_hbm, wide, base, lower, inverse, right, depend, scale, acc, sems):
    pairs = wide.shape[0]
    block = lower.shape[-1]
    level = jnp.where(meta[0] == 0, 1, turn)

    def loads(p):
        rows = pl.ds(2 * p, 2)
        return [
            pltpu.make_async_copy(source.at[level, rows], target.at[rows], sems.at[i, p])
            for i, (source, target) in enumerate(((lower_hbm, lower), (inverse_hbm, inverse), (right_hbm, right)))
        ]

    @pl.when((meta[0] > 0) | (turn == 0))
    def _():
        tables = [
            pltpu.make_async_copy(source, target, sems.at[3, i])
            for i, (source, target) in enumerate(((depend_hbm, depend), (scale_hbm, scale)))
        ]
        for table in tables:
            table.start()
        for p in range(pairs):
            for load in loads(p):
                load.start()
        for table in tables:
            table.wait()

        @pl.loop(0, pairs)
        def _(p):
            for load in loads(p):
                load.wait()
            for half in range(2):
                q = 2 * p + half
                blocks = [lower[q, k] for k in range(lower.shape[1])]
                premultiplied(meta, depend, scale, blocks, inverse[q], acc.at[half], level, q)
                at = slice(half * block, (half + 1) * block)
                for d in range(SPAN):
                    wide[p, at, (d + half) * block : (d + half + 1) * block] = (-acc[half, d]).astype(wide.dtype)
                other = 0 if half else SPAN
                wide[p, at, other * block : (other + 1) * block] = jnp.zeros((block, block), wide.dtype)
                base[q] = dot(inverse[q], right[q])


def order_kernel(meta, even_a, odd_a, even_b, odd_b, edges):
    @pl.when(meta[0] > 1)
    def _():
        odd = meta[1]
        soon = even_a.shape[0]
        edges[1 - odd, :soon] = even_a[...]
        edges[1 - odd, soon:] = even_b[...]
        edges[odd, :soon] = odd_a[...]
        edges[odd, soon:] = odd_b[...]


def flat(ref, start, count, at=slice(None)):
    block = ref[start : start + count, :, at]
    return block.reshape(count * block.shape[1], block.shape[2])


def place(window, odd, even_in, odd_in, at=slice(None)):
    halo = even_in.shape[0]
    low, high = 0, window.shape[0] - halo
    window[pl.ds(jnp.where(odd == 1, low, high), halo)] = even_in[:, :, at]
    window[pl.ds(jnp.where(odd == 1, high, low), halo)] = odd_in[:, :, at]


def clear_beyond(meta, window, halo):
    for end in range(2):
        start = end * (window.shape[0] - halo)

        @pl.when(meta[3 + end] == 1)
        def _():
            window[start : start + halo] = jnp.zeros((halo, *window.shape[1:]), window.dtype)


def columns(chunk, cases):
    return slice(None) if chunk is None else slice(chunk * cases, (chunk + 1) * cases)


def first_of_group(wide_a, first, window, level_a, put, at):
    for p in range(wide_a.shape[0]):
        rows = dot(wide_a[p], flat(window, 2 * p, SPAN + 1)) + flat(first, 2 * p, 2, at).astype(jnp.float32)
        level_a[put + 2 * p : put + 2 * p + 2] = rows.astype(level_a.dtype).reshape(2, *level_a.shape[1:])


def second_of_group(wide_b, base_b, level_a, solved, at, done=None):
    for p in range(wide_b.shape[0]):
        rows = dot(wide_b[p], flat(level_a, 2 * p, SPAN + 1)) + flat(base_b, 2 * p, 2, at)
        solved[2 * p : 2 * p + 2] = rows.astype(solved.dtype).reshape(2, *solved.shape[1:])
        if done is not None:
            done(p)


def emit_sends(odd, solved, sends):
    if sends:
        size = sends[0].shape[0]
        count = solved.shape[0]
        by_parity(odd, lambda: solved[:size], lambda: solved[count - size :], *sends)


def store(level_a, solved, out, at, sems):
    copies = [
        pltpu.make_async_copy(source, out.at[level, :, :, at], sems.at[level])
        for level, source in ((0, level_a), (1, solved))
    ]
    for copy in copies:
        copy.start()
    for copy in copies:
        copy.wait()


def exchanged_step(group, chunk, meta, own, even_in, odd_in, wide_b, base_b, solved, even_out, odd_out, level_a):
    @pl.when(meta[0] == group)
    def _():
        at = columns(chunk, solved.shape[-1])
        count, block = own.shape[0], own.shape[1]
        level_a[REACH : REACH + count] = own[:, :, at]
        if even_in.shape[0] == REACH:
            place(level_a, meta[1], even_in, odd_in, at)
        else:
            parts = even_in.shape[0] // REACH
            low, high = 0, count + REACH
            for i in range(REACH):
                for part in range(parts):
                    cols = slice(part * block, (part + 1) * block)
                    level_a[i + jnp.where(meta[1] == 1, low, high), :, cols] = even_in[i * parts + part]
                    level_a[i + jnp.where(meta[1] == 1, high, low), :, cols] = odd_in[i * parts + part]
        clear_beyond(meta, level_a, REACH)
        second_of_group(wide_b, base_b, level_a, solved, at)
        emit_sends(meta[1], solved, (even_out, odd_out))


def level_step(group, meta, centre, even_in, odd_in, first, wide_a, old_b, out, solved, even_out, odd_out, window, sems):
    count = first.shape[0]

    @pl.when(meta[0] == group)
    def _():
        window[REACH : REACH + count] = centre[...]
        place(window, meta[1], even_in, odd_in)
        clear_beyond(meta, window, REACH)
        first_of_group(wide_a, first, window, solved, 0, slice(None))
        emit_sends(meta[1], solved, (even_out, odd_out))

    @pl.when(meta[0] == group - 1)
    def _():
        store(first, old_b, out, slice(None), sems)


def later_step(group, chunk, final, meta, *refs):
    stages = final and chunk == CHUNKS - 1
    if final:
        even_in, odd_in, low, high, *rest = refs
        centre = [low, high]
    else:
        one, even_in, odd_in, *rest = refs
        centre = [one]
    edges, first, wide_a, wide_b, base_b, old_a, old_b, *rest = rest
    if stages:
        made_a, made_b, _, out, window, level_a, solved, stage, sems = rest
    else:
        _, out, solved, solved_a, *sends, window, level_a, sems = rest
    cases = solved.shape[-1]
    at = columns(chunk, cases)
    on_out = pl.ds(chunk * cases, cases)
    count = first.shape[0]

    @pl.when(meta[0] == group)
    def _():
        odd = meta[1]
        halo = 2 * REACH
        for i, part in enumerate(centre):
            window[halo + i * part.shape[0] : halo + (i + 1) * part.shape[0]] = part[...]
        place(window, odd, even_in, odd_in)
        clear_beyond(meta, window, halo)
        first_of_group(wide_a, first, window.at[pl.ds(REACH, count + halo)], level_a, REACH, at)
        done, copies = None, []
        if stages:
            copies = [
                pltpu.make_async_copy(stage.at[level, pl.ds(2 * p, 2)], out.at[level, pl.ds(2 * p, 2)], sems.at[level, p])
                for level in range(2)
                for p in range(count // 2)
            ]
            before = slice(0, chunk * cases)
            stage[0, :, :, before] = made_a[...]
            stage[1, :, :, before] = made_b[...]
            stage[0, :, :, at] = level_a[REACH : REACH + count]
            for copy in copies[: count // 2]:
                copy.start()

            def done(p):
                stage[1, 2 * p : 2 * p + 2, :, at] = solved[2 * p : 2 * p + 2]
                copies[count // 2 + p].start()

        for side in range(2):
            for i in range(REACH):
                put = side * (count + REACH) + i
                base = edges[side, i * EDGE + SPAN + chunk]
                blocks = jnp.concatenate([edges[side, i * EDGE + d] for d in range(SPAN)], axis=1)
                row = dot(blocks, flat(window, put, SPAN)) + base.astype(jnp.float32)
                level_a[put] = row.astype(level_a.dtype)
        clear_beyond(meta, level_a, REACH)
        second_of_group(wide_b, base_b, level_a, solved, at, done)
        if stages:
            for copy in copies:
                copy.wait()
        else:
            emit_sends(odd, solved, sends[:2])
            for i, part in enumerate(sends[2:]):
                part[...] = solved[i * part.shape[0] : (i + 1) * part.shape[0]]
            solved_a[...] = level_a[REACH : REACH + count]

    @pl.when(meta[0] == group - 1)
    def _():
        store(old_a.at[:, :, at] if old_a.shape[-1] > cases else old_a, old_b, out, on_out, *([sems.at[0]] if stages else [sems]))


def shaped(shape, dtype=jnp.bfloat16):
    return jax.ShapeDtypeStruct(shape, dtype)


def params(**more):
    return pltpu.CompilerParams(vmem_limit_bytes=24 * 1024 * 1024, **more)


def in_hbm(value):
    return pltpu.with_memory_space_constraint(value, pltpu.HBM)


def after(values, *earlier):
    return lax.optimization_barrier((values, earlier))[0]


def per_device(chain, rows, right_side, lower_blocks, block_scale, diag_inverse, depend_rows):
    _, count, block, cases = right_side.shape
    terms = lower_blocks.shape[2]
    width = SPAN * block
    part = cases // CHUNKS
    halo = 2 * REACH
    row = lax.axis_index("rows")
    ends = [row == 0, row == rows - 1]
    meta = jnp.stack([lax.axis_index("chain"), row % 2, row * count, *ends]).astype(jnp.int32)
    depend = in_hbm(depend_rows.transpose(2, 0, 1))
    scale = in_hbm(block_scale.transpose(2, 0, 1))
    tables = [pltpu.SMEM(depend.shape, jnp.int32), pltpu.SMEM(scale.shape, jnp.float32)]
    right_side, lower_blocks, diag_inverse = in_hbm(right_side), in_hbm(lower_blocks), in_hbm(diag_inverse)
    mates = (even_mate, odd_mate)

    def exchange(groups, values, idle=None):
        return [
            lax.ppermute(value, AXES, inner_pairs(groups, mate, chain, rows, idle))
            for value, mate in zip(values, mates)
        ]

    def travel(group, centre, sides):
        *sides, = sides
        centres = sides[2:] or [centre]
        kinds = [lax.ppermute(value, AXES, hop_pairs(group, same_row, chain, rows)) for value in centres]
        kinds += [lax.ppermute(value, AXES, hop_pairs(group, mate, chain, rows)) for value, mate in zip(sides, mates)]
        return [kinds[i] for i in (2, 3, 0, 1)] if len(kinds) > 3 else kinds

    def call(kernel, name, in_specs, out_shape, out_specs=None, **more):
        return pl.pallas_call(
            kernel,
            in_specs=in_specs,
            out_specs=out_specs or [VMEM] * len(out_shape),
            out_shape=out_shape,
            compiler_params=params(),
            name=name,
            **more,
        )

    whole, half = shaped((count, block, cases)), shaped((count, block, part))
    whole_edge, half_edge = shaped((REACH, block, cases)), shaped((halo, block, part))

    total = REACH * EDGE
    soon = REACH * cases // block
    edge_shapes = [shaped((size, block, block)) for size in (soon, total - soon)]
    first, *edge_w = call(
        first_kernel,
        "first_level",
        [SMEM] + [HBM] * 5,
        [whole, *(shape for shape in edge_shapes for _ in range(2))],
        scratch_shapes=[
            pltpu.VMEM((count, block, block), jnp.bfloat16),
            pltpu.VMEM(whole.shape, jnp.bfloat16),
            pltpu.VMEM((2, REACH, terms, block, block), jnp.bfloat16),
            *tables,
            pltpu.VMEM((REACH, SPAN, block, block), jnp.float32),
            pltpu.VMEM((2, total, block, block), jnp.bfloat16),
            pltpu.SemaphoreType.DMA((3, 4)),
        ],
    )(meta, depend, scale, lower_blocks, diag_inverse, right_side)
    sides = exchange([0, *range(2, chain)], edge_w[:2], 1)

    pairs = count // 2
    wide_shape = shaped((pairs, 2 * block, width + block))

    def prepare(turn, meta):
        return call(
            functools.partial(prepare_kernel, turn),
            f"prepare_{turn}",
            [SMEM] + [HBM] * 5,
            [wide_shape, shaped(whole.shape, jnp.float32)],
            scratch_shapes=[
                pltpu.VMEM(lower_blocks.shape[1:], jnp.bfloat16),
                pltpu.VMEM(diag_inverse.shape[1:], jnp.bfloat16),
                pltpu.VMEM(whole.shape, jnp.bfloat16),
                *tables,
                pltpu.VMEM((2, SPAN, block, block), jnp.float32),
                pltpu.SemaphoreType.DMA((4, pairs)),
            ],
        )(meta, depend, scale, lower_blocks, diag_inverse, right_side)

    wide_a, base_0 = prepare(0, meta)

    padded = pltpu.VMEM((count + halo, block, cases), jnp.bfloat16)
    padded_half = pltpu.VMEM((count + halo, block, part), jnp.bfloat16)
    solved, *sends = call(
        functools.partial(exchanged_step, 0, None),
        "step_0",
        [SMEM] + [VMEM] * 5,
        [whole, whole_edge, whole_edge],
        scratch_shapes=[padded],
    )(meta, first, *sides, wide_a, base_0)
    wide_b, base_b = prepare(1, after(meta, solved))
    arrived = travel(0, solved, sends)

    later_w = exchange(range(2, chain), after(edge_w[2:], sides))
    edges, = call(
        order_kernel, "order", [SMEM] + [VMEM] * 4, [shaped((2, total, block, block))]
    )(meta, *sides, *later_w)

    out, own, *sides = call(
        functools.partial(level_step, 1),
        "step_1",
        [SMEM] + [VMEM] * 6,
        [shaped(right_side.shape), whole, whole_edge, whole_edge],
        [ANY] + [VMEM] * 3,
        scratch_shapes=[padded, pltpu.SemaphoreType.DMA((2,))],
    )(meta, *arrived, first, wide_a, solved)
    sides = exchange([1], sides, 0)
    made_a = [own] * CHUNKS
    sent = []
    for chunk in range(CHUNKS):
        sent.append(
            call(
                functools.partial(exchanged_step, 1, chunk),
                f"step_1_{chunk}",
                [SMEM] + [VMEM] * 5,
                [half, half_edge, half_edge],
                scratch_shapes=[padded_half],
            )(meta, own, *sides, wide_b, base_b)
        )

    for group in range(2, chain):
        final = group == chain - 1
        arrived = [travel(group - 1, solved, sends) for solved, *sends in sent]
        made = []
        for chunk in range(CHUNKS):
            stages = final and chunk == CHUNKS - 1
            splits = group == chain - 2
            outs = [] if stages else [half, half] + ([] if final else [half_edge] * (4 if splits else 2))
            extra = [made[0][1], made[0][0][0]] if stages else []
            sems = (2, pairs) if stages else (2,)
            out, *now = call(
                functools.partial(later_step, group, chunk, final),
                f"step_{group}_{chunk}",
                [SMEM] + [VMEM] * (7 + len(arrived[chunk]) + len(extra)) + [ANY],
                [shaped(right_side.shape), *outs],
                [ANY] + [VMEM] * len(outs),
                scratch_shapes=[
                    pltpu.VMEM((count + 2 * halo, block, part), jnp.bfloat16),
                    padded_half,
                    *([pltpu.VMEM(shape, jnp.bfloat16) for shape in (half.shape, (2, *whole.shape))] if stages else []),
                    pltpu.SemaphoreType.DMA(sems),
                ],
                input_output_aliases={8 + len(arrived[chunk]) + len(extra): 0},
            )(
                meta,
                *arrived[chunk],
                edges,
                first,
                wide_a,
                wide_b,
                base_b,
                made_a[chunk],
                sent[chunk][0],
                *extra,
                out,
            )
            if now:
                solved, level, *sends = now
                made.append(((solved, *sends), level))
        sent, made_a = [values[0] for values in made], [values[1] for values in made]
    return out


def solution(mesh):
    placed = (
        P("chain", "rows", None, None),
        P("chain", "rows", None, None, None),
        P("chain", "rows", None),
        P("chain", "rows", None, None),
        P("chain", "rows", None),
    )
    return jax.shard_map(
        functools.partial(per_device, mesh.shape["chain"], mesh.shape["rows"]),
        mesh=mesh,
        in_specs=placed,
        out_specs=P("chain", "rows", None, None),
        check_vma=False,
    )
```

```python
import functools

import jax
import jax.numpy as jnp
from jax import lax
from jax.experimental import pallas as pl
from jax.experimental.pallas import tpu as pltpu
from jax.sharding import PartitionSpec as P

REACH = 2
SPAN = 2 * REACH + 1
CHUNKS = 2
EDGE = SPAN + CHUNKS
AXES = ("chain", "rows")
VMEM = pl.BlockSpec(memory_space=pltpu.VMEM)
SMEM = pl.BlockSpec(memory_space=pltpu.SMEM)
ANY = pl.BlockSpec(memory_space=pl.ANY)
HBM = pl.BlockSpec(memory_space=pltpu.HBM)


def even_mate(row, rows):
    return row ^ 1


def odd_mate(row, rows):
    mate = row + 1 if row % 2 else row - 1
    return mate if 0 <= mate < rows else row


def same_row(row, rows):
    return row


def swap_groups(chain, taken=()):
    return {g: g ^ 1 for g in range(chain) if g not in taken}


def hop_pairs(group, mate, chain, rows, ahead=False):
    if group % 2 == 0:
        moves = swap_groups(chain)
        if group and ahead:
            moves.update({group + 1: group - 1, group - 1: group - 2, group - 2: group})
    else:
        moves = swap_groups(chain, range(group - 1, group + 3))
        moves.update({group: group + 1, group - 1: group, group + 1: group + 2, group + 2: group - 1})
    return [
        (source * rows + r, target * rows + (mate(r, rows) if source == group else r))
        for source, target in moves.items()
        for r in range(rows)
    ]


def inner_pairs(groups, mate, chain, rows, idle=None):
    pairs = []
    paired = [r for r in range(rows) if mate(r, rows) != r]
    for r in range(rows):
        if r not in paired:
            moves = swap_groups(chain)
        else:
            moves = swap_groups(chain, [*groups, idle])
            pairs += [(g * rows + r, g * rows + mate(r, rows)) for g in groups]
            if idle is not None:
                alike = [q for q in paired if q % 2 == r % 2]
                pairs.append((idle * rows + r, idle * rows + alike[(alike.index(r) + 1) % len(alike)]))
        pairs += [(a * rows + r, b * rows + r) for a, b in moves.items()]
    return pairs


def dot(a, b):
    return jnp.dot(a, b, preferred_element_type=jnp.float32)


def by_parity(odd, low_value, high_value, even_ref, odd_ref):
    @pl.when(odd == 0)
    def _():
        even_ref[...] = high_value()
        odd_ref[...] = low_value()

    @pl.when(odd == 1)
    def _():
        even_ref[...] = low_value()
        odd_ref[...] = high_value()


def premultiplied(meta, depend, scale, lower, inverse, acc, level, q):
    acc[...] = jnp.zeros_like(acc)
    for k in range(len(lower)):
        column = jnp.clip(depend[k, level, q] - (meta[2] + q) + REACH, 0, SPAN - 1)
        acc[column] += scale[k, level, q] * dot(inverse, lower[k])


def first_kernel(meta, depend_hbm, scale_hbm, lower_hbm, inverse_hbm, right_hbm, solved, even_a, odd_a, even_b, odd_b, inverse, right, lower, depend, scale, acc, edges, sems):
    count = inverse.shape[0]
    block = inverse.shape[1]
    parts = right.shape[2] // block
    steps = 4
    size = count // steps
    loads = []
    for step in range(steps):
        rows = pl.ds(step * size, size)
        loads.append(
            (
                pltpu.make_async_copy(inverse_hbm.at[0, rows], inverse.at[rows], sems.at[0, step]),
                pltpu.make_async_copy(right_hbm.at[0, rows], right.at[rows], sems.at[1, step]),
            )
        )
    ends = (0, count - REACH)

    def edge_load(side):
        rows = pl.ds(ends[side], REACH)
        return pltpu.make_async_copy(lower_hbm.at[0, rows], lower.at[side], sems.at[2, side])

    tables = [
        pltpu.make_async_copy(source, target, sems.at[2, 2 + i])
        for i, (source, target) in enumerate(((depend_hbm, depend), (scale_hbm, scale)))
    ]

    for pair in loads:
        for load in pair:
            load.start()

    @pl.when(meta[0] > 1)
    def _():
        for load in (edge_load(0), edge_load(1), *tables):
            load.start()

    for step in range(steps):
        for load in loads[step]:
            load.wait()
        for q in range(step * size, (step + 1) * size):
            solved[q] = dot(inverse[q], right[q]).astype(solved.dtype)

    def row_parts(q):
        return [solved[q, :, part * block : (part + 1) * block] for part in range(parts)]

    @pl.when(meta[0] < 2)
    def _():
        for side in range(2):
            for i in range(REACH):
                for part, value in enumerate(row_parts(ends[side] + i)):
                    edges[side, i * parts + part] = value

    @pl.when(meta[0] > 1)
    def _():
        for table in tables:
            table.wait()
        for side in range(2):
            edge_load(side).wait()
            for i in range(REACH):
                q = ends[side] + i
                blocks = [lower[side, i, k] for k in range(lower.shape[2])]
                premultiplied(meta, depend, scale, blocks, inverse[q], acc.at[i], 0, q)
                for d in range(SPAN):
                    edges[side, i * EDGE + d] = (-acc[i, d]).astype(edges.dtype)
                for part, value in enumerate(row_parts(q)):
                    edges[side, i * EDGE + SPAN + part] = value

    soon = even_a.shape[0]
    by_parity(meta[1], lambda: edges[0, :soon], lambda: edges[1, :soon], even_a, odd_a)

    @pl.when(meta[0] > 1)
    def _():
        by_parity(meta[1], lambda: edges[0, soon:], lambda: edges[1, soon:], even_b, odd_b)


def prepare_kernel(turn, meta, depend_hbm, scale_hbm, lower_hbm, inverse_hbm, right_hbm, wide, base, lower, inverse, right, depend, scale, acc, sems):
    pairs = wide.shape[0]
    block = lower.shape[-1]
    level = jnp.where(meta[0] == 0, 1, turn)

    def loads(p):
        rows = pl.ds(2 * p, 2)
        return [
            pltpu.make_async_copy(source.at[level, rows], target.at[rows], sems.at[i, p])
            for i, (source, target) in enumerate(((lower_hbm, lower), (inverse_hbm, inverse), (right_hbm, right)))
        ]

    @pl.when((meta[0] > 0) | (turn == 0))
    def _():
        tables = [
            pltpu.make_async_copy(source, target, sems.at[3, i])
            for i, (source, target) in enumerate(((depend_hbm, depend), (scale_hbm, scale)))
        ]
        for table in tables:
            table.start()
        for p in range(pairs):
            for load in loads(p):
                load.start()
        for table in tables:
            table.wait()

        @pl.loop(0, pairs)
        def _(p):
            for load in loads(p):
                load.wait()
            for half in range(2):
                q = 2 * p + half
                blocks = [lower[q, k] for k in range(lower.shape[1])]
                premultiplied(meta, depend, scale, blocks, inverse[q], acc.at[half], level, q)
                at = slice(half * block, (half + 1) * block)
                for d in range(SPAN):
                    wide[p, at, (d + half) * block : (d + half + 1) * block] = (-acc[half, d]).astype(wide.dtype)
                other = 0 if half else SPAN
                wide[p, at, other * block : (other + 1) * block] = jnp.zeros((block, block), wide.dtype)
                base[q] = dot(inverse[q], right[q])


def order_kernel(meta, even_a, odd_a, even_b, odd_b, edges):
    @pl.when(meta[0] > 1)
    def _():
        odd = meta[1]
        soon = even_a.shape[0]
        edges[1 - odd, :soon] = even_a[...]
        edges[1 - odd, soon:] = even_b[...]
        edges[odd, :soon] = odd_a[...]
        edges[odd, soon:] = odd_b[...]


def flat(ref, start, count, at=slice(None)):
    block = ref[start : start + count, :, at]
    return block.reshape(count * block.shape[1], block.shape[2])


def place(window, odd, even_in, odd_in, at=slice(None)):
    halo = even_in.shape[0]
    low, high = 0, window.shape[0] - halo
    window[pl.ds(jnp.where(odd == 1, low, high), halo)] = even_in[:, :, at]
    window[pl.ds(jnp.where(odd == 1, high, low), halo)] = odd_in[:, :, at]


def clear_beyond(meta, window, halo):
    for end in range(2):
        start = end * (window.shape[0] - halo)

        @pl.when(meta[3 + end] == 1)
        def _():
            window[start : start + halo] = jnp.zeros((halo, *window.shape[1:]), window.dtype)


def columns(chunk, cases):
    return slice(None) if chunk is None else slice(chunk * cases, (chunk + 1) * cases)


def first_of_group(wide_a, first, window, level_a, put, at):
    for p in range(wide_a.shape[0]):
        rows = dot(wide_a[p], flat(window, 2 * p, SPAN + 1)) + flat(first, 2 * p, 2, at).astype(jnp.float32)
        level_a[put + 2 * p : put + 2 * p + 2] = rows.astype(level_a.dtype).reshape(2, *level_a.shape[1:])


def second_of_group(wide_b, base_b, level_a, solved, at, done=None):
    for p in range(wide_b.shape[0]):
        rows = dot(wide_b[p], flat(level_a, 2 * p, SPAN + 1)) + flat(base_b, 2 * p, 2, at)
        solved[2 * p : 2 * p + 2] = rows.astype(solved.dtype).reshape(2, *solved.shape[1:])
        if done is not None:
            done(p)


def emit_sends(odd, solved, sends):
    if sends:
        size = sends[0].shape[0]
        count = solved.shape[0]
        by_parity(odd, lambda: solved[:size], lambda: solved[count - size :], *sends)


def store(level_a, solved, out, at, sems):
    copies = [
        pltpu.make_async_copy(source, out.at[level, :, :, at], sems.at[level])
        for level, source in ((0, level_a), (1, solved))
    ]
    for copy in copies:
        copy.start()
    for copy in copies:
        copy.wait()


def exchanged_step(group, chunk, meta, own, even_in, odd_in, wide_b, base_b, solved, even_out, odd_out, level_a):
    @pl.when(meta[0] == group)
    def _():
        at = columns(chunk, solved.shape[-1])
        count, block = own.shape[0], own.shape[1]
        level_a[REACH : REACH + count] = own[:, :, at]
        if even_in.shape[0] == REACH:
            place(level_a, meta[1], even_in, odd_in, at)
        else:
            parts = even_in.shape[0] // REACH
            low, high = 0, count + REACH
            for i in range(REACH):
                for part in range(parts):
                    cols = slice(part * block, (part + 1) * block)
                    level_a[i + jnp.where(meta[1] == 1, low, high), :, cols] = even_in[i * parts + part]
                    level_a[i + jnp.where(meta[1] == 1, high, low), :, cols] = odd_in[i * parts + part]
        clear_beyond(meta, level_a, REACH)
        second_of_group(wide_b, base_b, level_a, solved, at)
        emit_sends(meta[1], solved, (even_out, odd_out))


def level_step(group, meta, centre, even_in, odd_in, first, wide_a, old_b, out, solved, even_out, odd_out, window, sems):
    count = first.shape[0]

    @pl.when(meta[0] == group)
    def _():
        window[REACH : REACH + count] = centre[...]
        place(window, meta[1], even_in, odd_in)
        clear_beyond(meta, window, REACH)
        first_of_group(wide_a, first, window, solved, 0, slice(None))
        emit_sends(meta[1], solved, (even_out, odd_out))

    @pl.when(meta[0] == group - 1)
    def _():
        store(first, old_b, out, slice(None), sems)


def later_step(group, chunk, final, meta, *refs):
    stages = final and chunk == CHUNKS - 1
    if final:
        even_in, odd_in, low, high, *rest = refs
        centre = [low, high]
    else:
        one, even_in, odd_in, *rest = refs
        centre = [one]
    edges, first, wide_a, wide_b, base_b, old_a, old_b, *rest = rest
    if stages:
        made_a, made_b, _, out, window, level_a, solved, stage, sems = rest
    else:
        _, out, solved, solved_a, *sends, window, level_a, sems = rest
    cases = solved.shape[-1]
    at = columns(chunk, cases)
    on_out = pl.ds(chunk * cases, cases)
    count = first.shape[0]

    @pl.when(meta[0] == group)
    def _():
        odd = meta[1]
        halo = 2 * REACH
        for i, part in enumerate(centre):
            window[halo + i * part.shape[0] : halo + (i + 1) * part.shape[0]] = part[...]
        place(window, odd, even_in, odd_in)
        clear_beyond(meta, window, halo)
        first_of_group(wide_a, first, window.at[pl.ds(REACH, count + halo)], level_a, REACH, at)
        done, copies = None, []
        if stages:
            copies = [
                pltpu.make_async_copy(stage.at[level, pl.ds(2 * p, 2)], out.at[level, pl.ds(2 * p, 2)], sems.at[level, p])
                for level in range(2)
                for p in range(count // 2)
            ]
            before = slice(0, chunk * cases)
            stage[0, :, :, before] = made_a[...]
            stage[1, :, :, before] = made_b[...]
            stage[0, :, :, at] = level_a[REACH : REACH + count]
            for copy in copies[: count // 2]:
                copy.start()

            def done(p):
                stage[1, 2 * p : 2 * p + 2, :, at] = solved[2 * p : 2 * p + 2]
                copies[count // 2 + p].start()

        for side in range(2):
            for i in range(REACH):
                put = side * (count + REACH) + i
                base = edges[side, i * EDGE + SPAN + chunk]
                blocks = jnp.concatenate([edges[side, i * EDGE + d] for d in range(SPAN)], axis=1)
                row = dot(blocks, flat(window, put, SPAN)) + base.astype(jnp.float32)
                level_a[put] = row.astype(level_a.dtype)
        clear_beyond(meta, level_a, REACH)
        second_of_group(wide_b, base_b, level_a, solved, at, done)
        if stages:
            for copy in copies:
                copy.wait()
        else:
            emit_sends(odd, solved, sends[:2])
            for i, part in enumerate(sends[2:]):
                part[...] = solved[i * part.shape[0] : (i + 1) * part.shape[0]]
            solved_a[...] = level_a[REACH : REACH + count]

    @pl.when(meta[0] == group - 1)
    def _():
        store(old_a.at[:, :, at] if old_a.shape[-1] > cases else old_a, old_b, out, on_out, *([sems.at[0]] if stages else [sems]))


def shaped(shape, dtype=jnp.bfloat16):
    return jax.ShapeDtypeStruct(shape, dtype)


def params(**more):
    return pltpu.CompilerParams(vmem_limit_bytes=24 * 1024 * 1024, **more)


def in_hbm(value):
    return pltpu.with_memory_space_constraint(value, pltpu.HBM)


def after(values, *earlier):
    return lax.optimization_barrier((values, earlier))[0]


def per_device(chain, rows, right_side, lower_blocks, block_scale, diag_inverse, depend_rows):
    _, count, block, cases = right_side.shape
    terms = lower_blocks.shape[2]
    width = SPAN * block
    part = cases // CHUNKS
    halo = 2 * REACH
    row = lax.axis_index("rows")
    ends = [row == 0, row == rows - 1]
    meta = jnp.stack([lax.axis_index("chain"), row % 2, row * count, *ends]).astype(jnp.int32)
    depend = in_hbm(depend_rows.transpose(2, 0, 1))
    scale = in_hbm(block_scale.transpose(2, 0, 1))
    tables = [pltpu.SMEM(depend.shape, jnp.int32), pltpu.SMEM(scale.shape, jnp.float32)]
    right_side, lower_blocks, diag_inverse = in_hbm(right_side), in_hbm(lower_blocks), in_hbm(diag_inverse)
    mates = (even_mate, odd_mate)

    def exchange(groups, values, idle=None):
        return [
            lax.ppermute(value, AXES, inner_pairs(groups, mate, chain, rows, idle))
            for value, mate in zip(values, mates)
        ]

    def travel(group, centre, sides, ahead):
        *sides, = sides
        centres = sides[2:] or [centre]
        kinds = [lax.ppermute(value, AXES, hop_pairs(group, same_row, chain, rows)) for value in centres]
        kinds += [lax.ppermute(value, AXES, hop_pairs(group, mate, chain, rows, ahead)) for value, mate in zip(sides, mates)]
        return [kinds[i] for i in (2, 3, 0, 1)] if len(kinds) > 3 else kinds

    def call(kernel, name, in_specs, out_shape, out_specs=None, **more):
        return pl.pallas_call(
            kernel,
            in_specs=in_specs,
            out_specs=out_specs or [VMEM] * len(out_shape),
            out_shape=out_shape,
            compiler_params=params(),
            name=name,
            **more,
        )

    whole, half = shaped((count, block, cases)), shaped((count, block, part))
    whole_edge, half_edge = shaped((REACH, block, cases)), shaped((halo, block, part))

    total = REACH * EDGE
    soon = REACH * cases // block
    edge_shapes = [shaped((size, block, block)) for size in (soon, total - soon)]
    first, *edge_w = call(
        first_kernel,
        "first_level",
        [SMEM] + [HBM] * 5,
        [whole, *(shape for shape in edge_shapes for _ in range(2))],
        scratch_shapes=[
            pltpu.VMEM((count, block, block), jnp.bfloat16),
            pltpu.VMEM(whole.shape, jnp.bfloat16),
            pltpu.VMEM((2, REACH, terms, block, block), jnp.bfloat16),
            *tables,
            pltpu.VMEM((REACH, SPAN, block, block), jnp.float32),
            pltpu.VMEM((2, total, block, block), jnp.bfloat16),
            pltpu.SemaphoreType.DMA((3, 4)),
        ],
    )(meta, depend, scale, lower_blocks, diag_inverse, right_side)
    sides = exchange([0, *range(2, chain)], edge_w[:2], 1)

    pairs = count // 2
    wide_shape = shaped((pairs, 2 * block, width + block))

    def prepare(turn, meta):
        return call(
            functools.partial(prepare_kernel, turn),
            f"prepare_{turn}",
            [SMEM] + [HBM] * 5,
            [wide_shape, shaped(whole.shape, jnp.float32)],
            scratch_shapes=[
                pltpu.VMEM(lower_blocks.shape[1:], jnp.bfloat16),
                pltpu.VMEM(diag_inverse.shape[1:], jnp.bfloat16),
                pltpu.VMEM(whole.shape, jnp.bfloat16),
                *tables,
                pltpu.VMEM((2, SPAN, block, block), jnp.float32),
                pltpu.SemaphoreType.DMA((4, pairs)),
            ],
        )(meta, depend, scale, lower_blocks, diag_inverse, right_side)

    wide_a, base_0 = prepare(0, meta)

    padded = pltpu.VMEM((count + halo, block, cases), jnp.bfloat16)
    padded_half = pltpu.VMEM((count + halo, block, part), jnp.bfloat16)
    solved, *sends = call(
        functools.partial(exchanged_step, 0, None),
        "step_0",
        [SMEM] + [VMEM] * 5,
        [whole, whole_edge, whole_edge],
        scratch_shapes=[padded],
    )(meta, first, *sides, wide_a, base_0)
    wide_b, base_b = prepare(1, after(meta, solved))
    arrived = travel(0, solved, sends, False)

    later_w = exchange(range(2, chain), after(edge_w[2:], sides))
    edges, = call(
        order_kernel, "order", [SMEM] + [VMEM] * 4, [shaped((2, total, block, block))]
    )(meta, *sides, *later_w)

    out, own, *sides = call(
        functools.partial(level_step, 1),
        "step_1",
        [SMEM] + [VMEM] * 6,
        [shaped(right_side.shape), whole, whole_edge, whole_edge],
        [ANY] + [VMEM] * 3,
        scratch_shapes=[padded, pltpu.SemaphoreType.DMA((2,))],
    )(meta, *arrived, first, wide_a, solved)
    sides = exchange([1], sides, 0)
    made_a = [own] * CHUNKS
    sent = []
    for chunk in range(CHUNKS):
        sent.append(
            call(
                functools.partial(exchanged_step, 1, chunk),
                f"step_1_{chunk}",
                [SMEM] + [VMEM] * 5,
                [half, half_edge, half_edge],
                scratch_shapes=[padded_half],
            )(meta, own, *sides, wide_b, base_b)
        )

    for group in range(2, chain):
        final = group == chain - 1
        arrived = [travel(group - 1, solved, sends, i == 0) for i, (solved, *sends) in enumerate(sent)]
        made = []
        for chunk in range(CHUNKS):
            stages = final and chunk == CHUNKS - 1
            splits = group == chain - 2
            outs = [] if stages else [half, half] + ([] if final else [half_edge] * (4 if splits else 2))
            extra = [made[0][1], made[0][0][0]] if stages else []
            sems = (2, pairs) if stages else (2,)
            out, *now = call(
                functools.partial(later_step, group, chunk, final),
                f"step_{group}_{chunk}",
                [SMEM] + [VMEM] * (7 + len(arrived[chunk]) + len(extra)) + [ANY],
                [shaped(right_side.shape), *outs],
                [ANY] + [VMEM] * len(outs),
                scratch_shapes=[
                    pltpu.VMEM((count + 2 * halo, block, part), jnp.bfloat16),
                    padded_half,
                    *([pltpu.VMEM(shape, jnp.bfloat16) for shape in (half.shape, (2, *whole.shape))] if stages else []),
                    pltpu.SemaphoreType.DMA(sems),
                ],
                input_output_aliases={8 + len(arrived[chunk]) + len(extra): 0},
            )(
                meta,
                *arrived[chunk],
                edges,
                first,
                wide_a,
                wide_b,
                base_b,
                made_a[chunk],
                sent[chunk][0],
                *extra,
                out,
            )
            if now:
                solved, level, *sends = now
                made.append(((solved, *sends), level))
        sent, made_a = [values[0] for values in made], [values[1] for values in made]
    return out


def solution(mesh):
    placed = (
        P("chain", "rows", None, None),
        P("chain", "rows", None, None, None),
        P("chain", "rows", None),
        P("chain", "rows", None, None),
        P("chain", "rows", None),
    )
    return jax.shard_map(
        functools.partial(per_device, mesh.shape["chain"], mesh.shape["rows"]),
        mesh=mesh,
        in_specs=placed,
        out_specs=P("chain", "rows", None, None),
        check_vma=False,
    )
```
